32 devices in a mesh: req: 8 (over z, x), grp: 4 (over y, core).
Axes of the slice: x: 2, y: 2, z: 4, core: 2. Of those that a mesh axis runs over, the one named last changes fastest.
Arguments:
- hidden: bfloat16 [256, 16, 1024], P(('grp', 'req')), parts along dimension 0, may hold values from -6 to 6
- norm_gain: float32 [1024], replicated, may hold values from 0.1 to 1.9
- in_weight: bfloat16 [1024, 4096], replicated, may hold values from -0.1875 to 0.1875
- conv_weight: float32 [4, 2048], P(None, 'req'), may hold values from -3 to 3
- conv_bias: float32 [2048], P('req'), may hold values from -3 to 3
- x_weight: bfloat16 [2048, 160], P('req'), may hold values from -0.125 to 0.125
- step_weight: bfloat16 [128, 2048], P(None, 'req'), may hold values from -0.5 to 0.5
- step_bias: float32 [2048], P('req'), may hold values from -5 to -1
- log_decay: float32 [16, 2048], P(None, 'req'), may hold values from -0.7 to 2.8
- skip_gain: float32 [2048], P('req'), may hold values from 0.5 to 1.5
- out_weight: bfloat16 [2048, 1024], replicated, may hold values from -0.125 to 0.125
- old_states: float32 [256, 16, 2048], P(('grp', 'req')), parts along dimension 0, may hold values from -3 to 3
- old_edges: bfloat16 [256, 3, 2048], P(('grp', 'req')), parts along dimension 0, may hold values from -6 to 6
- anchor: int32 [256], P('grp'), parts along dimension 0, may hold values from 0 to 63, each once
- fresh_flag: int32 [256], P('grp'), parts along dimension 0, may hold values 0 or 1
- accepted: int32 [256], P('grp'), parts along dimension 0, may hold values from 1 to 16
- request_ages: int32 [256], P('grp'), parts along dimension 0, may hold values from 0 to 7
Outputs:
- layer_out: bfloat16 [256, 16, 1024], P(('grp', 'req')), parts along dimension 0
- new_states: float32 [256, 16, 2048], P(('grp', 'req')), parts along dimension 0
The draws below stay inside these ranges and needn't reach their ends.
There are 4 independent parts, one for each index of `grp`. The reference program is written for one: setup_inputs(seed, part) draws one part's arguments, and reference() takes and returns one part's arrays. A program takes and returns all parts, laid end to end along the dimension named above; an argument that names none is the same for every part. Nothing has to cross between parts.
Inputs may be any that keep to these rules, and one draw needn't show every extreme that they name: Every old slot is the anchor of exactly one request.
All inputs are finite; a program needn't handle non-finite values.
Results may differ from the reference program's by a relative error of at most 0.0091.
Values may be sent and summed in bfloat16 or wider, within the bound.
No kernel may reach another device: no remote copies, remote signals or barrier semaphores. Data moves between devices by JAX's collectives and lax.ppermute only.
A program may use at most 128 MiB of HBM per device.

```python
import jax
import jax.numpy as jnp
from jax import lax

D = 1024
E = 2048
DSTATE = 16
RANK = 128
KCONV = 4
DRAFT = 16
REQS = 64


def with_ends(values, own_key, least, top_value):
    dims = values.shape
    place = [jax.random.randint(jax.random.fold_in(own_key, axis), (), 0, dims[axis]) for axis in range(len(dims))]
    values = values.at[tuple(place)].set(least)
    longest = dims.index(max(dims))
    place[longest] = (place[longest] + 1) % dims[longest]
    return values.at[tuple(place)].set(top_value)


def shard_levels(key, shape, pieces, smallest, high):
    factor_of = 1.0
    for dim, blocks in pieces:
        steps = jax.random.uniform(jax.random.fold_in(jax.random.fold_in(key, 6), dim), (blocks,), jnp.float32, smallest / len(pieces), high / len(pieces))
        factor_of = factor_of * jnp.repeat(jnp.exp(steps), shape[dim] // blocks).reshape((-1,) + (1,) * (len(shape) - 1 - dim))
    return factor_of


def bell_draw(key, shape, deviation, most, shards=(), kind=jnp.bfloat16):
    level = shard_levels(key, shape, shards, -0.22, 0.18) if shards else 1.0
    values = jax.random.normal(key, shape, jnp.float32) * deviation * level
    return jnp.minimum(jnp.maximum(values, -most), most).astype(kind)


def setup_inputs(seed: int = 0, part: int = 0) -> dict:
    arg_keys = jax.random.split(jax.random.key(seed), 18)
    part_keys = jax.random.split(jax.random.fold_in(arg_keys[17], part), 18)
    hidden = bell_draw(part_keys[0], (REQS, DRAFT, D), 1.0, 6.0, ((0, 8),))
    norm_gain = jnp.clip(1.0 + 0.18 * jax.random.normal(arg_keys[1], (D,), jnp.float32), 0.1, 1.9)
    in_weight = bell_draw(arg_keys[2], (D, 2 * E), D ** -0.5, 0.1875)
    conv_weight = bell_draw(arg_keys[3], (KCONV, E), KCONV ** -0.5, 3.0, ((1, 8),), jnp.float32)
    conv_bias = bell_draw(arg_keys[4], (E,), 0.5, 3.0, ((0, 8),), jnp.float32)
    x_weight = bell_draw(arg_keys[5], (E, RANK + 2 * DSTATE), E ** -0.5, 0.125, ((0, 8),))
    step_weight = bell_draw(arg_keys[6], (RANK, E), RANK ** -0.5, 0.5, ((1, 8),))
    step_bias = jnp.clip(-5.0 + 4.0 * jax.random.uniform(arg_keys[7], (E,), jnp.float32) ** shard_levels(arg_keys[7], (E,), ((0, 8),), -0.2, 0.2), -5.0, -1.0)
    log_decay = jnp.clip(-0.7 + 3.5 * jax.random.uniform(arg_keys[8], (DSTATE, E), jnp.float32) ** shard_levels(arg_keys[8], (DSTATE, E), ((1, 8),), -0.2, 0.2), -0.7, 2.8)
    skip_gain = jnp.clip(0.5 + 1.0 * jax.random.uniform(arg_keys[9], (E,), jnp.float32) ** shard_levels(arg_keys[9], (E,), ((0, 8),), -0.2, 0.2), 0.5, 1.5)
    out_weight = bell_draw(arg_keys[10], (E, D), E ** -0.5, 0.125)
    old_states = bell_draw(part_keys[11], (REQS, DSTATE, E), 0.5, 3.0, ((0, 8),), jnp.float32)
    old_edges = bell_draw(part_keys[12], (REQS, KCONV - 1, E), 1.0, 6.0, ((0, 8),))
    anchor = jax.random.permutation(part_keys[13], REQS).astype(jnp.int32)
    fresh_flag = with_ends((jax.random.randint(part_keys[14], (REQS,), 0, 3) < 1).astype(jnp.int32), jax.random.fold_in(part_keys[14], 1), 0, 1)
    accepted = with_ends(jax.random.randint(part_keys[15], (REQS,), 1, DRAFT + 1), jax.random.fold_in(part_keys[15], 1), 1, DRAFT).astype(jnp.int32)
    request_ages = with_ends(jax.random.randint(part_keys[16], (REQS,), 0, 8), jax.random.fold_in(part_keys[16], 1), 0, 7).astype(jnp.int32)
    return {"hidden": hidden, "norm_gain": norm_gain, "in_weight": in_weight, "conv_weight": conv_weight, "conv_bias": conv_bias, "x_weight": x_weight, "step_weight": step_weight, "step_bias": step_bias, "log_decay": log_decay, "skip_gain": skip_gain, "out_weight": out_weight, "old_states": old_states, "old_edges": old_edges, "anchor": anchor, "fresh_flag": fresh_flag, "accepted": accepted, "request_ages": request_ages}


EPS = 1e-05

def rms_normed(hidden, norm_gain):
    values = hidden.astype(jnp.float32)
    factor = lax.rsqrt(lax.optimization_barrier(jnp.mean(values * values, axis=-1, keepdims=True)) + EPS)
    return (values * factor * norm_gain).astype(jnp.bfloat16)

def edge_history(edges, fresh_flag, request_ages):
    span = edges.shape[1]
    distance = span - jnp.arange(span, dtype=jnp.int32)
    usable = (distance[None, :] <= request_ages[:, None]) & (fresh_flag[:, None] == 0)
    return jnp.where(usable[:, :, None], edges.astype(jnp.float32), jnp.zeros((), jnp.float32))

def causal_conv(history, inputs, conv_weight, conv_bias, length):
    sequence = jnp.concatenate([history, inputs.astype(jnp.float32)], axis=1)
    running = conv_bias + conv_weight[0] * sequence[:, 0:length]
    for offset in range(1, conv_weight.shape[0]):
        running = running + conv_weight[offset] * sequence[:, offset:offset + length]
    return jax.nn.silu(running).astype(jnp.bfloat16)

def selective_scan(start_state, step_sizes, b_coeff, c_coeff, inputs, decay, accepted):

    def advance(carried, sliced):
        current, chosen = carried
        step_delta, step_b, step_c, step_input, step_index = sliced
        factor = jnp.exp(step_delta[:, None, :] * decay[None, :, :])
        current = factor * current + (step_delta * step_input)[:, None, :] * step_b[:, :, None]
        result = lax.optimization_barrier(jnp.sum(step_c[:, :, None] * current, axis=1))
        chosen = jnp.where((accepted == step_index + 1)[:, None, None], current, chosen)
        return ((current, chosen), result)
    length = step_sizes.shape[1]
    sliced = (jnp.swapaxes(step_sizes, 0, 1), jnp.swapaxes(b_coeff, 0, 1), jnp.swapaxes(c_coeff, 0, 1), jnp.swapaxes(inputs, 0, 1), jnp.arange(length, dtype=jnp.int32))
    (final_state, chosen), outputs = lax.scan(advance, (start_state, start_state), sliced)
    return (jnp.swapaxes(outputs, 0, 1), chosen)

def reference(hidden, norm_gain, in_weight, conv_weight, conv_bias, x_weight, step_weight, step_bias, log_decay, skip_gain, out_weight, old_states, old_edges, anchor, fresh_flag, accepted, request_ages):
    normed = rms_normed(hidden, norm_gain)
    projected = jnp.dot(normed.reshape(REQS * DRAFT, D), in_weight, preferred_element_type=jnp.float32).astype(jnp.bfloat16)
    projected = projected.reshape(REQS, DRAFT, 2, E)
    inner_part = projected[:, :, 0]
    gate_part = projected[:, :, 1]
    keep_state = (1 - fresh_flag).astype(jnp.float32)
    start_state = jnp.take(old_states, anchor, axis=0) * keep_state[:, None, None]
    history = edge_history(jnp.take(old_edges, anchor, axis=0), fresh_flag, request_ages)
    conv_out = causal_conv(history, inner_part, conv_weight, conv_bias, DRAFT)
    conv_rows = conv_out.reshape(REQS * DRAFT, E)
    mixed_rows = jnp.dot(conv_rows, x_weight, preferred_element_type=jnp.float32).astype(jnp.bfloat16)
    step_sizes = jax.nn.softplus(jnp.dot(mixed_rows[:, :RANK], step_weight, preferred_element_type=jnp.float32) + step_bias)
    step_sizes = step_sizes.reshape(REQS, DRAFT, E)
    coeffs = mixed_rows[:, RANK:].astype(jnp.float32).reshape(REQS, DRAFT, 2 * DSTATE)
    b_coeff = coeffs[:, :, :DSTATE]
    c_coeff = coeffs[:, :, DSTATE:]
    inputs = conv_out.astype(jnp.float32)
    outputs, chosen = selective_scan(start_state, step_sizes, b_coeff, c_coeff, inputs, -jnp.exp(log_decay), accepted)
    gated_rows = ((outputs + skip_gain * inputs) * jax.nn.silu(gate_part.astype(jnp.float32))).astype(jnp.bfloat16)
    layer_out = jnp.dot(gated_rows.reshape(REQS * DRAFT, E), out_weight, preferred_element_type=jnp.float32).astype(jnp.bfloat16)
    return (layer_out.reshape(REQS, DRAFT, D), chosen)
```

```python
import functools

import jax
import jax.numpy as jnp
from jax import lax
from jax.experimental import pallas as pl
from jax.experimental.pallas import tpu as pltpu
from jax.sharding import PartitionSpec as P

EPS = 1e-05
LOG2E = 1.4426950408889634
LANES = 128
BLOCK = 256


def rms_normed(values_in, norm_gain):
    values = values_in.astype(jnp.float32)
    factor = lax.rsqrt(jnp.mean(values * values, axis=-1, keepdims=True) + EPS)
    return (values * factor * norm_gain).astype(jnp.bfloat16)


def pack_kernel(state_ref, edge_ref, out_ref, tile_ref):
    blocks, slots, _ = out_ref.shape
    width = state_ref.shape[1] // blocks
    states = state_ref.shape[0] // slots
    for dest in range(blocks):
        cols = pl.ds(dest * width, width)
        for part in range(width // LANES):
            at = dest * width + part * LANES
            tile = tile_ref.at[at // LANES]
            tile[...] = state_ref[:, pl.ds(at, LANES)]
            for n in range(states):
                rows = tile[pl.ds(n, slots, stride=states), :]
                out_ref[dest, :, pl.ds(n * width + part * LANES, LANES)] = rows.astype(jnp.bfloat16)
        for e in range(edge_ref.shape[0]):
            out_ref[dest, :, pl.ds((states + e) * width, width)] = edge_ref[e, :, cols]


def pack(old_states, old_edges, blocks):
    slots, states, inner = old_states.shape
    span = old_edges.shape[1]
    width = inner // blocks
    edges = jnp.swapaxes(old_edges, 0, 1)
    if width % LANES == 0 and slots == 8:
        return pl.pallas_call(
            pack_kernel,
            out_shape=jax.ShapeDtypeStruct((blocks, slots, (states + span) * width), jnp.bfloat16),
            in_specs=[pl.BlockSpec(memory_space=pltpu.VMEM)] * 2,
            out_specs=pl.BlockSpec(memory_space=pltpu.VMEM),
            scratch_shapes=[pltpu.VMEM((inner // LANES, slots * states, LANES), jnp.float32)],
            compiler_params=pltpu.CompilerParams(vmem_limit_bytes=16 << 20),
            name="pack_states",
        )(old_states.reshape(slots * states, inner), edges)
    lead = jnp.swapaxes(old_states.astype(jnp.bfloat16), 0, 1)
    both = jnp.concatenate([lead, edges], axis=0)
    both = both.reshape(states + span, slots, blocks, width)
    return both.transpose(2, 1, 0, 3).reshape(blocks, slots, (states + span) * width)


def scan_kernel(
    h0_ref, dt_ref, conv_ref, gate_ref, coef_ref, acc_ref, decay_ref, skip_ref, ow_ref,
    out_ref, ns_ref, b_ref, c_ref, pick_ref, y_ref, sum_ref,
):
    step = pl.program_id(0)
    reqs, draft, _ = out_ref.shape
    states = decay_ref.shape[0]

    @pl.when(step == 0)
    def _():
        for t in range(draft):
            rows = coef_ref[pl.ds(t * reqs, reqs), :]
            for n in range(states):
                b_ref[t * states + n] = jnp.broadcast_to(rows[:, n : n + 1], (reqs, LANES))
                c_ref[t * states + n] = jnp.broadcast_to(
                    rows[:, states + n : states + n + 1], (reqs, LANES)
                )
        sum_ref[...] = jnp.zeros_like(sum_ref)

    accepted = acc_ref[...]
    for tile in range(BLOCK // LANES):
        cols = pl.ds(tile * LANES, LANES)
        decay = [
            jnp.broadcast_to(decay_ref[pl.ds(n, 1), cols], (reqs, LANES)) for n in range(states)
        ]
        state = [
            h0_ref[0, :, pl.ds(n * BLOCK + tile * LANES, LANES)].astype(jnp.float32)
            for n in range(states)
        ]
        values = conv_ref[:, cols].astype(jnp.float32)
        for t in range(draft):
            delta = dt_ref[pl.ds(t * reqs, reqs), cols]
            driven = delta * values[t * reqs : (t + 1) * reqs]
            chosen = accepted == t + 1
            totals = [None, None]
            for n in range(states):
                state[n] = jnp.exp2(delta * decay[n]) * state[n] + driven * b_ref[t * states + n]
                term = c_ref[t * states + n] * state[n]
                totals[n % 2] = term if totals[n % 2] is None else totals[n % 2] + term
                pltpu.store(pick_ref.at[pl.ds(n * reqs, reqs), :], state[n], mask=chosen)
            y_ref[pl.ds(t * reqs, reqs), cols] = totals[0] + totals[1]
        for r in range(reqs):
            ns_ref[pl.ds(r * states, states), cols] = pick_ref[pl.ds(r, states, stride=reqs), :]
    gate = gate_ref[...].astype(jnp.float32)
    mixed = y_ref[...] + skip_ref[...] * conv_ref[...].astype(jnp.float32)
    gated = (mixed * (gate / (1.0 + jnp.exp(-gate)))).astype(jnp.bfloat16)
    added = jnp.dot(gated, ow_ref[...], preferred_element_type=jnp.float32)
    for k in range(sum_ref.shape[0]):
        sum_ref[k] += added[:, k * LANES : (k + 1) * LANES]

    @pl.when(step == pl.num_programs(0) - 1)
    def _():
        for k in range(sum_ref.shape[0]):
            for r in range(reqs):
                rows = sum_ref[k, pl.ds(r, draft, stride=reqs), :]
                out_ref[r, :, pl.ds(k * LANES, LANES)] = rows.astype(jnp.bfloat16)


def scan_layer(h0, dt, conv_rows, projected, coeffs, accepted, decay2, skip, out_weight):
    blocks, reqs, _ = h0.shape
    tokens, inner = dt.shape
    draft = tokens // reqs
    states = decay2.shape[0]
    width = out_weight.shape[1]
    once = lambda j: (0, 0)
    cols = lambda j: (0, j)
    return pl.pallas_call(
        scan_kernel,
        grid=(blocks,),
        out_shape=(
            jax.ShapeDtypeStruct((reqs, draft, width), jnp.bfloat16),
            jax.ShapeDtypeStruct((reqs * states, inner), jnp.float32),
        ),
        in_specs=[
            pl.BlockSpec((1, reqs, states * BLOCK), lambda j: (j, 0, 0)),
            pl.BlockSpec((tokens, BLOCK), cols),
            pl.BlockSpec((tokens, BLOCK), cols),
            pl.BlockSpec((tokens, BLOCK), lambda j: (0, blocks + j)),
            pl.BlockSpec((tokens, 2 * states), once),
            pl.BlockSpec((reqs, LANES), once),
            pl.BlockSpec((states, BLOCK), cols),
            pl.BlockSpec((1, BLOCK), cols),
            pl.BlockSpec((BLOCK, width), lambda j: (j, 0)),
        ],
        out_specs=(
            pl.BlockSpec((reqs, draft, width), lambda j: (0, 0, 0)),
            pl.BlockSpec((reqs * states, BLOCK), cols),
        ),
        scratch_shapes=[
            pltpu.VMEM((draft * states, reqs, LANES), jnp.float32),
            pltpu.VMEM((draft * states, reqs, LANES), jnp.float32),
            pltpu.VMEM((states * reqs, LANES), jnp.float32),
            pltpu.VMEM((tokens, BLOCK), jnp.float32),
            pltpu.VMEM((width // LANES, tokens, LANES), jnp.float32),
        ],
        compiler_params=pltpu.CompilerParams(vmem_limit_bytes=32 << 20),
        cost_estimate=pl.CostEstimate(
            flops=2 * tokens * inner * width, bytes_accessed=8 << 20, transcendentals=tokens * inner * states
        ),
        name="scan_layer",
    )(h0, dt, conv_rows, projected, coeffs, accepted, decay2, skip, out_weight)


def exchange(values):
    return lax.all_to_all(values, "req", split_axis=0, concat_axis=0, tiled=True)


def split_float(values):
    high = values.astype(jnp.bfloat16)
    low = (values - high.astype(jnp.float32)).astype(jnp.bfloat16)
    return high, low


def gather_weights(x_weight, step_weight, vectors, groups):
    channels, mixed = x_weight.shape
    rank = step_weight.shape[0]
    count = vectors.shape[0]
    blocks = lax.axis_size("req")
    high, low = split_float(vectors)
    pad = (-2 * count) % (16 * groups)
    tail = jnp.concatenate([high, low, jnp.zeros((pad, channels), jnp.bfloat16)], axis=0)
    pieces = [x_weight.T, step_weight, tail]
    rows = [p.shape[0] // groups for p in pieces]
    stacked = jnp.concatenate([p.reshape(groups, -1, channels) for p in pieces], axis=1)
    mine = lax.dynamic_index_in_dim(stacked, lax.axis_index("grp"), 0, keepdims=False)
    share = mine.shape[0]
    sent = jnp.broadcast_to(mine[None], (blocks, share, channels))
    held = exchange(sent.reshape(blocks * share, channels))
    full = lax.all_gather(held, "grp", axis=0, tiled=True)
    full = full.reshape(groups, blocks, share, channels).swapaxes(1, 2)
    at = 0
    outs = []
    for size in rows:
        part = full[:, at : at + size].reshape(groups * size, blocks * channels)
        outs.append(part)
        at += size
    x_full, step_full, tail_full = outs
    tail_full = tail_full.astype(jnp.float32)
    return x_full, step_full, tail_full[:count] + tail_full[count : 2 * count]


def on_device(
    groups,
    hidden,
    norm_gain,
    in_weight,
    conv_weight,
    conv_bias,
    x_weight,
    step_weight,
    step_bias,
    log_decay,
    skip_gain,
    out_weight,
    old_states,
    old_edges,
    anchor,
    fresh_flag,
    accepted,
    request_ages,
):
    local_reqs, draft_len, width = hidden.shape
    inner_width = out_weight.shape[0]
    channels = conv_weight.shape[1]
    taps = conv_weight.shape[0]
    state_size = log_decay.shape[0]
    low_rank = step_weight.shape[0]
    span = old_edges.shape[1]
    all_reqs = anchor.shape[0]
    blocks = inner_width // channels
    tokens = draft_len * local_reqs

    arrived = exchange(
        pack(old_states, old_edges, blocks).reshape(all_reqs, (state_size + span) * channels)
    )
    old_slot = jnp.arange(all_reqs, dtype=jnp.int32)
    select = (anchor[:, None] == old_slot[None, :]) & (fresh_flag[:, None] == 0)

    def picked(mask, values):
        return jnp.dot(
            mask.astype(jnp.bfloat16), values, preferred_element_type=jnp.float32
        ).astype(jnp.bfloat16)

    edge_at = state_size * channels
    edges = jnp.concatenate(
        [
            picked(
                select & (span - e <= request_ages)[:, None],
                arrived[:, edge_at + e * channels : edge_at + (e + 1) * channels],
            )
            for e in range(span)
        ],
        axis=1,
    )
    history = exchange(edges).reshape(blocks, local_reqs, span, channels)
    history = history.transpose(2, 1, 0, 3).reshape(span, local_reqs, inner_width)
    starts = exchange(picked(select, arrived[:, :edge_at]))
    if channels == BLOCK:
        starts = starts.reshape(blocks, local_reqs, state_size * BLOCK)
    else:
        starts = starts.reshape(blocks, local_reqs, state_size, channels)
        starts = starts.transpose(1, 2, 0, 3).reshape(local_reqs, state_size, -1, BLOCK)
        starts = starts.transpose(2, 0, 1, 3).reshape(-1, local_reqs, state_size * BLOCK)

    vectors = jnp.concatenate(
        [conv_weight, conv_bias[None], step_bias[None], skip_gain[None], log_decay], axis=0
    )
    x_full, step_full, vectors = gather_weights(x_weight, step_weight, vectors, groups)
    conv_full = vectors[:taps]
    bias_full = vectors[taps]
    step_bias_full = vectors[taps + 1]
    skip_full = vectors[taps + 2 : taps + 3]
    decay2 = jnp.exp(vectors[taps + 3 :]) * (-LOG2E)

    token_major = jnp.swapaxes(hidden, 0, 1).reshape(tokens, width)
    normed = rms_normed(token_major, norm_gain)
    projected = jnp.dot(normed, in_weight, preferred_element_type=jnp.float32).astype(jnp.bfloat16)
    inner_part = projected[:, :inner_width].reshape(draft_len, local_reqs, inner_width)
    sequence = jnp.concatenate([history, inner_part], axis=0).astype(jnp.float32)
    running = bias_full + conv_full[0] * sequence[0:draft_len]
    for offset in range(1, taps):
        running = running + conv_full[offset] * sequence[offset : offset + draft_len]
    conv_rows = jax.nn.silu(running).astype(jnp.bfloat16).reshape(tokens, inner_width)
    mixed_rows = lax.dot_general(
        conv_rows, x_full, (((1,), (1,)), ((), ())), preferred_element_type=jnp.float32
    ).astype(jnp.bfloat16)
    dt = jax.nn.softplus(
        jnp.dot(mixed_rows[:, :low_rank], step_full, preferred_element_type=jnp.float32)
        + step_bias_full
    )
    coeffs = mixed_rows[:, low_rank:].astype(jnp.float32)
    mine = lax.dynamic_slice_in_dim(accepted, lax.axis_index("req") * local_reqs, local_reqs, 0)
    mine = jnp.broadcast_to(mine[:, None], (local_reqs, LANES))
    layer_out, new_states = scan_layer(
        starts, dt, conv_rows, projected, coeffs, mine, decay2, skip_full, out_weight
    )
    return layer_out, new_states.reshape(local_reqs, state_size, inner_width)


def solution(mesh):
    return jax.shard_map(
        functools.partial(on_device, mesh.shape["grp"]),
        mesh=mesh,
        in_specs=(
            P(("grp", "req"), None, None),
            P(),
            P(),
            P(None, "req"),
            P("req"),
            P("req", None),
            P(None, "req"),
            P("req"),
            P(None, "req"),
            P("req"),
            P(),
            P(("grp", "req"), None, None),
            P(("grp", "req"), None, None),
            P("grp"),
            P("grp"),
            P("grp"),
            P("grp"),
        ),
        out_specs=(P(("grp", "req"), None, None), P(("grp", "req"), None, None)),
        check_vma=False,
    )
```

```python
import functools

import jax
import jax.numpy as jnp
from jax import lax
from jax.experimental import pallas as pl
from jax.experimental.pallas import tpu as pltpu
from jax.sharding import PartitionSpec as P

EPS = 1e-05
LOG2E = 1.4426950408889634
LANES = 128
BLOCK = 256
SHARE = 88


def rms_normed(values_in, norm_gain):
    values = values_in.astype(jnp.float32)
    factor = lax.rsqrt(jnp.mean(values * values, axis=-1, keepdims=True) + EPS)
    return (values * factor * norm_gain).astype(jnp.bfloat16)


def pack_kernel(state_ref, edge_ref, out_ref, tile_ref):
    blocks, slots, _ = out_ref.shape
    width = state_ref.shape[1] // blocks
    states = state_ref.shape[0] // slots
    for dest in range(blocks):
        cols = pl.ds(dest * width, width)
        for part in range(width // LANES):
            at = dest * width + part * LANES
            tile = tile_ref.at[at // LANES]
            tile[...] = state_ref[:, pl.ds(at, LANES)]
            for n in range(states):
                rows = tile[pl.ds(n, slots, stride=states), :]
                out_ref[dest, :, pl.ds(n * width + part * LANES, LANES)] = rows.astype(jnp.bfloat16)
        for e in range(edge_ref.shape[0]):
            out_ref[dest, :, pl.ds((states + e) * width, width)] = edge_ref[e, :, cols]


def pack(old_states, old_edges, blocks):
    slots, states, inner = old_states.shape
    span = old_edges.shape[1]
    width = inner // blocks
    edges = jnp.swapaxes(old_edges, 0, 1)
    if width % LANES == 0 and slots == 8:
        return pl.pallas_call(
            pack_kernel,
            out_shape=jax.ShapeDtypeStruct((blocks, slots, (states + span) * width), jnp.bfloat16),
            in_specs=[pl.BlockSpec(memory_space=pltpu.VMEM)] * 2,
            out_specs=pl.BlockSpec(memory_space=pltpu.VMEM),
            scratch_shapes=[pltpu.VMEM((inner // LANES, slots * states, LANES), jnp.float32)],
            compiler_params=pltpu.CompilerParams(vmem_limit_bytes=16 << 20),
            name="pack_states",
        )(old_states.reshape(slots * states, inner), edges)
    lead = jnp.swapaxes(old_states.astype(jnp.bfloat16), 0, 1)
    both = jnp.concatenate([lead, edges], axis=0)
    both = both.reshape(states + span, slots, blocks, width)
    return both.transpose(2, 1, 0, 3).reshape(blocks, slots, (states + span) * width)


def share_kernel(group_ref, xt_ref, sw_ref, cw_ref, cb_ref, sb_ref, sk_ref, ld_ref, out_ref, vec_ref):
    rank = sw_ref.shape[0]
    groups = rank // 32
    vec_ref[...] = jnp.zeros_like(vec_ref)
    vec_ref[pl.ds(0, 4), :] = cw_ref[...]
    vec_ref[pl.ds(4, 1), :] = cb_ref[...]
    vec_ref[pl.ds(5, 1), :] = sb_ref[...]
    vec_ref[pl.ds(6, 1), :] = sk_ref[...]
    vec_ref[pl.ds(8, 16), :] = ld_ref[...]
    for k in range(groups):

        @pl.when(group_ref[0] == k)
        def _():
            vec = vec_ref[pl.ds(16 * (k % 2), 16), :]
            high = vec.astype(jnp.bfloat16).astype(jnp.float32)
            part = high if k < 2 else vec - high
            rows = [
                xt_ref[pl.ds(32 * k, 32), :].astype(jnp.float32),
                xt_ref[pl.ds(rank + 8 * k, 8), :].astype(jnp.float32),
                part[:8],
                sw_ref[pl.ds(32 * k, 32), :].astype(jnp.float32),
                part[8:],
            ]
            out_ref[...] = jnp.concatenate(rows, axis=0).astype(jnp.bfloat16)


def weight_share(groups, x_weight, step_weight, conv_weight, conv_bias, step_bias, skip_gain, log_decay):
    channels = x_weight.shape[0]
    rank = step_weight.shape[0]
    xt = x_weight.T
    group = lax.axis_index("grp").astype(jnp.int32)
    if channels % LANES == 0:
        return pl.pallas_call(
            share_kernel,
            out_shape=jax.ShapeDtypeStruct((SHARE, channels), jnp.bfloat16),
            in_specs=[pl.BlockSpec(memory_space=pltpu.SMEM)] + [pl.BlockSpec(memory_space=pltpu.VMEM)] * 7,
            out_specs=pl.BlockSpec(memory_space=pltpu.VMEM),
            scratch_shapes=[pltpu.VMEM((32, channels), jnp.float32)],
            name="weight_share",
        )(
            group[None], xt, step_weight, conv_weight, conv_bias[None], step_bias[None],
            skip_gain[None], log_decay,
        )
    vec = jnp.concatenate(
        [conv_weight, conv_bias[None], step_bias[None], skip_gain[None], jnp.zeros_like(conv_bias)[None], log_decay],
        axis=0,
    )
    vec = jnp.pad(vec, ((0, 8), (0, 0)))
    high = vec.astype(jnp.bfloat16)
    both = jnp.concatenate([high, (vec - high.astype(jnp.float32)).astype(jnp.bfloat16)], axis=0)
    both = both.reshape(4, 16, channels)
    stacked = jnp.concatenate(
        [
            xt[:rank].reshape(4, 32, channels),
            xt[rank:].reshape(4, 8, channels),
            both[:, :8],
            step_weight.reshape(4, 32, channels),
            both[:, 8:],
        ],
        axis=1,
    )
    return lax.dynamic_index_in_dim(stacked, group, 0, keepdims=False)


def doubled(values, axis):
    size = lax.axis_size(axis)
    bit = size // 2
    while bit:
        other = lax.ppermute(values, axis, [(i, i ^ bit) for i in range(size)])
        values = jnp.concatenate([values, other], axis=0)
        bit //= 2
    return values


def places(axis):
    size = lax.axis_size(axis)
    offset = jnp.arange(size, dtype=jnp.int32) ^ lax.axis_index(axis).astype(jnp.int32)
    place = jnp.zeros_like(offset)
    bit, top = 1, size // 2
    while top:
        place = place | jnp.where((offset & bit) != 0, top, 0)
        bit, top = bit * 2, top // 2
    return place


def block_weights(w_ref, q_ref, j_ref, j):
    at = j_ref[j]
    quarters = [w_ref.at[q_ref[q], at] for q in range(4)]
    f32 = jnp.float32
    xw = jnp.concatenate(
        [w[pl.ds(0, 32), :].astype(f32) for w in quarters] + [w[pl.ds(32, 8), :].astype(f32) for w in quarters],
        axis=0,
    ).astype(jnp.bfloat16)
    sw = jnp.concatenate([w[pl.ds(48, 32), :] for w in quarters], axis=0)
    first = [w[pl.ds(40, 8), :].astype(f32) for w in quarters]
    second = [w[pl.ds(80, 8), :].astype(f32) for w in quarters]
    high = jnp.concatenate([first[0], second[0], first[1]], axis=0)
    low = jnp.concatenate([first[2], second[2], first[3]], axis=0)
    return xw, sw, high + low


def silu(values):
    return values / (1.0 + jnp.exp(-values))


def convolved(sequence, vec, count):
    reqs = (sequence.shape[0] - count) // 3
    running = vec[4:5]
    for k in range(4):
        running = running + vec[k : k + 1] * sequence[k * reqs : k * reqs + count]
    return silu(running).astype(jnp.bfloat16)


def softplus(values):
    return jnp.maximum(values, 0.0) + jnp.log1p(jnp.exp(-jnp.abs(values)))


def mixed_of(conv, xw):
    return lax.dot_general(conv, xw, (((1,), (1,)), ((), ())), preferred_element_type=jnp.float32)


def early_kernel(q_ref, j_ref, inner_ref, w_ref, conv_ref, dt_ref, coef_ref, vec_ref):
    blocks = w_ref.shape[1]
    count = conv_ref.shape[0]
    rank = coef_ref.shape[1] * 4
    mixed = jnp.zeros((count, rank + coef_ref.shape[1]), jnp.float32)
    steps = []
    for j in range(blocks):
        cols = pl.ds(j * BLOCK, BLOCK)
        xw, sw, vec = block_weights(w_ref, q_ref, j_ref, j)
        conv = convolved(inner_ref[:, cols].astype(jnp.float32), vec, count)
        conv_ref[:, cols] = conv
        vec_ref[:, cols] = vec
        mixed = mixed + mixed_of(conv, xw)
        steps.append((sw, vec[5:6]))
    rounded = mixed.astype(jnp.bfloat16)
    coef_ref[...] = rounded[:, rank:].astype(jnp.float32)
    for j in range(blocks):
        cols = pl.ds(j * BLOCK, BLOCK)
        sw, bias = steps[j]
        dt_ref[:, cols] = softplus(
            jnp.dot(rounded[:, :rank], sw, preferred_element_type=jnp.float32) + bias
        )


def early(q_place, j_place, projected, weights, late):
    tokens = projected.shape[0]
    blocks = weights.shape[1]
    inner = blocks * BLOCK
    count = tokens - late
    smem = pl.BlockSpec(memory_space=pltpu.SMEM)
    return pl.pallas_call(
        early_kernel,
        grid=(1,),
        out_shape=(
            jax.ShapeDtypeStruct((count, inner), jnp.bfloat16),
            jax.ShapeDtypeStruct((count, inner), jnp.float32),
            jax.ShapeDtypeStruct((count, 32), jnp.float32),
            jax.ShapeDtypeStruct((24, inner), jnp.float32),
        ),
        in_specs=[
            smem,
            smem,
            pl.BlockSpec((tokens, inner), lambda i: (0, 0)),
            pl.BlockSpec(weights.shape, lambda i: (0, 0, 0, 0)),
        ],
        out_specs=(
            pl.BlockSpec((count, inner), lambda i: (0, 0)),
            pl.BlockSpec((count, inner), lambda i: (0, 0)),
            pl.BlockSpec((count, 32), lambda i: (0, 0)),
            pl.BlockSpec((24, inner), lambda i: (0, 0)),
        ),
        compiler_params=pltpu.CompilerParams(vmem_limit_bytes=32 << 20),
        cost_estimate=pl.CostEstimate(flops=140_000_000, bytes_accessed=4 << 20, transcendentals=800_000),
        name="early_tokens",
    )(q_place, j_place, projected, weights)


def scan_kernel(
    q_ref, j_ref, moved_ref, inner_ref, w_ref, dt_ref, conv_ref, gate_ref, coef_ref, acc_ref, vec_ref, ow_ref,
    out_ref, ns_ref, b_ref, c_ref, pick_ref, y_ref, sum_ref, dt_late, conv_late,
):
    step = pl.program_id(0)
    reqs, draft, _ = out_ref.shape
    states = 16
    blocks = moved_ref.shape[0]
    late = conv_late.shape[1]
    rank = coef_ref.shape[1] * 4

    def spread(rows, t):
        for n in range(states):
            b_ref[t * states + n] = jnp.broadcast_to(rows[:, n : n + 1], (reqs, LANES))
            c_ref[t * states + n] = jnp.broadcast_to(
                rows[:, states + n : states + n + 1], (reqs, LANES)
            )

    @pl.when(step == 0)
    def _():
        mixed = jnp.zeros((late, rank + coef_ref.shape[1]), jnp.float32)
        steps = []
        for j in range(blocks):
            xw, sw, vec = block_weights(w_ref, q_ref, j_ref, j)
            history = [
                moved_ref[j, :, pl.ds((states + e) * BLOCK, BLOCK)].astype(jnp.float32) for e in range(3)
            ]
            drafted = inner_ref[:, pl.ds(j * BLOCK, BLOCK)].astype(jnp.float32)[:late]
            conv = convolved(jnp.concatenate(history + [drafted], axis=0), vec, late)
            conv_late[j] = conv.astype(jnp.float32)
            mixed = mixed + mixed_of(conv, xw)
            steps.append((sw, vec[5:6]))
        rounded = mixed.astype(jnp.bfloat16)
        for j in range(blocks):
            sw, bias = steps[j]
            dt_late[j] = softplus(
                jnp.dot(rounded[:, :rank], sw, preferred_element_type=jnp.float32) + bias
            )
        coefs = rounded[:, rank:].astype(jnp.float32)
        for t in range(draft):
            if t * reqs < late:
                spread(coefs[t * reqs : (t + 1) * reqs], t)
            else:
                spread(coef_ref[pl.ds(t * reqs - late, reqs), :], t)
        sum_ref[...] = jnp.zeros_like(sum_ref)

    accepted = acc_ref[...]
    for tile in range(BLOCK // LANES):
        cols = pl.ds(tile * LANES, LANES)
        decay2 = jnp.exp(vec_ref[pl.ds(8, states), cols]) * (-LOG2E)
        decay = [jnp.broadcast_to(decay2[n : n + 1], (reqs, LANES)) for n in range(states)]
        skip = vec_ref[pl.ds(6, 1), cols]
        state = [
            moved_ref[step, :, pl.ds(n * BLOCK + tile * LANES, LANES)].astype(jnp.float32)
            for n in range(states)
        ]
        values = conv_ref[:, cols].astype(jnp.float32)
        for t in range(draft):
            at = t * reqs - late
            if at < 0:
                delta = dt_late[step, pl.ds(t * reqs, reqs), cols]
                value = conv_late[step, pl.ds(t * reqs, reqs), cols]
            else:
                delta = dt_ref[pl.ds(at, reqs), cols]
                value = values[at : at + reqs]
            driven = delta * value
            chosen = accepted == t + 1
            totals = [None, None]
            for n in range(states):
                state[n] = jnp.exp2(delta * decay[n]) * state[n] + driven * b_ref[t * states + n]
                term = c_ref[t * states + n] * state[n]
                totals[n % 2] = term if totals[n % 2] is None else totals[n % 2] + term
                pltpu.store(pick_ref.at[pl.ds(n * reqs, reqs), :], state[n], mask=chosen)
            y_ref[pl.ds(t * reqs, reqs), cols] = totals[0] + totals[1] + skip * value
        for r in range(reqs):
            ns_ref[pl.ds(r * states, states), cols] = pick_ref[pl.ds(r, states, stride=reqs), :]
    gated = (y_ref[...] * silu(gate_ref[...].astype(jnp.float32))).astype(jnp.bfloat16)
    added = jnp.dot(gated, ow_ref[...], preferred_element_type=jnp.float32)
    for k in range(sum_ref.shape[0]):
        sum_ref[k] += added[:, k * LANES : (k + 1) * LANES]

    @pl.when(step == pl.num_programs(0) - 1)
    def _():
        for k in range(sum_ref.shape[0]):
            for r in range(reqs):
                rows = sum_ref[k, pl.ds(r, draft, stride=reqs), :]
                out_ref[r, :, pl.ds(k * LANES, LANES)] = rows.astype(jnp.bfloat16)


def scan_layer(q_place, j_place, moved, weights, dt, conv_rows, projected, coeffs, accepted, vectors, out_weight):
    blocks, reqs, _ = moved.shape
    count, inner = dt.shape
    tokens = projected.shape[0]
    late = tokens - count
    draft = tokens // reqs
    states = 16
    width = out_weight.shape[1]
    smem = pl.BlockSpec(memory_space=pltpu.SMEM)
    once = lambda j: (0, 0)
    cols = lambda j: (0, j)
    return pl.pallas_call(
        scan_kernel,
        grid=(blocks,),
        out_shape=(
            jax.ShapeDtypeStruct((reqs, draft, width), jnp.bfloat16),
            jax.ShapeDtypeStruct((reqs * states, inner), jnp.float32),
        ),
        in_specs=[
            smem,
            smem,
            pl.BlockSpec(moved.shape, lambda j: (0, 0, 0)),
            pl.BlockSpec((32, inner), once),
            pl.BlockSpec(weights.shape, lambda j: (0, 0, 0, 0)),
            pl.BlockSpec((count, BLOCK), cols),
            pl.BlockSpec((count, BLOCK), cols),
            pl.BlockSpec((tokens, BLOCK), lambda j: (0, blocks + j)),
            pl.BlockSpec((count, 2 * states), once),
            pl.BlockSpec((reqs, LANES), once),
            pl.BlockSpec((24, BLOCK), cols),
            pl.BlockSpec((BLOCK, width), lambda j: (j, 0)),
        ],
        out_specs=(
            pl.BlockSpec((reqs, draft, width), lambda j: (0, 0, 0)),
            pl.BlockSpec((reqs * states, BLOCK), cols),
        ),
        scratch_shapes=[
            pltpu.VMEM((draft * states, reqs, LANES), jnp.float32),
            pltpu.VMEM((draft * states, reqs, LANES), jnp.float32),
            pltpu.VMEM((states * reqs, LANES), jnp.float32),
            pltpu.VMEM((tokens, BLOCK), jnp.float32),
            pltpu.VMEM((width // LANES, tokens, LANES), jnp.float32),
            pltpu.VMEM((blocks, late, BLOCK), jnp.float32),
            pltpu.VMEM((blocks, late, BLOCK), jnp.float32),
        ],
        compiler_params=pltpu.CompilerParams(vmem_limit_bytes=32 << 20),
        cost_estimate=pl.CostEstimate(
            flops=2 * tokens * inner * width, bytes_accessed=8 << 20, transcendentals=tokens * inner * states
        ),
        name="scan_layer",
    )(q_place, j_place, moved, projected, weights, dt, conv_rows, projected, coeffs, accepted, vectors, out_weight)


def exchange(values):
    return lax.all_to_all(values, "req", split_axis=0, concat_axis=0, tiled=True)


def select_kernel(mask_ref, arrived_ref, out_ref):
    width = arrived_ref.shape[1] // 19
    at = 16 * width
    spans = [(0, 0, at)] + [(e + 1, at + e * width, width) for e in range(3)]
    for which, start, size in spans:
        cols = pl.ds(start, size)
        out_ref[:, cols] = jnp.dot(
            mask_ref[which], arrived_ref[:, cols], preferred_element_type=jnp.float32
        ).astype(jnp.bfloat16)


def select(masks, arrived):
    if arrived.shape[1] % (19 * LANES) == 0:
        return pl.pallas_call(
            select_kernel,
            out_shape=jax.ShapeDtypeStruct(arrived.shape, jnp.bfloat16),
            in_specs=[pl.BlockSpec(memory_space=pltpu.VMEM)] * 2,
            out_specs=pl.BlockSpec(memory_space=pltpu.VMEM),
            compiler_params=pltpu.CompilerParams(vmem_limit_bytes=16 << 20),
            name="select_slots",
        )(masks, arrived)
    width = arrived.shape[1] // 19
    cut = [0] + [(16 + e) * width for e in range(4)]
    return jnp.concatenate(
        [
            jnp.dot(
                masks[i], arrived[:, cut[i] : cut[i + 1]], preferred_element_type=jnp.float32
            ).astype(jnp.bfloat16)
            for i in range(4)
        ],
        axis=1,
    )


def on_device(
    groups,
    hidden,
    norm_gain,
    in_weight,
    conv_weight,
    conv_bias,
    x_weight,
    step_weight,
    step_bias,
    log_decay,
    skip_gain,
    out_weight,
    old_states,
    old_edges,
    anchor,
    fresh_flag,
    accepted,
    request_ages,
):
    local_reqs, draft_len, width = hidden.shape
    inner_width = out_weight.shape[0]
    channels = conv_weight.shape[1]
    state_size = log_decay.shape[0]
    span = old_edges.shape[1]
    all_reqs = anchor.shape[0]
    blocks = inner_width // channels
    tokens = draft_len * local_reqs

    arrived = exchange(
        pack(old_states, old_edges, blocks).reshape(all_reqs, (state_size + span) * channels)
    )
    old_slot = jnp.arange(all_reqs, dtype=jnp.int32)
    chosen = (anchor[:, None] == old_slot[None, :]) & (fresh_flag[:, None] == 0)
    masks = jnp.stack([chosen] + [chosen & (span - e <= request_ages)[:, None] for e in range(span)])
    moved = exchange(select(masks.astype(jnp.bfloat16), arrived))

    share = weight_share(
        groups, x_weight, step_weight, conv_weight, conv_bias, step_bias, skip_gain, log_decay
    )
    weights = doubled(doubled(share[None], "req")[None], "grp")
    q_place, j_place = places("grp"), places("req")
    if channels != BLOCK:
        moved = moved.reshape(blocks, local_reqs, state_size + span, channels).transpose(1, 2, 0, 3)
        moved = moved.reshape(local_reqs, state_size + span, -1, BLOCK).transpose(2, 0, 1, 3)
        weights = jnp.take(weights, j_place, axis=1).swapaxes(1, 2)
        weights = weights.reshape(groups, SHARE, -1, BLOCK).swapaxes(1, 2)
        j_place = jnp.arange(inner_width // BLOCK, dtype=jnp.int32)
    moved = moved.reshape(inner_width // BLOCK, local_reqs, (state_size + span) * BLOCK)

    token_major = jnp.swapaxes(hidden, 0, 1).reshape(tokens, width)
    normed = rms_normed(token_major, norm_gain)
    projected = jnp.dot(normed, in_weight, preferred_element_type=jnp.float32).astype(jnp.bfloat16)
    conv_rows, dt, coeffs, vectors = early(q_place, j_place, projected, weights, span * local_reqs)
    mine = lax.dynamic_slice_in_dim(accepted, lax.axis_index("req") * local_reqs, local_reqs, 0)
    mine = jnp.broadcast_to(mine[:, None], (local_reqs, LANES))
    layer_out, new_states = scan_layer(
        q_place, j_place, moved, weights, dt, conv_rows, projected, coeffs, mine, vectors, out_weight
    )
    return layer_out, new_states.reshape(local_reqs, state_size, inner_width)


def solution(mesh):
    return jax.shard_map(
        functools.partial(on_device, mesh.shape["grp"]),
        mesh=mesh,
        in_specs=(
            P(("grp", "req"), None, None),
            P(),
            P(),
            P(None, "req"),
            P("req"),
            P("req", None),
            P(None, "req"),
            P("req"),
            P(None, "req"),
            P("req"),
            P(),
            P(("grp", "req"), None, None),
            P(("grp", "req"), None, None),
            P("grp"),
            P("grp"),
            P("grp"),
            P("grp"),
        ),
        out_specs=(P(("grp", "req"), None, None), P(("grp", "req"), None, None)),
        check_vma=False,
    )
```

```python
import functools

import jax
import jax.numpy as jnp
from jax import lax
from jax.experimental import pallas as pl
from jax.experimental.pallas import tpu as pltpu
from jax.sharding import PartitionSpec as P

EPS = 1e-05
LOG2E = 1.4426950408889634
LANES = 128
BLOCK = 256
SHARE = 88


def rms_normed(values_in, norm_gain):
    values = values_in.astype(jnp.float32)
    factor = lax.rsqrt(jnp.mean(values * values, axis=-1, keepdims=True) + EPS)
    return (values * factor * norm_gain).astype(jnp.bfloat16)


def in_hbm(values):
    return pltpu.with_memory_space_constraint(values, pltpu.HBM)


def pack_kernel(state_ref, edge_ref, out_ref, tile_ref, held_ref, send_ref, sems):
    blocks, slots, _ = out_ref.shape
    width = state_ref.shape[1] // blocks
    states = state_ref.shape[0] // slots
    per = width // LANES

    def load(tile):
        cols = pl.ds(tile * LANES, LANES)
        return pltpu.make_async_copy(state_ref.at[:, cols], tile_ref.at[tile], sems.at[0, tile])

    def store(dest):
        return pltpu.make_async_copy(send_ref.at[dest], out_ref.at[dest], sems.at[1, dest])

    edges = pltpu.make_async_copy(edge_ref, held_ref, sems.at[1, blocks])
    edges.start()
    for tile in range(blocks * per):
        load(tile).start()
    edges.wait()
    for dest in range(blocks):
        for e in range(edge_ref.shape[0]):
            at = (states + e) * width
            send_ref[dest, :, pl.ds(at, width)] = held_ref[e, :, pl.ds(dest * width, width)]
        for part in range(per):
            tile = dest * per + part
            load(tile).wait()
            for n in range(states):
                rows = tile_ref[tile, pl.ds(n, slots, stride=states), :]
                send_ref[dest, :, pl.ds(n * width + part * LANES, LANES)] = rows.astype(jnp.bfloat16)
        store(dest).start()
    for dest in range(blocks):
        store(dest).wait()


def pack(old_states, old_edges, blocks):
    slots, states, inner = old_states.shape
    span = old_edges.shape[1]
    width = inner // blocks
    edges = jnp.swapaxes(old_edges, 0, 1)
    if width % LANES == 0 and slots == 8:
        tiles = inner // LANES
        return pl.pallas_call(
            pack_kernel,
            out_shape=pltpu.HBM((blocks, slots, (states + span) * width), jnp.bfloat16),
            in_specs=[pl.BlockSpec(memory_space=pltpu.HBM)] * 2,
            out_specs=pl.BlockSpec(memory_space=pltpu.HBM),
            scratch_shapes=[
                pltpu.VMEM((tiles, slots * states, LANES), jnp.float32),
                pltpu.VMEM((span, slots, inner), jnp.bfloat16),
                pltpu.VMEM((blocks, slots, (states + span) * width), jnp.bfloat16),
                pltpu.SemaphoreType.DMA((2, max(tiles, blocks + 1))),
            ],
            compiler_params=pltpu.CompilerParams(vmem_limit_bytes=16 << 20),
            name="pack_states",
        )(in_hbm(old_states.reshape(slots * states, inner)), in_hbm(edges))
    lead = jnp.swapaxes(old_states.astype(jnp.bfloat16), 0, 1)
    both = jnp.concatenate([lead, edges], axis=0)
    both = both.reshape(states + span, slots, blocks, width)
    return both.transpose(2, 1, 0, 3).reshape(blocks, slots, (states + span) * width)


def share_kernel(group_ref, xt_ref, sw_ref, cw_ref, cb_ref, sb_ref, sk_ref, ld_ref, out_ref, vec_ref):
    rank = sw_ref.shape[0]
    groups = rank // 32
    vec_ref[...] = jnp.zeros_like(vec_ref)
    vec_ref[pl.ds(0, 4), :] = cw_ref[...]
    vec_ref[pl.ds(4, 1), :] = cb_ref[...]
    vec_ref[pl.ds(5, 1), :] = sb_ref[...]
    vec_ref[pl.ds(6, 1), :] = sk_ref[...]
    vec_ref[pl.ds(8, 16), :] = ld_ref[...]
    for k in range(groups):

        @pl.when(group_ref[0] == k)
        def _():
            vec = vec_ref[pl.ds(16 * (k % 2), 16), :]
            high = vec.astype(jnp.bfloat16).astype(jnp.float32)
            part = high if k < 2 else vec - high
            rows = [
                xt_ref[pl.ds(32 * k, 32), :].astype(jnp.float32),
                xt_ref[pl.ds(rank + 8 * k, 8), :].astype(jnp.float32),
                part[:8],
                sw_ref[pl.ds(32 * k, 32), :].astype(jnp.float32),
                part[8:],
            ]
            out_ref[...] = jnp.concatenate(rows, axis=0).astype(jnp.bfloat16)


def weight_share(groups, x_weight, step_weight, conv_weight, conv_bias, step_bias, skip_gain, log_decay):
    channels = x_weight.shape[0]
    rank = step_weight.shape[0]
    xt = x_weight.T
    group = lax.axis_index("grp").astype(jnp.int32)
    if channels % LANES == 0:
        return pl.pallas_call(
            share_kernel,
            out_shape=jax.ShapeDtypeStruct((SHARE, channels), jnp.bfloat16),
            in_specs=[pl.BlockSpec(memory_space=pltpu.SMEM)] + [pl.BlockSpec(memory_space=pltpu.VMEM)] * 7,
            out_specs=pl.BlockSpec(memory_space=pltpu.VMEM),
            scratch_shapes=[pltpu.VMEM((32, channels), jnp.float32)],
            name="weight_share",
        )(
            group[None], xt, step_weight, conv_weight, conv_bias[None], step_bias[None],
            skip_gain[None], log_decay,
        )
    vec = jnp.concatenate(
        [conv_weight, conv_bias[None], step_bias[None], skip_gain[None], jnp.zeros_like(conv_bias)[None], log_decay],
        axis=0,
    )
    vec = jnp.pad(vec, ((0, 8), (0, 0)))
    high = vec.astype(jnp.bfloat16)
    both = jnp.concatenate([high, (vec - high.astype(jnp.float32)).astype(jnp.bfloat16)], axis=0)
    both = both.reshape(4, 16, channels)
    stacked = jnp.concatenate(
        [
            xt[:rank].reshape(4, 32, channels),
            xt[rank:].reshape(4, 8, channels),
            both[:, :8],
            step_weight.reshape(4, 32, channels),
            both[:, 8:],
        ],
        axis=1,
    )
    return lax.dynamic_index_in_dim(stacked, group, 0, keepdims=False)


def doubled(values, axis):
    size = lax.axis_size(axis)
    bit = size // 2
    while bit:
        other = lax.ppermute(values, axis, [(i, i ^ bit) for i in range(size)])
        values = jnp.concatenate([values, other], axis=0)
        bit //= 2
    return values


def places(axis):
    size = lax.axis_size(axis)
    offset = jnp.arange(size, dtype=jnp.int32) ^ lax.axis_index(axis).astype(jnp.int32)
    place = jnp.zeros_like(offset)
    bit, top = 1, size // 2
    while top:
        place = place | jnp.where((offset & bit) != 0, top, 0)
        bit, top = bit * 2, top // 2
    return place


def block_weights(w_ref, q_ref, j_ref, j):
    at = j_ref[j]
    quarters = [w_ref.at[q_ref[q], at] for q in range(4)]
    f32 = jnp.float32
    xw = jnp.concatenate(
        [w[pl.ds(0, 32), :].astype(f32) for w in quarters] + [w[pl.ds(32, 8), :].astype(f32) for w in quarters],
        axis=0,
    ).astype(jnp.bfloat16)
    sw = jnp.concatenate([w[pl.ds(48, 32), :] for w in quarters], axis=0)
    first = [w[pl.ds(40, 8), :].astype(f32) for w in quarters]
    second = [w[pl.ds(80, 8), :].astype(f32) for w in quarters]
    high = jnp.concatenate([first[0], second[0], first[1]], axis=0)
    low = jnp.concatenate([first[2], second[2], first[3]], axis=0)
    return xw, sw, high + low


def silu(values):
    return values / (1.0 + jnp.exp(-values))


def convolved(sequence, vec, count):
    reqs = (sequence.shape[0] - count) // 3
    running = vec[4:5]
    for k in range(4):
        running = running + vec[k : k + 1] * sequence[k * reqs : k * reqs + count]
    return silu(running).astype(jnp.bfloat16)


def softplus(values):
    return jnp.maximum(values, 0.0) + jnp.log1p(jnp.exp(-jnp.abs(values)))


def mixed_of(conv, xw):
    return lax.dot_general(conv, xw, (((1,), (1,)), ((), ())), preferred_element_type=jnp.float32)


def spread(rows, t, b_ref, c_ref):
    reqs, both = rows.shape
    states = both // 2
    for n in range(states):
        b_ref[t * states + n] = jnp.broadcast_to(rows[:, n : n + 1], (reqs, LANES))
        c_ref[t * states + n] = jnp.broadcast_to(rows[:, states + n : states + n + 1], (reqs, LANES))


def before_kernel(q_ref, j_ref, proj_ref, w_ref, acc_ref, *refs):
    results, kept, (dt_ref, cv_ref, b_ref, dec_ref, sems) = refs[:10], refs[10:20], refs[20:]
    y_ref, sg_ref, sum_ref, at_ref, ga_ref, c_ref, xw_ref, sw_ref, vec_ref, x_ref = kept
    blocks = w_ref.shape[1]
    tiles, count, _ = y_ref.shape
    tokens = sg_ref.shape[1]
    late = tokens - count
    reqs = late // 3
    states = b_ref.shape[0] * reqs // count
    inner = blocks * BLOCK
    rank = sw_ref.shape[1]
    per = BLOCK // LANES
    copies = [pltpu.make_async_copy(kept[i], results[i], sems.at[i]) for i in range(len(kept))]
    mixed = jnp.zeros((count, rank + 2 * states), jnp.float32)
    for j in range(blocks):
        xw, sw, vec = block_weights(w_ref, q_ref, j_ref, j)
        values = proj_ref[:, pl.ds(j * BLOCK, BLOCK)].astype(jnp.float32)
        conv = convolved(values, vec, count)
        mixed = mixed + mixed_of(conv, xw)
        xw_ref[j] = xw
        sw_ref[j] = sw
        x_ref[j] = values[:late]
        vec_ref[j, pl.ds(0, 8), :] = vec[:8]
        decay2 = jnp.exp(vec[8:]) * (-LOG2E)
        vec_ref[j, pl.ds(8, states), :] = decay2
        full = conv.astype(jnp.float32)
        gate = silu(proj_ref[:, pl.ds(inner + j * BLOCK, BLOCK)].astype(jnp.float32))
        for k in range(per):
            tile = j * per + k
            lanes = slice(k * LANES, (k + 1) * LANES)
            cv_ref[tile] = full[:, lanes]
            sg_ref[tile] = gate[:, lanes]
            y_ref[tile] = vec[6:7, lanes] * full[:, lanes]
            for n in range(states):
                dec_ref[tile, n] = jnp.broadcast_to(decay2[n : n + 1, lanes], (reqs, LANES))
    for i in (1, 6, 7, 8, 9):
        copies[i].start()
    rounded = mixed.astype(jnp.bfloat16)
    for j in range(blocks):
        dt = softplus(
            jnp.dot(rounded[:, :rank], sw_ref[j], preferred_element_type=jnp.float32)
            + vec_ref[j, pl.ds(5, 1), :]
        )
        for k in range(per):
            dt_ref[j * per + k] = dt[:, k * LANES : (k + 1) * LANES]
    coefs = rounded[:, rank:].astype(jnp.float32)
    for t in range(count // reqs):
        spread(coefs[t * reqs : (t + 1) * reqs], t, b_ref, c_ref)
    copies[5].start()
    accepted = acc_ref[...]
    ga_ref[...] = jnp.zeros_like(ga_ref)
    at_ref[...] = jnp.zeros_like(at_ref)

    @pl.loop(0, tiles)
    def _(tile):
        state = [None] * states
        passed = None
        for t in range(count // reqs):
            rows = pl.ds(t * reqs, reqs)
            delta = dt_ref[tile, rows, :]
            passed = delta if t == 0 else passed + delta
            sum_ref[tile, rows, :] = passed
            driven = delta * cv_ref[tile, rows, :]
            chosen = accepted == t + 4
            pltpu.store(at_ref.at[tile], passed, mask=chosen)
            totals = [None, None]
            for n in range(states):
                at = t * states + n
                added = driven * b_ref[at]
                state[n] = added if t == 0 else jnp.exp2(delta * dec_ref[tile, n]) * state[n] + added
                term = c_ref[at] * state[n]
                totals[n % 2] = term if totals[n % 2] is None else totals[n % 2] + term
                pltpu.store(ga_ref.at[tile, pl.ds(n * reqs, reqs), :], state[n], mask=chosen)
            y_ref[tile, rows, :] = y_ref[tile, rows, :] + (totals[0] + totals[1])

    for i in (0, 2, 3, 4):
        copies[i].start()
    for copy in copies:
        copy.wait()


def before(q_place, j_place, projected, weights, accepted, late, states):
    tokens = projected.shape[0]
    blocks = weights.shape[1]
    tiles = blocks * (BLOCK // LANES)
    count = tokens - late
    reqs = accepted.shape[0]
    rank = 4 * 32
    smem = pl.BlockSpec(memory_space=pltpu.SMEM)
    vmem = pl.BlockSpec(memory_space=pltpu.VMEM)
    f32 = jnp.float32
    spots = count // reqs * states
    results = [
        ((tiles, count, LANES), f32),
        ((tiles, tokens, LANES), f32),
        ((tiles, count, LANES), f32),
        ((tiles, reqs, LANES), f32),
        ((tiles, states * reqs, LANES), f32),
        ((spots, reqs, LANES), f32),
        ((blocks, rank + 2 * states, BLOCK), jnp.bfloat16),
        ((blocks, rank, BLOCK), jnp.bfloat16),
        ((blocks, 24, BLOCK), f32),
        ((blocks, late, BLOCK), f32),
    ]
    return pl.pallas_call(
        before_kernel,
        out_shape=tuple(pltpu.HBM(shape, dtype) for shape, dtype in results),
        in_specs=[smem, smem, vmem, vmem, vmem],
        out_specs=(pl.BlockSpec(memory_space=pltpu.HBM),) * len(results),
        scratch_shapes=[pltpu.VMEM(shape, dtype) for shape, dtype in results]
        + [
            pltpu.VMEM((tiles, count, LANES), f32),
            pltpu.VMEM((tiles, count, LANES), f32),
            pltpu.VMEM((spots, reqs, LANES), f32),
            pltpu.VMEM((tiles, states, reqs, LANES), f32),
            pltpu.SemaphoreType.DMA((len(results),)),
        ],
        compiler_params=pltpu.CompilerParams(vmem_limit_bytes=24 << 20),
        cost_estimate=pl.CostEstimate(flops=200_000_000, bytes_accessed=8 << 20, transcendentals=4_000_000),
        name="before_states",
    )(q_place, j_place, projected, weights, accepted)


def after_kernel(moved_ref, acc_ref, *refs):
    given, (out_ref, ns_ref) = refs[:11], refs[11:13]
    held, refs = refs[13:24], refs[24:]
    new_ref, pick_ref, total_ref, dt_ref, cv_ref, b_ref, cl_ref, sems, ns_sem = refs
    y_ref, sg_ref, sum_ref, at_ref, ga_ref, c_ref, xw_ref, sw_ref, vec_ref, x_ref, ow_ref = held
    reqs, draft, _ = out_ref.shape
    blocks, late, _ = x_ref.shape
    tiles, count, _ = y_ref.shape
    states = ga_ref.shape[1] // reqs
    rank = sw_ref.shape[1]
    per = BLOCK // LANES

    def state_copy(j):
        return pltpu.make_async_copy(new_ref.at[j], ns_ref.at[:, pl.ds(j * BLOCK, BLOCK)], ns_sem.at[j])

    copies = [pltpu.make_async_copy(given[i], held[i], sems.at[i]) for i in range(len(held))]
    for i in (9, 8, 6, 7, 5, 2, 0, 1, 3, 4, 10):
        copies[i].start()
    for i in (9, 8, 6):
        copies[i].wait()
    mixed = jnp.zeros((late, rank + 2 * states), jnp.float32)
    for j in range(blocks):
        history = [
            moved_ref[j, :, pl.ds((states + e) * BLOCK, BLOCK)].astype(jnp.float32) for e in range(3)
        ]
        conv = convolved(jnp.concatenate(history + [x_ref[j]], axis=0), vec_ref[j], late)
        cv_ref[j] = conv.astype(jnp.float32)
        mixed = mixed + mixed_of(conv, xw_ref[j])
    rounded = mixed.astype(jnp.bfloat16)
    copies[7].wait()
    for j in range(blocks):
        dt_ref[j] = softplus(
            jnp.dot(rounded[:, :rank], sw_ref[j], preferred_element_type=jnp.float32)
            + vec_ref[j, pl.ds(5, 1), :]
        )
    coefs = rounded[:, rank:].astype(jnp.float32)
    for t in range(late // reqs):
        spread(coefs[t * reqs : (t + 1) * reqs], t, b_ref, cl_ref)
    accepted = acc_ref[...]
    for i in (5, 2, 0, 1, 3, 4, 10):
        copies[i].wait()
    for j in range(blocks):
        gated = []
        for k in range(per):
            tile = j * per + k
            lanes = pl.ds(k * LANES, LANES)
            skip = vec_ref[j, pl.ds(6, 1), lanes]
            state = [
                moved_ref[j, :, pl.ds(n * BLOCK + k * LANES, LANES)].astype(jnp.float32)
                for n in range(states)
            ]
            decay = [
                jnp.broadcast_to(vec_ref[j, pl.ds(8 + n, 1), lanes], (reqs, LANES))
                for n in range(states)
            ]
            outs = []
            for t in range(late // reqs):
                rows = pl.ds(t * reqs, reqs)
                delta = dt_ref[j, rows, lanes]
                value = cv_ref[j, rows, lanes]
                driven = delta * value
                chosen = accepted == t + 1
                totals = [skip * value, None]
                for n in range(states):
                    at = t * states + n
                    state[n] = jnp.exp2(delta * decay[n]) * state[n] + driven * b_ref[at]
                    term = cl_ref[at] * state[n]
                    totals[n % 2] = term if totals[n % 2] is None else totals[n % 2] + term
                    pltpu.store(pick_ref.at[tile, pl.ds(n * reqs, reqs), :], state[n], mask=chosen)
                outs.append(totals[0] + totals[1])
            beyond = accepted > late // reqs
            passed = at_ref[tile]
            for n in range(states):
                keep = pl.ds(n * reqs, reqs)
                value = jnp.exp2(passed * decay[n]) * state[n] + ga_ref[tile, keep, :]
                pltpu.store(pick_ref.at[tile, keep, :], value, mask=beyond)
            for t in range(count // reqs):
                rows = pl.ds(t * reqs, reqs)
                passed = sum_ref[tile, rows, :]
                totals = [y_ref[tile, rows, :], None]
                for n in range(states):
                    term = c_ref[t * states + n] * (jnp.exp2(passed * decay[n]) * state[n])
                    totals[n % 2] = term if totals[n % 2] is None else totals[n % 2] + term
                outs.append(totals[0] + totals[1])
            for r in range(reqs):
                new_ref[j, pl.ds(r * states, states), lanes] = pick_ref[
                    tile, pl.ds(r, states, stride=reqs), :
                ]
            gated.append(jnp.concatenate(outs, axis=0) * sg_ref[tile])
        state_copy(j).start()
        added = jnp.dot(
            jnp.concatenate(gated, axis=1).astype(jnp.bfloat16),
            ow_ref[pl.ds(j * BLOCK, BLOCK), :],
            preferred_element_type=jnp.float32,
        )
        for k in range(total_ref.shape[0]):
            part = added[:, k * LANES : (k + 1) * LANES]
            total_ref[k] = part if j == 0 else total_ref[k] + part
    for k in range(total_ref.shape[0]):
        for r in range(reqs):
            rows = total_ref[k, pl.ds(r, draft, stride=reqs), :]
            out_ref[r, :, pl.ds(k * LANES, LANES)] = rows.astype(jnp.bfloat16)
    for j in range(blocks):
        state_copy(j).wait()


def after(moved, accepted, early, out_weight):
    blocks, reqs, _ = moved.shape
    tiles, tokens, _ = early[1].shape
    states = early[4].shape[1] // reqs
    late = early[9].shape[1]
    draft = tokens // reqs
    inner, width = out_weight.shape
    vmem = pl.BlockSpec(memory_space=pltpu.VMEM)
    hbm = pl.BlockSpec(memory_space=pltpu.HBM)
    f32 = jnp.float32
    spots = late // reqs * states
    given = tuple(in_hbm(x) for x in (*early, out_weight))
    return pl.pallas_call(
        after_kernel,
        out_shape=(
            jax.ShapeDtypeStruct((reqs, draft, width), jnp.bfloat16),
            jax.ShapeDtypeStruct((reqs * states, inner), f32),
        ),
        in_specs=[vmem] * 2 + [hbm] * len(given),
        out_specs=(vmem, hbm),
        scratch_shapes=[pltpu.VMEM(x.shape, x.dtype) for x in given]
        + [
            pltpu.VMEM((blocks, reqs * states, BLOCK), f32),
            pltpu.VMEM((tiles, states * reqs, LANES), f32),
            pltpu.VMEM((width // LANES, tokens, LANES), f32),
            pltpu.VMEM((blocks, late, BLOCK), f32),
            pltpu.VMEM((blocks, late, BLOCK), f32),
            pltpu.VMEM((spots, reqs, LANES), f32),
            pltpu.VMEM((spots, reqs, LANES), f32),
            pltpu.SemaphoreType.DMA((len(given),)),
            pltpu.SemaphoreType.DMA((blocks,)),
        ],
        compiler_params=pltpu.CompilerParams(vmem_limit_bytes=24 << 20),
        cost_estimate=pl.CostEstimate(
            flops=2 * tokens * inner * width, bytes_accessed=12 << 20, transcendentals=4_000_000
        ),
        name="after_states",
    )(moved, accepted, *given)


def exchange(values):
    return lax.all_to_all(values, "req", split_axis=0, concat_axis=0, tiled=True)


def select_kernel(mask_ref, arrived_ref, out_ref):
    width = arrived_ref.shape[1] // 19
    at = 16 * width
    spans = [(0, 0, at)] + [(e + 1, at + e * width, width) for e in range(3)]
    for which, start, size in spans:
        cols = pl.ds(start, size)
        out_ref[:, cols] = jnp.dot(
            mask_ref[which], arrived_ref[:, cols], preferred_element_type=jnp.float32
        ).astype(jnp.bfloat16)


def select(masks, arrived):
    if arrived.shape[1] % (19 * LANES) == 0:
        return pl.pallas_call(
            select_kernel,
            out_shape=jax.ShapeDtypeStruct(arrived.shape, jnp.bfloat16),
            in_specs=[pl.BlockSpec(memory_space=pltpu.VMEM)] * 2,
            out_specs=pl.BlockSpec(memory_space=pltpu.VMEM),
            compiler_params=pltpu.CompilerParams(vmem_limit_bytes=16 << 20),
            name="select_slots",
        )(masks, arrived)
    width = arrived.shape[1] // 19
    cut = [0] + [(16 + e) * width for e in range(4)]
    return jnp.concatenate(
        [
            jnp.dot(
                masks[i], arrived[:, cut[i] : cut[i + 1]], preferred_element_type=jnp.float32
            ).astype(jnp.bfloat16)
            for i in range(4)
        ],
        axis=1,
    )


def on_device(
    groups,
    hidden,
    norm_gain,
    in_weight,
    conv_weight,
    conv_bias,
    x_weight,
    step_weight,
    step_bias,
    log_decay,
    skip_gain,
    out_weight,
    old_states,
    old_edges,
    anchor,
    fresh_flag,
    accepted,
    request_ages,
):
    local_reqs, draft_len, width = hidden.shape
    inner_width = out_weight.shape[0]
    channels = conv_weight.shape[1]
    state_size = log_decay.shape[0]
    span = old_edges.shape[1]
    all_reqs = anchor.shape[0]
    blocks = inner_width // channels
    tokens = draft_len * local_reqs

    arrived = exchange(
        pack(old_states, old_edges, blocks).reshape(all_reqs, (state_size + span) * channels)
    )
    old_slot = jnp.arange(all_reqs, dtype=jnp.int32)
    chosen = (anchor[:, None] == old_slot[None, :]) & (fresh_flag[:, None] == 0)
    masks = jnp.stack([chosen] + [chosen & (span - e <= request_ages)[:, None] for e in range(span)])
    token_major = jnp.swapaxes(hidden, 0, 1).reshape(tokens, width)
    normed = rms_normed(token_major, norm_gain)
    projected = jnp.dot(normed, in_weight, preferred_element_type=jnp.float32).astype(jnp.bfloat16)
    masks, projected = lax.optimization_barrier((masks.astype(jnp.bfloat16), projected))
    moved = exchange(select(masks, arrived))

    share = weight_share(
        groups, x_weight, step_weight, conv_weight, conv_bias, step_bias, skip_gain, log_decay
    )
    weights = doubled(doubled(share[None], "req")[None], "grp")
    q_place, j_place = places("grp"), places("req")
    if channels != BLOCK:
        moved = moved.reshape(blocks, local_reqs, state_size + span, channels).transpose(1, 2, 0, 3)
        moved = moved.reshape(local_reqs, state_size + span, -1, BLOCK).transpose(2, 0, 1, 3)
        weights = jnp.take(weights, j_place, axis=1).swapaxes(1, 2)
        weights = weights.reshape(groups, SHARE, -1, BLOCK).swapaxes(1, 2)
        j_place = jnp.arange(inner_width // BLOCK, dtype=jnp.int32)
    moved = moved.reshape(inner_width // BLOCK, local_reqs, (state_size + span) * BLOCK)

    mine = lax.dynamic_slice_in_dim(accepted, lax.axis_index("req") * local_reqs, local_reqs, 0)
    mine = jnp.broadcast_to(mine[:, None], (local_reqs, LANES))
    early = before(q_place, j_place, projected, weights, mine, span * local_reqs, state_size)
    layer_out, new_states = after(moved, mine, early, out_weight)
    return layer_out, new_states.reshape(local_reqs, state_size, inner_width)


def solution(mesh):
    return jax.shard_map(
        functools.partial(on_device, mesh.shape["grp"]),
        mesh=mesh,
        in_specs=(
            P(("grp", "req"), None, None),
            P(),
            P(),
            P(None, "req"),
            P("req"),
            P("req", None),
            P(None, "req"),
            P("req"),
            P(None, "req"),
            P("req"),
            P(),
            P(("grp", "req"), None, None),
            P(("grp", "req"), None, None),
            P("grp"),
            P("grp"),
            P("grp"),
            P("grp"),
        ),
        out_specs=(P(("grp", "req"), None, None), P(("grp", "req"), None, None)),
        check_vma=False,
    )
```

```python
import functools

import jax
import jax.numpy as jnp
from jax import lax
from jax.experimental import pallas as pl
from jax.experimental.pallas import tpu as pltpu
from jax.sharding import PartitionSpec as P

EPS = 1e-05
LOG2E = 1.4426950408889634
LANES = 128
BLOCK = 256
SHARE = 88


def rms_normed(values_in, norm_gain):
    values = values_in.astype(jnp.float32)
    factor = lax.rsqrt(jnp.mean(values * values, axis=-1, keepdims=True) + EPS)
    return (values * factor * norm_gain).astype(jnp.bfloat16)


def in_hbm(values):
    return pltpu.with_memory_space_constraint(values, pltpu.HBM)


def send_kernel(
    group_ref, state_ref, edge_ref, xt_ref, sw_ref, cw_ref, cb_ref, sb_ref, sk_ref, ld_ref,
    out_ref, share_ref,
    tile_ref, held_ref, send_ref, xt_in, sw_in, vec_ref, sems, few,
):
    blocks, slots, _ = out_ref.shape
    width = state_ref.shape[1] // blocks
    states = state_ref.shape[0] // slots
    per = width // LANES
    rank = sw_ref.shape[0]

    def load(tile):
        cols = pl.ds(tile * LANES, LANES)
        return pltpu.make_async_copy(state_ref.at[:, cols], tile_ref.at[tile], sems.at[0, tile])

    def store(dest):
        return pltpu.make_async_copy(send_ref.at[dest], out_ref.at[dest], sems.at[1, dest])

    small = [
        (edge_ref, held_ref),
        (xt_ref, xt_in),
        (sw_ref, sw_in),
        (cw_ref, vec_ref.at[pl.ds(0, 4), :]),
        (cb_ref, vec_ref.at[pl.ds(4, 1), :]),
        (sb_ref, vec_ref.at[pl.ds(5, 1), :]),
        (sk_ref, vec_ref.at[pl.ds(6, 1), :]),
        (ld_ref, vec_ref.at[pl.ds(8, 16), :]),
    ]
    copies = [pltpu.make_async_copy(x, y, few.at[i]) for i, (x, y) in enumerate(small)]
    vec_ref[pl.ds(7, 1), :] = jnp.zeros((1, width), jnp.float32)
    vec_ref[pl.ds(24, 8), :] = jnp.zeros((8, width), jnp.float32)
    for copy in copies:
        copy.start()
    for tile in range(blocks * per):
        load(tile).start()
    for copy in copies:
        copy.wait()
    for k in range(4):

        @pl.when(group_ref[0] == k)
        def _():
            vec = vec_ref[pl.ds(16 * (k % 2), 16), :]
            high = vec.astype(jnp.bfloat16).astype(jnp.float32)
            part = high if k < 2 else vec - high
            rows = [
                xt_in[pl.ds(32 * k, 32), :].astype(jnp.float32),
                xt_in[pl.ds(rank + 8 * k, 8), :].astype(jnp.float32),
                part[:8],
                sw_in[pl.ds(32 * k, 32), :].astype(jnp.float32),
                part[8:],
            ]
            share_ref[...] = jnp.concatenate(rows, axis=0).astype(jnp.bfloat16)

    for dest in range(blocks):
        for e in range(edge_ref.shape[0]):
            at = (states + e) * width
            send_ref[dest, :, pl.ds(at, width)] = held_ref[e, :, pl.ds(dest * width, width)]
        for part in range(per):
            tile = dest * per + part
            load(tile).wait()
            for n in range(states):
                rows = tile_ref[tile, pl.ds(n, slots, stride=states), :]
                send_ref[dest, :, pl.ds(n * width + part * LANES, LANES)] = rows.astype(jnp.bfloat16)
        store(dest).start()
    for dest in range(blocks):
        store(dest).wait()


def prepared(
    old_states, old_edges, x_weight, step_weight, conv_weight, conv_bias, step_bias, skip_gain, log_decay
):
    slots, states, inner = old_states.shape
    span = old_edges.shape[1]
    width = x_weight.shape[0]
    blocks = inner // width
    rank = step_weight.shape[0]
    edges = jnp.swapaxes(old_edges, 0, 1)
    xt = x_weight.T
    group = lax.axis_index("grp").astype(jnp.int32)
    if width % LANES == 0 and slots == 8:
        tiles = inner // LANES
        vmem = pl.BlockSpec(memory_space=pltpu.VMEM)
        hbm = pl.BlockSpec(memory_space=pltpu.HBM)
        given = (
            old_states.reshape(slots * states, inner), edges, xt, step_weight, conv_weight,
            conv_bias[None], step_bias[None], skip_gain[None], log_decay,
        )
        return pl.pallas_call(
            send_kernel,
            out_shape=(
                pltpu.HBM((blocks, slots, (states + span) * width), jnp.bfloat16),
                jax.ShapeDtypeStruct((SHARE, width), jnp.bfloat16),
            ),
            in_specs=[pl.BlockSpec(memory_space=pltpu.SMEM)] + [hbm] * len(given),
            out_specs=(hbm, vmem),
            scratch_shapes=[
                pltpu.VMEM((tiles, slots * states, LANES), jnp.float32),
                pltpu.VMEM((span, slots, inner), jnp.bfloat16),
                pltpu.VMEM((blocks, slots, (states + span) * width), jnp.bfloat16),
                pltpu.VMEM(xt.shape, jnp.bfloat16),
                pltpu.VMEM(step_weight.shape, jnp.bfloat16),
                pltpu.VMEM((32, width), jnp.float32),
                pltpu.SemaphoreType.DMA((2, tiles)),
                pltpu.SemaphoreType.DMA((8,)),
            ],
            compiler_params=pltpu.CompilerParams(vmem_limit_bytes=16 << 20),
            name="send_states",
        )(group[None], *[in_hbm(x) for x in given])
    lead = jnp.swapaxes(old_states.astype(jnp.bfloat16), 0, 1)
    both = jnp.concatenate([lead, edges], axis=0)
    both = both.reshape(states + span, slots, blocks, width)
    packed = both.transpose(2, 1, 0, 3).reshape(blocks, slots, (states + span) * width)
    none = jnp.zeros_like(conv_bias)[None]
    vec = jnp.concatenate(
        [conv_weight, conv_bias[None], step_bias[None], skip_gain[None], none, log_decay], axis=0
    )
    vec = jnp.pad(vec, ((0, 8), (0, 0)))
    high = vec.astype(jnp.bfloat16)
    halves = jnp.concatenate([high, (vec - high.astype(jnp.float32)).astype(jnp.bfloat16)], axis=0)
    halves = halves.reshape(4, 16, width)
    stacked = jnp.concatenate(
        [
            xt[:rank].reshape(4, 32, width),
            xt[rank:].reshape(4, 8, width),
            halves[:, :8],
            step_weight.reshape(4, 32, width),
            halves[:, 8:],
        ],
        axis=1,
    )
    return packed, lax.dynamic_index_in_dim(stacked, group, 0, keepdims=False)


def moved_by(values, axis, bits):
    return lax.ppermute(values, axis, [(i, i ^ bits) for i in range(lax.axis_size(axis))])


def doubled(values, axis, bit):
    while bit:
        values = jnp.concatenate([values, moved_by(values, axis, bit)], axis=0)
        bit //= 2
    return values


def places(axis):
    size = lax.axis_size(axis)
    offset = jnp.arange(size, dtype=jnp.int32) ^ lax.axis_index(axis).astype(jnp.int32)
    place = jnp.zeros_like(offset)
    bit, top = 1, size // 2
    while top:
        place = place | jnp.where((offset & bit) != 0, top, 0)
        bit, top = bit * 2, top // 2
    return place


def block_weights(w_ref, q_ref, j_ref, j):
    at = j_ref[j]
    quarters = [w_ref.at[q_ref[q], at] for q in range(4)]
    f32 = jnp.float32
    xw = jnp.concatenate(
        [w[pl.ds(0, 32), :].astype(f32) for w in quarters] + [w[pl.ds(32, 8), :].astype(f32) for w in quarters],
        axis=0,
    ).astype(jnp.bfloat16)
    sw = jnp.concatenate([w[pl.ds(48, 32), :] for w in quarters], axis=0)
    first = [w[pl.ds(40, 8), :].astype(f32) for w in quarters]
    second = [w[pl.ds(80, 8), :].astype(f32) for w in quarters]
    high = jnp.concatenate([first[0], second[0], first[1]], axis=0)
    low = jnp.concatenate([first[2], second[2], first[3]], axis=0)
    return xw, sw, high + low


def silu(values):
    return values / (1.0 + jnp.exp(-values))


def convolved(sequence, vec, count):
    reqs = (sequence.shape[0] - count) // 3
    running = vec[4:5]
    for k in range(4):
        running = running + vec[k : k + 1] * sequence[k * reqs : k * reqs + count]
    return silu(running).astype(jnp.bfloat16)


def softplus(values):
    return jnp.maximum(values, 0.0) + jnp.log1p(jnp.exp(-jnp.abs(values)))


def mixed_of(conv, xw):
    return lax.dot_general(conv, xw, (((1,), (1,)), ((), ())), preferred_element_type=jnp.float32)


def spread(rows, t, b_ref, c_ref):
    reqs, both = rows.shape
    states = both // 2
    for n in range(states):
        b_ref[t * states + n] = jnp.broadcast_to(rows[:, n : n + 1], (reqs, LANES))
        c_ref[t * states + n] = jnp.broadcast_to(rows[:, states + n : states + n + 1], (reqs, LANES))


def before_kernel(
    q_ref, j_ref, proj_ref, w_ref, acc_ref,
    rows_out, at_ref, coef_ref, xw_ref, sw_ref, vec_ref, x_ref,
    rows_ref, dt_ref, cv_ref, b_ref, c_ref, dec_ref, sems,
):
    blocks = w_ref.shape[1]
    tiles, count, _ = dt_ref.shape
    tokens = proj_ref.shape[0]
    late = tokens - count
    reqs = late // 3
    states = b_ref.shape[0] * reqs // count
    inner = blocks * BLOCK
    rank = sw_ref.shape[1]
    per = BLOCK // LANES
    y_at, sum_at, gate_at, state_at = row_offsets(count, tokens)

    def copy(j):
        some = pl.ds(j * per, per)
        return pltpu.make_async_copy(rows_ref.at[some], rows_out.at[some], sems.at[j])

    mixed = jnp.zeros((count, rank + 2 * states), jnp.float32)
    for j in range(blocks):
        xw, sw, vec = block_weights(w_ref, q_ref, j_ref, j)
        values = proj_ref[:, pl.ds(j * BLOCK, BLOCK)].astype(jnp.float32)
        conv = convolved(values, vec, count)
        mixed = mixed + mixed_of(conv, xw)
        xw_ref[j] = xw
        sw_ref[j] = sw
        x_ref[j] = values[:late]
        vec_ref[j, pl.ds(0, 8), :] = vec[:8]
        decay2 = jnp.exp(vec[8:]) * (-LOG2E)
        vec_ref[j, pl.ds(8, states), :] = decay2
        full = conv.astype(jnp.float32)
        gate = silu(proj_ref[:, pl.ds(inner + j * BLOCK, BLOCK)].astype(jnp.float32))
        for k in range(per):
            tile = j * per + k
            lanes = slice(k * LANES, (k + 1) * LANES)
            cv_ref[tile] = full[:, lanes]
            rows_ref[tile, pl.ds(gate_at, tokens), :] = gate[:, lanes]
            rows_ref[tile, pl.ds(y_at, count), :] = vec[6:7, lanes] * full[:, lanes]
            for n in range(states):
                dec_ref[tile, n] = jnp.broadcast_to(decay2[n : n + 1, lanes], (reqs, LANES))
    rounded = mixed.astype(jnp.bfloat16)
    for j in range(blocks):
        dt = softplus(
            jnp.dot(rounded[:, :rank], sw_ref[j], preferred_element_type=jnp.float32)
            + vec_ref[j, pl.ds(5, 1), :]
        )
        for k in range(per):
            dt_ref[j * per + k] = dt[:, k * LANES : (k + 1) * LANES]
    coefs = rounded[:, rank:].astype(jnp.float32)
    coef_ref[...] = coefs
    for t in range(count // reqs):
        spread(coefs[t * reqs : (t + 1) * reqs], t, b_ref, c_ref)
    accepted = acc_ref[...]
    at_ref[...] = jnp.zeros_like(at_ref)

    @pl.loop(0, tiles)
    def _(tile):
        state = [None] * states
        passed = None
        rows_ref[tile, pl.ds(state_at, states * reqs), :] = jnp.zeros((states * reqs, LANES), jnp.float32)
        for t in range(count // reqs):
            delta = dt_ref[tile, pl.ds(t * reqs, reqs), :]
            passed = delta if t == 0 else passed + delta
            rows_ref[tile, pl.ds(sum_at + t * reqs, reqs), :] = passed
            driven = delta * cv_ref[tile, pl.ds(t * reqs, reqs), :]
            chosen = accepted == t + late // reqs + 1
            pltpu.store(at_ref.at[tile], passed, mask=chosen)
            totals = [rows_ref[tile, pl.ds(y_at + t * reqs, reqs), :], None]
            for n in range(states):
                at = t * states + n
                added = driven * b_ref[at]
                state[n] = added if t == 0 else jnp.exp2(delta * dec_ref[tile, n]) * state[n] + added
                term = c_ref[at] * state[n]
                totals[n % 2] = term if totals[n % 2] is None else totals[n % 2] + term
                pltpu.store(
                    rows_ref.at[tile, pl.ds(state_at + n * reqs, reqs), :], state[n], mask=chosen
                )
            rows_ref[tile, pl.ds(y_at + t * reqs, reqs), :] = totals[0] + totals[1]

        @pl.when(tile % per == per - 1)
        def _():
            copy(tile // per).start()

    for j in range(blocks):
        copy(j).wait()


def row_offsets(count, tokens):
    return 0, count, 2 * count, 2 * count + tokens


def before(q_place, j_place, projected, weights, accepted, late, states):
    tokens = projected.shape[0]
    blocks = weights.shape[1]
    tiles = blocks * (BLOCK // LANES)
    count = tokens - late
    reqs = accepted.shape[0]
    rank = 4 * 32
    smem = pl.BlockSpec(memory_space=pltpu.SMEM)
    vmem = pl.BlockSpec(memory_space=pltpu.VMEM)
    f32 = jnp.float32
    spots = count // reqs * states
    rows = (tiles, 2 * count + tokens + states * reqs, LANES)
    return pl.pallas_call(
        before_kernel,
        out_shape=(
            pltpu.HBM(rows, f32),
            jax.ShapeDtypeStruct((tiles, reqs, LANES), f32),
            jax.ShapeDtypeStruct((count, 2 * states), f32),
            jax.ShapeDtypeStruct((blocks, rank + 2 * states, BLOCK), jnp.bfloat16),
            jax.ShapeDtypeStruct((blocks, rank, BLOCK), jnp.bfloat16),
            jax.ShapeDtypeStruct((blocks, 24, BLOCK), f32),
            jax.ShapeDtypeStruct((blocks, late, BLOCK), f32),
        ),
        in_specs=[smem, smem, vmem, vmem, vmem],
        out_specs=(pl.BlockSpec(memory_space=pltpu.HBM),) + (vmem,) * 6,
        scratch_shapes=[
            pltpu.VMEM(rows, f32),
            pltpu.VMEM((tiles, count, LANES), f32),
            pltpu.VMEM((tiles, count, LANES), f32),
            pltpu.VMEM((spots, reqs, LANES), f32),
            pltpu.VMEM((spots, reqs, LANES), f32),
            pltpu.VMEM((tiles, states, reqs, LANES), f32),
            pltpu.SemaphoreType.DMA((blocks,)),
        ],
        compiler_params=pltpu.CompilerParams(vmem_limit_bytes=24 << 20),
        cost_estimate=pl.CostEstimate(flops=200_000_000, bytes_accessed=8 << 20, transcendentals=4_000_000),
        name="before_states",
    )(q_place, j_place, projected, weights, accepted)


def after_kernel(
    moved_ref, acc_ref, at_ref, coef_ref, xw_ref, sw_ref, vec_ref, x_ref, rows_in, ow_in,
    out_ref, ns_ref,
    rows_ref, ow_ref, new_ref, pick_ref, total_ref, dt_ref, cv_ref, b_ref, c_ref, sems,
):
    reqs, draft, _ = out_ref.shape
    blocks, late, _ = x_ref.shape
    tiles = rows_ref.shape[0]
    tokens = reqs * draft
    count = tokens - late
    states = coef_ref.shape[1] // 2
    rank = sw_ref.shape[1]
    per = BLOCK // LANES
    y_at, sum_at, gate_at, state_at = row_offsets(count, tokens)

    def copies(j):
        some, cols = pl.ds(j * per, per), pl.ds(j * BLOCK, BLOCK)
        return [
            pltpu.make_async_copy(rows_in.at[some], rows_ref.at[some], sems.at[0, j]),
            pltpu.make_async_copy(ow_in.at[cols, :], ow_ref.at[cols, :], sems.at[1, j]),
            pltpu.make_async_copy(new_ref.at[j], ns_ref.at[:, cols], sems.at[2, j]),
        ]

    for j in range(blocks):
        for copy in copies(j)[:2]:
            copy.start()
    mixed = jnp.zeros((late, rank + 2 * states), jnp.float32)
    for j in range(blocks):
        history = [
            moved_ref[j, :, pl.ds((states + e) * BLOCK, BLOCK)].astype(jnp.float32) for e in range(3)
        ]
        conv = convolved(jnp.concatenate(history + [x_ref[j]], axis=0), vec_ref[j], late)
        cv_ref[j] = conv.astype(jnp.float32)
        mixed = mixed + mixed_of(conv, xw_ref[j])
    rounded = mixed.astype(jnp.bfloat16)
    for j in range(blocks):
        dt_ref[j] = softplus(
            jnp.dot(rounded[:, :rank], sw_ref[j], preferred_element_type=jnp.float32)
            + vec_ref[j, pl.ds(5, 1), :]
        )
    coefs = rounded[:, rank:].astype(jnp.float32)
    for t in range(draft):
        if t * reqs < late:
            rows = coefs[t * reqs : (t + 1) * reqs]
        else:
            rows = coef_ref[pl.ds(t * reqs - late, reqs), :]
        for n in range(states):
            at = t * states + n
            if t * reqs < late:
                b_ref[at] = jnp.broadcast_to(rows[:, n : n + 1], (reqs, LANES))
            c_ref[at] = jnp.broadcast_to(rows[:, states + n : states + n + 1], (reqs, LANES))
    accepted = acc_ref[...]
    for j in range(blocks):
        gated = []
        copies(j)[0].wait()
        for k in range(per):
            tile = j * per + k
            lanes = pl.ds(k * LANES, LANES)
            skip = vec_ref[j, pl.ds(6, 1), lanes]
            state = [
                moved_ref[j, :, pl.ds(n * BLOCK + k * LANES, LANES)].astype(jnp.float32)
                for n in range(states)
            ]
            decay = [
                jnp.broadcast_to(vec_ref[j, pl.ds(8 + n, 1), lanes], (reqs, LANES))
                for n in range(states)
            ]
            outs = []
            for t in range(late // reqs):
                rows = pl.ds(t * reqs, reqs)
                delta = dt_ref[j, rows, lanes]
                value = cv_ref[j, rows, lanes]
                driven = delta * value
                chosen = accepted == t + 1
                totals = [skip * value, None]
                for n in range(states):
                    at = t * states + n
                    state[n] = jnp.exp2(delta * decay[n]) * state[n] + driven * b_ref[at]
                    term = c_ref[at] * state[n]
                    totals[n % 2] = term if totals[n % 2] is None else totals[n % 2] + term
                    pltpu.store(pick_ref.at[tile, pl.ds(n * reqs, reqs), :], state[n], mask=chosen)
                outs.append(totals[0] + totals[1])
            beyond = accepted > late // reqs
            passed = at_ref[tile]
            for n in range(states):
                keep = pl.ds(n * reqs, reqs)
                ahead = rows_ref[tile, pl.ds(state_at + n * reqs, reqs), :]
                value = jnp.exp2(passed * decay[n]) * state[n] + ahead
                pltpu.store(pick_ref.at[tile, keep, :], value, mask=beyond)
            for t in range(late // reqs, draft):
                row = t * reqs - late
                passed = rows_ref[tile, pl.ds(sum_at + row, reqs), :]
                totals = [rows_ref[tile, pl.ds(y_at + row, reqs), :], None]
                for n in range(states):
                    term = c_ref[t * states + n] * (jnp.exp2(passed * decay[n]) * state[n])
                    totals[n % 2] = term if totals[n % 2] is None else totals[n % 2] + term
                outs.append(totals[0] + totals[1])
            for r in range(reqs):
                new_ref[j, pl.ds(r * states, states), lanes] = pick_ref[
                    tile, pl.ds(r, states, stride=reqs), :
                ]
            gated.append(jnp.concatenate(outs, axis=0) * rows_ref[tile, pl.ds(gate_at, tokens), :])
        copies(j)[2].start()
        copies(j)[1].wait()
        added = jnp.dot(
            jnp.concatenate(gated, axis=1).astype(jnp.bfloat16),
            ow_ref[pl.ds(j * BLOCK, BLOCK), :],
            preferred_element_type=jnp.float32,
        )
        for k in range(total_ref.shape[0]):
            part = added[:, k * LANES : (k + 1) * LANES]
            total_ref[k] = part if j == 0 else total_ref[k] + part
    for k in range(total_ref.shape[0]):
        for r in range(reqs):
            rows = total_ref[k, pl.ds(r, draft, stride=reqs), :]
            out_ref[r, :, pl.ds(k * LANES, LANES)] = rows.astype(jnp.bfloat16)
    for j in range(blocks):
        copies(j)[2].wait()


def after(moved, accepted, early, out_weight):
    rows, at, coefs, xw, sw, vec, x = early
    blocks, reqs, _ = moved.shape
    tiles = at.shape[0]
    states = coefs.shape[1] // 2
    late = x.shape[1]
    tokens = coefs.shape[0] + late
    draft = tokens // reqs
    inner, width = out_weight.shape
    vmem = pl.BlockSpec(memory_space=pltpu.VMEM)
    hbm = pl.BlockSpec(memory_space=pltpu.HBM)
    f32 = jnp.float32
    return pl.pallas_call(
        after_kernel,
        out_shape=(
            jax.ShapeDtypeStruct((reqs, draft, width), jnp.bfloat16),
            jax.ShapeDtypeStruct((reqs * states, inner), f32),
        ),
        in_specs=[vmem] * 8 + [hbm] * 2,
        out_specs=(vmem, hbm),
        scratch_shapes=[
            pltpu.VMEM(rows.shape, f32),
            pltpu.VMEM(out_weight.shape, jnp.bfloat16),
            pltpu.VMEM((blocks, reqs * states, BLOCK), f32),
            pltpu.VMEM((tiles, states * reqs, LANES), f32),
            pltpu.VMEM((width // LANES, tokens, LANES), f32),
            pltpu.VMEM((blocks, late, BLOCK), f32),
            pltpu.VMEM((blocks, late, BLOCK), f32),
            pltpu.VMEM((late // reqs * states, reqs, LANES), f32),
            pltpu.VMEM((draft * states, reqs, LANES), f32),
            pltpu.SemaphoreType.DMA((3, blocks)),
        ],
        compiler_params=pltpu.CompilerParams(vmem_limit_bytes=24 << 20),
        cost_estimate=pl.CostEstimate(
            flops=2 * tokens * inner * width, bytes_accessed=12 << 20, transcendentals=4_000_000
        ),
        name="after_states",
    )(moved, accepted, at, coefs, xw, sw, vec, x, in_hbm(rows), in_hbm(out_weight))


def exchange(values):
    return lax.all_to_all(values, "req", split_axis=0, concat_axis=0, tiled=True)


def select_kernel(mask_ref, arrived_ref, out_ref):
    width = arrived_ref.shape[1] // 19
    at = 16 * width
    spans = [(0, 0, at)] + [(e + 1, at + e * width, width) for e in range(3)]
    for which, start, size in spans:
        cols = pl.ds(start, size)
        out_ref[:, cols] = jnp.dot(
            mask_ref[which], arrived_ref[:, cols], preferred_element_type=jnp.float32
        ).astype(jnp.bfloat16)


def select(masks, arrived):
    if arrived.shape[1] % (19 * LANES) == 0:
        return pl.pallas_call(
            select_kernel,
            out_shape=jax.ShapeDtypeStruct(arrived.shape, jnp.bfloat16),
            in_specs=[pl.BlockSpec(memory_space=pltpu.VMEM)] * 2,
            out_specs=pl.BlockSpec(memory_space=pltpu.VMEM),
            compiler_params=pltpu.CompilerParams(vmem_limit_bytes=16 << 20),
            name="select_slots",
        )(masks, arrived)
    width = arrived.shape[1] // 19
    cut = [0] + [(16 + e) * width for e in range(4)]
    return jnp.concatenate(
        [
            jnp.dot(
                masks[i], arrived[:, cut[i] : cut[i + 1]], preferred_element_type=jnp.float32
            ).astype(jnp.bfloat16)
            for i in range(4)
        ],
        axis=1,
    )


def on_device(
    groups,
    hidden,
    norm_gain,
    in_weight,
    conv_weight,
    conv_bias,
    x_weight,
    step_weight,
    step_bias,
    log_decay,
    skip_gain,
    out_weight,
    old_states,
    old_edges,
    anchor,
    fresh_flag,
    accepted,
    request_ages,
):
    local_reqs, draft_len, width = hidden.shape
    inner_width = out_weight.shape[0]
    channels = conv_weight.shape[1]
    state_size = log_decay.shape[0]
    span = old_edges.shape[1]
    all_reqs = anchor.shape[0]
    blocks = inner_width // channels
    tokens = draft_len * local_reqs

    packed, share = prepared(
        old_states, old_edges, x_weight, step_weight, conv_weight, conv_bias, step_bias, skip_gain, log_decay
    )
    arrived = exchange(packed.reshape(all_reqs, (state_size + span) * channels))
    old_slot = jnp.arange(all_reqs, dtype=jnp.int32)
    chosen = (anchor[:, None] == old_slot[None, :]) & (fresh_flag[:, None] == 0)
    masks = jnp.stack([chosen] + [chosen & (span - e <= request_ages)[:, None] for e in range(span)])
    token_major = jnp.swapaxes(hidden, 0, 1).reshape(tokens, width)
    normed = rms_normed(token_major, norm_gain)
    projected = jnp.dot(normed, in_weight, preferred_element_type=jnp.float32).astype(jnp.bfloat16)
    masks, projected = lax.optimization_barrier((masks.astype(jnp.bfloat16), projected))
    moved = exchange(select(masks, arrived))

    top = blocks // 2
    weights = jnp.concatenate(
        [share[None]] + [moved_by(share[None], "req", bits) for bits in (top, top // 2, top + top // 2)]
    )
    weights = doubled(doubled(weights, "req", top // 4)[None], "grp", groups // 2)
    q_place, j_place = places("grp"), places("req")
    if channels != BLOCK:
        moved = moved.reshape(blocks, local_reqs, state_size + span, channels).transpose(1, 2, 0, 3)
        moved = moved.reshape(local_reqs, state_size + span, -1, BLOCK).transpose(2, 0, 1, 3)
        weights = jnp.take(weights, j_place, axis=1).swapaxes(1, 2)
        weights = weights.reshape(groups, SHARE, -1, BLOCK).swapaxes(1, 2)
        j_place = jnp.arange(inner_width // BLOCK, dtype=jnp.int32)
    moved = moved.reshape(inner_width // BLOCK, local_reqs, (state_size + span) * BLOCK)

    mine = lax.dynamic_slice_in_dim(accepted, lax.axis_index("req") * local_reqs, local_reqs, 0)
    mine = jnp.broadcast_to(mine[:, None], (local_reqs, LANES))
    early = before(q_place, j_place, projected, weights, mine, span * local_reqs, state_size)
    layer_out, new_states = after(moved, mine, early, out_weight)
    return layer_out, new_states.reshape(local_reqs, state_size, inner_width)


def solution(mesh):
    return jax.shard_map(
        functools.partial(on_device, mesh.shape["grp"]),
        mesh=mesh,
        in_specs=(
            P(("grp", "req"), None, None),
            P(),
            P(),
            P(None, "req"),
            P("req"),
            P("req", None),
            P(None, "req"),
            P("req"),
            P(None, "req"),
            P("req"),
            P(),
            P(("grp", "req"), None, None),
            P(("grp", "req"), None, None),
            P("grp"),
            P("grp"),
            P("grp"),
            P("grp"),
        ),
        out_specs=(P(("grp", "req"), None, None), P(("grp", "req"), None, None)),
        check_vma=False,
    )
```

```python
import functools

import jax
import jax.numpy as jnp
from jax import lax
from jax.experimental import pallas as pl
from jax.experimental.pallas import tpu as pltpu
from jax.sharding import PartitionSpec as P

EPS = 1e-05
LOG2E = 1.4426950408889634
LANES = 128
BLOCK = 256
SHARE = 88
AHEAD = 6


def rms_normed(values_in, norm_gain):
    values = values_in.astype(jnp.float32)
    factor = lax.rsqrt(jnp.mean(values * values, axis=-1, keepdims=True) + EPS)
    return (values * factor * norm_gain).astype(jnp.bfloat16)


def in_hbm(values):
    return pltpu.with_memory_space_constraint(values, pltpu.HBM)


def send_kernel(
    group_ref, state_ref, edge_ref, xt_ref, sw_ref, cw_ref, cb_ref, sb_ref, sk_ref, ld_ref,
    out_ref, share_ref,
    tile_ref, held_ref, send_ref, xt_in, sw_in, vec_ref, sems, few,
):
    blocks, slots, _ = out_ref.shape
    width = state_ref.shape[1] // blocks
    states = state_ref.shape[0] // slots
    per = width // LANES
    rank = sw_ref.shape[0]

    def load(tile):
        cols = pl.ds(tile * LANES, LANES)
        return pltpu.make_async_copy(state_ref.at[:, cols], tile_ref.at[tile], sems.at[0, tile])

    def store(dest):
        return pltpu.make_async_copy(send_ref.at[dest], out_ref.at[dest], sems.at[1, dest])

    small = [
        (edge_ref, held_ref),
        (xt_ref, xt_in),
        (sw_ref, sw_in),
        (cw_ref, vec_ref.at[pl.ds(0, 4), :]),
        (cb_ref, vec_ref.at[pl.ds(4, 1), :]),
        (sb_ref, vec_ref.at[pl.ds(5, 1), :]),
        (sk_ref, vec_ref.at[pl.ds(6, 1), :]),
        (ld_ref, vec_ref.at[pl.ds(8, 16), :]),
    ]
    copies = [pltpu.make_async_copy(x, y, few.at[i]) for i, (x, y) in enumerate(small)]
    vec_ref[pl.ds(7, 1), :] = jnp.zeros((1, width), jnp.float32)
    vec_ref[pl.ds(24, 8), :] = jnp.zeros((8, width), jnp.float32)
    for copy in copies:
        copy.start()
    for tile in range(blocks * per):
        load(tile).start()
    for copy in copies:
        copy.wait()
    for k in range(4):

        @pl.when(group_ref[0] == k)
        def _():
            vec = vec_ref[pl.ds(16 * (k % 2), 16), :]
            high = vec.astype(jnp.bfloat16).astype(jnp.float32)
            part = high if k < 2 else vec - high
            rows = [
                xt_in[pl.ds(32 * k, 32), :].astype(jnp.float32),
                xt_in[pl.ds(rank + 8 * k, 8), :].astype(jnp.float32),
                part[:8],
                sw_in[pl.ds(32 * k, 32), :].astype(jnp.float32),
                part[8:],
            ]
            share_ref[...] = jnp.concatenate(rows, axis=0).astype(jnp.bfloat16)

    for dest in range(blocks):
        for e in range(edge_ref.shape[0]):
            at = (states + e) * width
            send_ref[dest, :, pl.ds(at, width)] = held_ref[e, :, pl.ds(dest * width, width)]
        for part in range(per):
            tile = dest * per + part
            load(tile).wait()
            for n in range(states):
                rows = tile_ref[tile, pl.ds(n, slots, stride=states), :]
                send_ref[dest, :, pl.ds(n * width + part * LANES, LANES)] = rows.astype(jnp.bfloat16)
        store(dest).start()
    for dest in range(blocks):
        store(dest).wait()


def prepared(
    old_states, old_edges, x_weight, step_weight, conv_weight, conv_bias, step_bias, skip_gain, log_decay
):
    slots, states, inner = old_states.shape
    span = old_edges.shape[1]
    width = x_weight.shape[0]
    blocks = inner // width
    rank = step_weight.shape[0]
    edges = jnp.swapaxes(old_edges, 0, 1)
    xt = x_weight.T
    group = lax.axis_index("grp").astype(jnp.int32)
    if width % LANES == 0 and slots == 8:
        tiles = inner // LANES
        vmem = pl.BlockSpec(memory_space=pltpu.VMEM)
        hbm = pl.BlockSpec(memory_space=pltpu.HBM)
        given = (
            old_states.reshape(slots * states, inner), edges, xt, step_weight, conv_weight,
            conv_bias[None], step_bias[None], skip_gain[None], log_decay,
        )
        return pl.pallas_call(
            send_kernel,
            out_shape=(
                pltpu.HBM((blocks, slots, (states + span) * width), jnp.bfloat16),
                jax.ShapeDtypeStruct((SHARE, width), jnp.bfloat16),
            ),
            in_specs=[pl.BlockSpec(memory_space=pltpu.SMEM)] + [hbm] * len(given),
            out_specs=(hbm, vmem),
            scratch_shapes=[
                pltpu.VMEM((tiles, slots * states, LANES), jnp.float32),
                pltpu.VMEM((span, slots, inner), jnp.bfloat16),
                pltpu.VMEM((blocks, slots, (states + span) * width), jnp.bfloat16),
                pltpu.VMEM(xt.shape, jnp.bfloat16),
                pltpu.VMEM(step_weight.shape, jnp.bfloat16),
                pltpu.VMEM((32, width), jnp.float32),
                pltpu.SemaphoreType.DMA((2, tiles)),
                pltpu.SemaphoreType.DMA((8,)),
            ],
            compiler_params=pltpu.CompilerParams(vmem_limit_bytes=16 << 20),
            name="send_states",
        )(group[None], *[in_hbm(x) for x in given])
    lead = jnp.swapaxes(old_states.astype(jnp.bfloat16), 0, 1)
    both = jnp.concatenate([lead, edges], axis=0)
    both = both.reshape(states + span, slots, blocks, width)
    packed = both.transpose(2, 1, 0, 3).reshape(blocks, slots, (states + span) * width)
    none = jnp.zeros_like(conv_bias)[None]
    vec = jnp.concatenate(
        [conv_weight, conv_bias[None], step_bias[None], skip_gain[None], none, log_decay], axis=0
    )
    vec = jnp.pad(vec, ((0, 8), (0, 0)))
    high = vec.astype(jnp.bfloat16)
    halves = jnp.concatenate([high, (vec - high.astype(jnp.float32)).astype(jnp.bfloat16)], axis=0)
    halves = halves.reshape(4, 16, width)
    stacked = jnp.concatenate(
        [
            xt[:rank].reshape(4, 32, width),
            xt[rank:].reshape(4, 8, width),
            halves[:, :8],
            step_weight.reshape(4, 32, width),
            halves[:, 8:],
        ],
        axis=1,
    )
    return packed, lax.dynamic_index_in_dim(stacked, group, 0, keepdims=False)


def moved_by(values, axis, bits):
    return lax.ppermute(values, axis, [(i, i ^ bits) for i in range(lax.axis_size(axis))])


def doubled(values, axis, bit, stop=0):
    while bit > stop:
        values = jnp.concatenate([values, moved_by(values, axis, bit)], axis=0)
        bit //= 2
    return values


def places(axis):
    size = lax.axis_size(axis)
    offset = jnp.arange(size, dtype=jnp.int32) ^ lax.axis_index(axis).astype(jnp.int32)
    place = jnp.zeros_like(offset)
    bit, top = 1, size // 2
    while top:
        place = place | jnp.where((offset & bit) != 0, top, 0)
        bit, top = bit * 2, top // 2
    return place


def block_weights(near_ref, far_ref, q_ref, j_ref, j):
    at = j_ref[j]
    f32 = jnp.float32

    def rows(q, start, size):
        place = q_ref[q]
        some = pl.ds(start, size)
        near = near_ref[place % 2, at, some, :].astype(f32)
        return jnp.where(place < 2, near, far_ref[place % 2, at, some, :].astype(f32))

    xw = jnp.concatenate(
        [rows(q, 0, 32) for q in range(4)] + [rows(q, 32, 8) for q in range(4)], axis=0
    ).astype(jnp.bfloat16)
    sw = jnp.concatenate([rows(q, 48, 32) for q in range(4)], axis=0).astype(jnp.bfloat16)
    first = [rows(q, 40, 8) for q in range(4)]
    second = [rows(q, 80, 8) for q in range(4)]
    high = jnp.concatenate([first[0], second[0], first[1]], axis=0)
    low = jnp.concatenate([first[2], second[2], first[3]], axis=0)
    return xw, sw, high + low


def silu(values):
    return values / (1.0 + jnp.exp(-values))


def convolved(sequence, vec, count):
    reqs = (sequence.shape[0] - count) // 3
    running = vec[4:5]
    for k in range(4):
        running = running + vec[k : k + 1] * sequence[k * reqs : k * reqs + count]
    return silu(running).astype(jnp.bfloat16)


def softplus(values):
    return jnp.maximum(values, 0.0) + jnp.log1p(jnp.exp(-jnp.abs(values)))


def mixed_of(conv, xw):
    return lax.dot_general(conv, xw, (((1,), (1,)), ((), ())), preferred_element_type=jnp.float32)


def spread(rows, t, b_ref, c_ref):
    reqs, both = rows.shape
    states = both // 2
    for n in range(states):
        b_ref[t * states + n] = jnp.broadcast_to(rows[:, n : n + 1], (reqs, LANES))
        c_ref[t * states + n] = jnp.broadcast_to(rows[:, states + n : states + n + 1], (reqs, LANES))


def before_kernel(
    q_ref, j_ref, proj_ref, near_ref, far_ref, acc_ref,
    rows_out, at_ref, coef_ref, xw_ref, sw_ref, vec_ref, x_ref,
    rows_ref, dt_ref, cv_ref, b_ref, c_ref, dec_ref, sems,
):
    blocks = near_ref.shape[1]
    tiles, count, _ = dt_ref.shape
    tokens = proj_ref.shape[0]
    late = tokens - count
    reqs = late // 3
    states = b_ref.shape[0] * reqs // count
    inner = blocks * BLOCK
    rank = sw_ref.shape[1]
    per = BLOCK // LANES
    y_at, sum_at, gate_at, state_at = row_offsets(count, tokens)

    def copy(j):
        some = pl.ds(j * per, per)
        return pltpu.make_async_copy(rows_ref.at[some], rows_out.at[some], sems.at[j])

    mixed = jnp.zeros((count, rank + 2 * states), jnp.float32)
    for j in range(blocks):
        xw, sw, vec = block_weights(near_ref, far_ref, q_ref, j_ref, j)
        values = proj_ref[:, pl.ds(j * BLOCK, BLOCK)].astype(jnp.float32)
        conv = convolved(values, vec, count)
        mixed = mixed + mixed_of(conv, xw)
        xw_ref[j] = xw
        sw_ref[j] = sw
        x_ref[j] = values[:late]
        vec_ref[j, pl.ds(0, 8), :] = vec[:8]
        decay2 = jnp.exp(vec[8:]) * (-LOG2E)
        vec_ref[j, pl.ds(8, states), :] = decay2
        full = conv.astype(jnp.float32)
        gate = silu(proj_ref[:, pl.ds(inner + j * BLOCK, BLOCK)].astype(jnp.float32))
        for k in range(per):
            tile = j * per + k
            lanes = slice(k * LANES, (k + 1) * LANES)
            cv_ref[tile] = full[:, lanes]
            rows_ref[tile, pl.ds(gate_at, tokens), :] = gate[:, lanes]
            rows_ref[tile, pl.ds(y_at, count), :] = vec[6:7, lanes] * full[:, lanes]
            for n in range(states):
                dec_ref[tile, n] = jnp.broadcast_to(decay2[n : n + 1, lanes], (reqs, LANES))
    rounded = mixed.astype(jnp.bfloat16)
    for j in range(blocks):
        dt = softplus(
            jnp.dot(rounded[:, :rank], sw_ref[j], preferred_element_type=jnp.float32)
            + vec_ref[j, pl.ds(5, 1), :]
        )
        for k in range(per):
            dt_ref[j * per + k] = dt[:, k * LANES : (k + 1) * LANES]
    coefs = rounded[:, rank:].astype(jnp.float32)
    coef_ref[...] = coefs
    for t in range(count // reqs):
        spread(coefs[t * reqs : (t + 1) * reqs], t, b_ref, c_ref)
    accepted = acc_ref[...]
    at_ref[...] = jnp.zeros_like(at_ref)

    @pl.loop(0, tiles)
    def _(tile):
        state = [None] * states
        passed = None
        rows_ref[tile, pl.ds(state_at, states * reqs), :] = jnp.zeros((states * reqs, LANES), jnp.float32)
        for t in range(count // reqs):
            delta = dt_ref[tile, pl.ds(t * reqs, reqs), :]
            passed = delta if t == 0 else passed + delta
            rows_ref[tile, pl.ds(sum_at + t * reqs, reqs), :] = passed
            driven = delta * cv_ref[tile, pl.ds(t * reqs, reqs), :]
            chosen = accepted == t + late // reqs + 1
            pltpu.store(at_ref.at[tile], passed, mask=chosen)
            totals = [rows_ref[tile, pl.ds(y_at + t * reqs, reqs), :], None]
            for n in range(states):
                at = t * states + n
                added = driven * b_ref[at]
                state[n] = added if t == 0 else jnp.exp2(delta * dec_ref[tile, n]) * state[n] + added
                term = c_ref[at] * state[n]
                totals[n % 2] = term if totals[n % 2] is None else totals[n % 2] + term
                pltpu.store(
                    rows_ref.at[tile, pl.ds(state_at + n * reqs, reqs), :], state[n], mask=chosen
                )
            rows_ref[tile, pl.ds(y_at + t * reqs, reqs), :] = totals[0] + totals[1]

        @pl.when(tile % per == per - 1)
        def _():
            copy(tile // per).start()

    for j in range(blocks):
        copy(j).wait()


def row_offsets(count, tokens):
    return 0, count, 2 * count, 2 * count + tokens


def before(q_place, j_place, projected, weights, accepted, late, states):
    tokens = projected.shape[0]
    blocks = weights[0].shape[1]
    tiles = blocks * (BLOCK // LANES)
    count = tokens - late
    reqs = accepted.shape[0]
    rank = 4 * 32
    smem = pl.BlockSpec(memory_space=pltpu.SMEM)
    vmem = pl.BlockSpec(memory_space=pltpu.VMEM)
    f32 = jnp.float32
    spots = count // reqs * states
    rows = (tiles, 2 * count + tokens + states * reqs, LANES)
    return pl.pallas_call(
        before_kernel,
        out_shape=(
            pltpu.HBM(rows, f32),
            jax.ShapeDtypeStruct((tiles, reqs, LANES), f32),
            jax.ShapeDtypeStruct((count, 2 * states), f32),
            jax.ShapeDtypeStruct((blocks, rank + 2 * states, BLOCK), jnp.bfloat16),
            jax.ShapeDtypeStruct((blocks, rank, BLOCK), jnp.bfloat16),
            jax.ShapeDtypeStruct((blocks, 24, BLOCK), f32),
            jax.ShapeDtypeStruct((blocks, late, BLOCK), f32),
        ),
        in_specs=[smem, smem, vmem, vmem, vmem, vmem],
        out_specs=(pl.BlockSpec(memory_space=pltpu.HBM),) + (vmem,) * 6,
        scratch_shapes=[
            pltpu.VMEM(rows, f32),
            pltpu.VMEM((tiles, count, LANES), f32),
            pltpu.VMEM((tiles, count, LANES), f32),
            pltpu.VMEM((spots, reqs, LANES), f32),
            pltpu.VMEM((spots, reqs, LANES), f32),
            pltpu.VMEM((tiles, states, reqs, LANES), f32),
            pltpu.SemaphoreType.DMA((blocks,)),
        ],
        compiler_params=pltpu.CompilerParams(vmem_limit_bytes=24 << 20),
        cost_estimate=pl.CostEstimate(flops=200_000_000, bytes_accessed=8 << 20, transcendentals=4_000_000),
        name="before_states",
    )(q_place, j_place, projected, *weights, accepted)


def after_kernel(
    moved_ref, acc_ref, at_ref, coef_ref, xw_ref, sw_ref, vec_ref, x_ref, rows_in, ow_in,
    out_ref, ns_ref,
    rows_ref, ow_ref, new_ref, pick_ref, total_ref, dt_ref, cv_ref, b_ref, c_ref, done_ref, sems, out_sem,
):
    reqs, draft, _ = out_ref.shape
    blocks, late, _ = x_ref.shape
    tiles = rows_ref.shape[0]
    tokens = reqs * draft
    count = tokens - late
    states = coef_ref.shape[1] // 2
    rank = sw_ref.shape[1]
    per = BLOCK // LANES
    y_at, sum_at, gate_at, state_at = row_offsets(count, tokens)

    def copies(j):
        some, cols = pl.ds(j * per, per), pl.ds(j * BLOCK, BLOCK)
        return [
            pltpu.make_async_copy(rows_in.at[some], rows_ref.at[some], sems.at[0, j]),
            pltpu.make_async_copy(ow_in.at[cols, :], ow_ref.at[cols, :], sems.at[1, j]),
            pltpu.make_async_copy(new_ref.at[j], ns_ref.at[:, cols], sems.at[2, j]),
        ]

    def result(k):
        cols = pl.ds(k * LANES, LANES)
        return pltpu.make_async_copy(done_ref.at[k], out_ref.at[:, :, cols], out_sem.at[k])

    queue = [copies(j)[i] for j in range(blocks) for i in range(2)]
    for copy in queue[:AHEAD]:
        copy.start()
    mixed = jnp.zeros((late, rank + 2 * states), jnp.float32)
    for j in range(blocks):
        history = [
            moved_ref[j, :, pl.ds((states + e) * BLOCK, BLOCK)].astype(jnp.float32) for e in range(3)
        ]
        conv = convolved(jnp.concatenate(history + [x_ref[j]], axis=0), vec_ref[j], late)
        cv_ref[j] = conv.astype(jnp.float32)
        mixed = mixed + mixed_of(conv, xw_ref[j])
    rounded = mixed.astype(jnp.bfloat16)
    for j in range(blocks):
        dt_ref[j] = softplus(
            jnp.dot(rounded[:, :rank], sw_ref[j], preferred_element_type=jnp.float32)
            + vec_ref[j, pl.ds(5, 1), :]
        )
    coefs = rounded[:, rank:].astype(jnp.float32)
    for t in range(draft):
        if t * reqs < late:
            rows = coefs[t * reqs : (t + 1) * reqs]
        else:
            rows = coef_ref[pl.ds(t * reqs - late, reqs), :]
        for n in range(states):
            at = t * states + n
            if t * reqs < late:
                b_ref[at] = jnp.broadcast_to(rows[:, n : n + 1], (reqs, LANES))
            c_ref[at] = jnp.broadcast_to(rows[:, states + n : states + n + 1], (reqs, LANES))
    accepted = acc_ref[...]
    def project(j, gated):
        added = jnp.dot(
            gated, ow_ref[pl.ds(j * BLOCK, BLOCK), :], preferred_element_type=jnp.float32
        )
        for k in range(total_ref.shape[0]):
            part = added[:, k * LANES : (k + 1) * LANES]
            total_ref[k] = part if j == 0 else total_ref[k] + part

    ready = None
    for j in range(blocks):
        for at in (2 * j - 1, 2 * j):
            if at >= 0:
                queue[at].wait()
                if at + AHEAD < len(queue):
                    queue[at + AHEAD].start()
        if ready is not None:
            project(j - 1, ready)
        gated = []
        for k in range(per):
            tile = j * per + k
            lanes = pl.ds(k * LANES, LANES)
            skip = vec_ref[j, pl.ds(6, 1), lanes]
            state = [
                moved_ref[j, :, pl.ds(n * BLOCK + k * LANES, LANES)].astype(jnp.float32)
                for n in range(states)
            ]
            decay = [
                jnp.broadcast_to(vec_ref[j, pl.ds(8 + n, 1), lanes], (reqs, LANES))
                for n in range(states)
            ]
            outs = []
            for t in range(late // reqs):
                rows = pl.ds(t * reqs, reqs)
                delta = dt_ref[j, rows, lanes]
                value = cv_ref[j, rows, lanes]
                driven = delta * value
                chosen = accepted == t + 1
                totals = [skip * value, None]
                for n in range(states):
                    at = t * states + n
                    state[n] = jnp.exp2(delta * decay[n]) * state[n] + driven * b_ref[at]
                    term = c_ref[at] * state[n]
                    totals[n % 2] = term if totals[n % 2] is None else totals[n % 2] + term
                    pltpu.store(pick_ref.at[tile, pl.ds(n * reqs, reqs), :], state[n], mask=chosen)
                outs.append(totals[0] + totals[1])
            beyond = accepted > late // reqs
            passed = at_ref[tile]
            for n in range(states):
                keep = pl.ds(n * reqs, reqs)
                ahead = rows_ref[tile, pl.ds(state_at + n * reqs, reqs), :]
                value = jnp.exp2(passed * decay[n]) * state[n] + ahead
                pltpu.store(pick_ref.at[tile, keep, :], value, mask=beyond)
            for t in range(late // reqs, draft):
                row = t * reqs - late
                passed = rows_ref[tile, pl.ds(sum_at + row, reqs), :]
                totals = [rows_ref[tile, pl.ds(y_at + row, reqs), :], None]
                for n in range(states):
                    term = c_ref[t * states + n] * (jnp.exp2(passed * decay[n]) * state[n])
                    totals[n % 2] = term if totals[n % 2] is None else totals[n % 2] + term
                outs.append(totals[0] + totals[1])
            for r in range(reqs):
                new_ref[j, pl.ds(r * states, states), lanes] = pick_ref[
                    tile, pl.ds(r, states, stride=reqs), :
                ]
            gated.append(jnp.concatenate(outs, axis=0) * rows_ref[tile, pl.ds(gate_at, tokens), :])
        copies(j)[2].start()
        ready = jnp.concatenate(gated, axis=1).astype(jnp.bfloat16)
    queue[-1].wait()
    project(blocks - 1, ready)
    for k in range(total_ref.shape[0]):
        for r in range(reqs):
            rows = total_ref[k, pl.ds(r, draft, stride=reqs), :]
            done_ref[k, r] = rows.astype(jnp.bfloat16)
        result(k).start()
    for j in range(blocks):
        copies(j)[2].wait()
    for k in range(total_ref.shape[0]):
        result(k).wait()


def after(moved, accepted, early, out_weight):
    rows, at, coefs, xw, sw, vec, x = early
    blocks, reqs, _ = moved.shape
    tiles = at.shape[0]
    states = coefs.shape[1] // 2
    late = x.shape[1]
    tokens = coefs.shape[0] + late
    draft = tokens // reqs
    inner, width = out_weight.shape
    vmem = pl.BlockSpec(memory_space=pltpu.VMEM)
    hbm = pl.BlockSpec(memory_space=pltpu.HBM)
    f32 = jnp.float32
    return pl.pallas_call(
        after_kernel,
        out_shape=(
            jax.ShapeDtypeStruct((reqs, draft, width), jnp.bfloat16),
            jax.ShapeDtypeStruct((reqs * states, inner), f32),
        ),
        in_specs=[vmem] * 8 + [hbm] * 2,
        out_specs=(hbm, hbm),
        scratch_shapes=[
            pltpu.VMEM(rows.shape, f32),
            pltpu.VMEM(out_weight.shape, jnp.bfloat16),
            pltpu.VMEM((blocks, reqs * states, BLOCK), f32),
            pltpu.VMEM((tiles, states * reqs, LANES), f32),
            pltpu.VMEM((width // LANES, tokens, LANES), f32),
            pltpu.VMEM((blocks, late, BLOCK), f32),
            pltpu.VMEM((blocks, late, BLOCK), f32),
            pltpu.VMEM((late // reqs * states, reqs, LANES), f32),
            pltpu.VMEM((draft * states, reqs, LANES), f32),
            pltpu.VMEM((width // LANES, reqs, draft, LANES), jnp.bfloat16),
            pltpu.SemaphoreType.DMA((3, blocks)),
            pltpu.SemaphoreType.DMA((width // LANES,)),
        ],
        compiler_params=pltpu.CompilerParams(vmem_limit_bytes=24 << 20),
        cost_estimate=pl.CostEstimate(
            flops=2 * tokens * inner * width, bytes_accessed=12 << 20, transcendentals=4_000_000
        ),
        name="after_states",
    )(moved, accepted, at, coefs, xw, sw, vec, x, in_hbm(rows), in_hbm(out_weight))


def exchange(values):
    return lax.all_to_all(values, "req", split_axis=0, concat_axis=0, tiled=True)


def select_kernel(mask_ref, arrived_ref, out_ref):
    width = arrived_ref.shape[1] // 19
    at = 16 * width
    spans = [(0, 0, at)] + [(e + 1, at + e * width, width) for e in range(3)]
    for which, start, size in spans:
        cols = pl.ds(start, size)
        out_ref[:, cols] = jnp.dot(
            mask_ref[which], arrived_ref[:, cols], preferred_element_type=jnp.float32
        ).astype(jnp.bfloat16)


def select(masks, arrived):
    if arrived.shape[1] % (19 * LANES) == 0:
        return pl.pallas_call(
            select_kernel,
            out_shape=jax.ShapeDtypeStruct(arrived.shape, jnp.bfloat16),
            in_specs=[pl.BlockSpec(memory_space=pltpu.VMEM)] * 2,
            out_specs=pl.BlockSpec(memory_space=pltpu.VMEM),
            compiler_params=pltpu.CompilerParams(vmem_limit_bytes=16 << 20),
            name="select_slots",
        )(masks, arrived)
    width = arrived.shape[1] // 19
    cut = [0] + [(16 + e) * width for e in range(4)]
    return jnp.concatenate(
        [
            jnp.dot(
                masks[i], arrived[:, cut[i] : cut[i + 1]], preferred_element_type=jnp.float32
            ).astype(jnp.bfloat16)
            for i in range(4)
        ],
        axis=1,
    )


def on_device(
    groups,
    hidden,
    norm_gain,
    in_weight,
    conv_weight,
    conv_bias,
    x_weight,
    step_weight,
    step_bias,
    log_decay,
    skip_gain,
    out_weight,
    old_states,
    old_edges,
    anchor,
    fresh_flag,
    accepted,
    request_ages,
):
    local_reqs, draft_len, width = hidden.shape
    inner_width = out_weight.shape[0]
    channels = conv_weight.shape[1]
    state_size = log_decay.shape[0]
    span = old_edges.shape[1]
    all_reqs = anchor.shape[0]
    blocks = inner_width // channels
    tokens = draft_len * local_reqs

    packed, share = prepared(
        old_states, old_edges, x_weight, step_weight, conv_weight, conv_bias, step_bias, skip_gain, log_decay
    )
    arrived = exchange(packed.reshape(all_reqs, (state_size + span) * channels))
    old_slot = jnp.arange(all_reqs, dtype=jnp.int32)
    chosen = (anchor[:, None] == old_slot[None, :]) & (fresh_flag[:, None] == 0)
    masks = jnp.stack([chosen] + [chosen & (span - e <= request_ages)[:, None] for e in range(span)])
    token_major = jnp.swapaxes(hidden, 0, 1).reshape(tokens, width)
    normed = rms_normed(token_major, norm_gain)
    projected = jnp.dot(normed, in_weight, preferred_element_type=jnp.float32).astype(jnp.bfloat16)
    masks, projected = lax.optimization_barrier((masks.astype(jnp.bfloat16), projected))
    moved = exchange(select(masks, arrived))

    near = doubled(doubled(share[None], "req", blocks // 2)[None], "grp", groups // 2, 1)
    weights = (near, moved_by(near, "grp", 1))
    q_place, j_place = places("grp"), places("req")
    if channels != BLOCK:
        moved = moved.reshape(blocks, local_reqs, state_size + span, channels).transpose(1, 2, 0, 3)
        moved = moved.reshape(local_reqs, state_size + span, -1, BLOCK).transpose(2, 0, 1, 3)
        weights = tuple(
            jnp.take(w, j_place, axis=1).swapaxes(1, 2).reshape(-1, SHARE, inner_width // BLOCK, BLOCK).swapaxes(1, 2)
            for w in weights
        )
        j_place = jnp.arange(inner_width // BLOCK, dtype=jnp.int32)
    moved = moved.reshape(inner_width // BLOCK, local_reqs, (state_size + span) * BLOCK)

    mine = lax.dynamic_slice_in_dim(accepted, lax.axis_index("req") * local_reqs, local_reqs, 0)
    mine = jnp.broadcast_to(mine[:, None], (local_reqs, LANES))
    early = before(q_place, j_place, projected, weights, mine, span * local_reqs, state_size)
    layer_out, new_states = after(moved, mine, early, out_weight)
    return layer_out, new_states.reshape(local_reqs, state_size, inner_width)


def solution(mesh):
    return jax.shard_map(
        functools.partial(on_device, mesh.shape["grp"]),
        mesh=mesh,
        in_specs=(
            P(("grp", "req"), None, None),
            P(),
            P(),
            P(None, "req"),
            P("req"),
            P("req", None),
            P(None, "req"),
            P("req"),
            P(None, "req"),
            P("req"),
            P(),
            P(("grp", "req"), None, None),
            P(("grp", "req"), None, None),
            P("grp"),
            P("grp"),
            P("grp"),
            P("grp"),
        ),
        out_specs=(P(("grp", "req"), None, None), P(("grp", "req"), None, None)),
        check_vma=False,
    )
```

```python
import functools

import jax
import jax.numpy as jnp
from jax import lax
from jax.experimental import pallas as pl
from jax.experimental.pallas import tpu as pltpu
from jax.sharding import PartitionSpec as P

EPS = 1e-05
LOG2E = 1.4426950408889634
LANES = 128
BLOCK = 256
SHARE = 88
AHEAD = 6


def rms_normed(values_in, norm_gain):
    values = values_in.astype(jnp.float32)
    factor = lax.rsqrt(jnp.mean(values * values, axis=-1, keepdims=True) + EPS)
    return (values * factor * norm_gain).astype(jnp.bfloat16)


def in_hbm(values):
    return pltpu.with_memory_space_constraint(values, pltpu.HBM)


def send_kernel(
    group_ref, state_ref, edge_ref, xt_ref, sw_ref, cw_ref, cb_ref, sb_ref, sk_ref, ld_ref,
    out_ref, share_ref,
    tile_ref, held_ref, send_ref, xt_in, sw_in, vec_ref, sems, few,
):
    blocks, slots, _ = out_ref.shape
    width = state_ref.shape[1] // blocks
    states = state_ref.shape[0] // slots
    per = width // LANES
    rank = sw_ref.shape[0]

    def load(tile):
        cols = pl.ds(tile * LANES, LANES)
        return pltpu.make_async_copy(state_ref.at[:, cols], tile_ref.at[tile], sems.at[0, tile])

    def store(dest):
        return pltpu.make_async_copy(send_ref.at[dest], out_ref.at[dest], sems.at[1, dest])

    small = [
        (edge_ref, held_ref),
        (xt_ref, xt_in),
        (sw_ref, sw_in),
        (cw_ref, vec_ref.at[pl.ds(0, 4), :]),
        (cb_ref, vec_ref.at[pl.ds(4, 1), :]),
        (sb_ref, vec_ref.at[pl.ds(5, 1), :]),
        (sk_ref, vec_ref.at[pl.ds(6, 1), :]),
        (ld_ref, vec_ref.at[pl.ds(8, 16), :]),
    ]
    copies = [pltpu.make_async_copy(x, y, few.at[i]) for i, (x, y) in enumerate(small)]
    vec_ref[pl.ds(7, 1), :] = jnp.zeros((1, width), jnp.float32)
    vec_ref[pl.ds(24, 8), :] = jnp.zeros((8, width), jnp.float32)
    copies[0].start()
    for tile in range(blocks * per):
        load(tile).start()
    for copy in copies[1:]:
        copy.start()
    copies[0].wait()
    for dest in range(blocks):
        for e in range(edge_ref.shape[0]):
            at = (states + e) * width
            send_ref[dest, :, pl.ds(at, width)] = held_ref[e, :, pl.ds(dest * width, width)]
        for part in range(per):
            tile = dest * per + part
            load(tile).wait()
            for n in range(states):
                rows = tile_ref[tile, pl.ds(n, slots, stride=states), :]
                send_ref[dest, :, pl.ds(n * width + part * LANES, LANES)] = rows.astype(jnp.bfloat16)
        store(dest).start()
    for copy in copies[1:]:
        copy.wait()
    for k in range(4):

        @pl.when(group_ref[0] == k)
        def _():
            vec = vec_ref[pl.ds(16 * (k % 2), 16), :]
            high = vec.astype(jnp.bfloat16).astype(jnp.float32)
            part = high if k < 2 else vec - high
            rows = [
                xt_in[pl.ds(32 * k, 32), :].astype(jnp.float32),
                xt_in[pl.ds(rank + 8 * k, 8), :].astype(jnp.float32),
                part[:8],
                sw_in[pl.ds(32 * k, 32), :].astype(jnp.float32),
                part[8:],
            ]
            share_ref[...] = jnp.concatenate(rows, axis=0).astype(jnp.bfloat16)

    for dest in range(blocks):
        store(dest).wait()


def prepared(
    old_states, old_edges, x_weight, step_weight, conv_weight, conv_bias, step_bias, skip_gain, log_decay
):
    slots, states, inner = old_states.shape
    span = old_edges.shape[1]
    width = x_weight.shape[0]
    blocks = inner // width
    rank = step_weight.shape[0]
    edges = jnp.swapaxes(old_edges, 0, 1)
    xt = x_weight.T
    group = lax.axis_index("grp").astype(jnp.int32)
    if width % LANES == 0 and slots == 8:
        tiles = inner // LANES
        vmem = pl.BlockSpec(memory_space=pltpu.VMEM)
        hbm = pl.BlockSpec(memory_space=pltpu.HBM)
        given = (
            old_states.reshape(slots * states, inner), edges, xt, step_weight, conv_weight,
            conv_bias[None], step_bias[None], skip_gain[None], log_decay,
        )
        return pl.pallas_call(
            send_kernel,
            out_shape=(
                pltpu.HBM((blocks, slots, (states + span) * width), jnp.bfloat16),
                jax.ShapeDtypeStruct((SHARE, width), jnp.bfloat16),
            ),
            in_specs=[pl.BlockSpec(memory_space=pltpu.SMEM)] + [hbm] * len(given),
            out_specs=(hbm, vmem),
            scratch_shapes=[
                pltpu.VMEM((tiles, slots * states, LANES), jnp.float32),
                pltpu.VMEM((span, slots, inner), jnp.bfloat16),
                pltpu.VMEM((blocks, slots, (states + span) * width), jnp.bfloat16),
                pltpu.VMEM(xt.shape, jnp.bfloat16),
                pltpu.VMEM(step_weight.shape, jnp.bfloat16),
                pltpu.VMEM((32, width), jnp.float32),
                pltpu.SemaphoreType.DMA((2, tiles)),
                pltpu.SemaphoreType.DMA((8,)),
            ],
            compiler_params=pltpu.CompilerParams(vmem_limit_bytes=16 << 20),
            name="send_states",
        )(group[None], *[in_hbm(x) for x in given])
    lead = jnp.swapaxes(old_states.astype(jnp.bfloat16), 0, 1)
    both = jnp.concatenate([lead, edges], axis=0)
    both = both.reshape(states + span, slots, blocks, width)
    packed = both.transpose(2, 1, 0, 3).reshape(blocks, slots, (states + span) * width)
    none = jnp.zeros_like(conv_bias)[None]
    vec = jnp.concatenate(
        [conv_weight, conv_bias[None], step_bias[None], skip_gain[None], none, log_decay], axis=0
    )
    vec = jnp.pad(vec, ((0, 8), (0, 0)))
    high = vec.astype(jnp.bfloat16)
    halves = jnp.concatenate([high, (vec - high.astype(jnp.float32)).astype(jnp.bfloat16)], axis=0)
    halves = halves.reshape(4, 16, width)
    stacked = jnp.concatenate(
        [
            xt[:rank].reshape(4, 32, width),
            xt[rank:].reshape(4, 8, width),
            halves[:, :8],
            step_weight.reshape(4, 32, width),
            halves[:, 8:],
        ],
        axis=1,
    )
    return packed, lax.dynamic_index_in_dim(stacked, group, 0, keepdims=False)


def moved_by(values, axis, bits):
    return lax.ppermute(values, axis, [(i, i ^ bits) for i in range(lax.axis_size(axis))])


def doubled(values, axis, bit):
    while bit:
        values = jnp.concatenate([values, moved_by(values, axis, bit)], axis=0)
        bit //= 2
    return values


def places(axis):
    size = lax.axis_size(axis)
    offset = jnp.arange(size, dtype=jnp.int32) ^ lax.axis_index(axis).astype(jnp.int32)
    place = jnp.zeros_like(offset)
    bit, top = 1, size // 2
    while top:
        place = place | jnp.where((offset & bit) != 0, top, 0)
        bit, top = bit * 2, top // 2
    return place


def block_weights(w_ref, q_ref, j_ref, j):
    at = j_ref[j]
    quarters = [w_ref.at[q_ref[q], at] for q in range(4)]
    f32 = jnp.float32
    xw = jnp.concatenate(
        [w[pl.ds(0, 32), :].astype(f32) for w in quarters] + [w[pl.ds(32, 8), :].astype(f32) for w in quarters],
        axis=0,
    ).astype(jnp.bfloat16)
    sw = jnp.concatenate([w[pl.ds(48, 32), :] for w in quarters], axis=0)
    first = [w[pl.ds(40, 8), :].astype(f32) for w in quarters]
    second = [w[pl.ds(80, 8), :].astype(f32) for w in quarters]
    high = jnp.concatenate([first[0], second[0], first[1]], axis=0)
    low = jnp.concatenate([first[2], second[2], first[3]], axis=0)
    return xw, sw, high + low


def silu(values):
    return values / (1.0 + jnp.exp(-values))


def convolved(sequence, vec, count):
    reqs = (sequence.shape[0] - count) // 3
    running = vec[4:5]
    for k in range(4):
        running = running + vec[k : k + 1] * sequence[k * reqs : k * reqs + count]
    return silu(running).astype(jnp.bfloat16)


def softplus(values):
    return jnp.maximum(values, 0.0) + jnp.log1p(jnp.exp(-jnp.abs(values)))


def mixed_of(conv, xw):
    return lax.dot_general(conv, xw, (((1,), (1,)), ((), ())), preferred_element_type=jnp.float32)


def spread(rows, t, b_ref, c_ref):
    reqs, both = rows.shape
    states = both // 2
    for n in range(states):
        b_ref[t * states + n] = jnp.broadcast_to(rows[:, n : n + 1], (reqs, LANES))
        c_ref[t * states + n] = jnp.broadcast_to(rows[:, states + n : states + n + 1], (reqs, LANES))


def before_kernel(
    q_ref, j_ref, proj_ref, w_ref, acc_ref,
    rows_out, at_ref, coef_ref, xw_ref, sw_ref, vec_ref, x_ref,
    rows_ref, dt_ref, cv_ref, b_ref, c_ref, dec_ref, sems,
):
    blocks = w_ref.shape[1]
    tiles, count, _ = dt_ref.shape
    tokens = proj_ref.shape[0]
    late = tokens - count
    reqs = late // 3
    states = b_ref.shape[0] * reqs // count
    inner = blocks * BLOCK
    rank = sw_ref.shape[1]
    per = BLOCK // LANES
    y_at, sum_at, gate_at, state_at = row_offsets(count, tokens)

    def copy(j):
        some = pl.ds(j * per, per)
        return pltpu.make_async_copy(rows_ref.at[some], rows_out.at[some], sems.at[j])

    mixed = jnp.zeros((count, rank + 2 * states), jnp.float32)
    for j in range(blocks):
        xw, sw, vec = block_weights(w_ref, q_ref, j_ref, j)
        values = proj_ref[:, pl.ds(j * BLOCK, BLOCK)].astype(jnp.float32)
        conv = convolved(values, vec, count)
        mixed = mixed + mixed_of(conv, xw)
        xw_ref[j] = xw
        sw_ref[j] = sw
        x_ref[j] = values[:late]
        vec_ref[j, pl.ds(0, 8), :] = vec[:8]
        decay2 = jnp.exp(vec[8:]) * (-LOG2E)
        vec_ref[j, pl.ds(8, states), :] = decay2
        full = conv.astype(jnp.float32)
        gate = silu(proj_ref[:, pl.ds(inner + j * BLOCK, BLOCK)].astype(jnp.float32))
        for k in range(per):
            tile = j * per + k
            lanes = slice(k * LANES, (k + 1) * LANES)
            cv_ref[tile] = full[:, lanes]
            rows_ref[tile, pl.ds(gate_at, tokens), :] = gate[:, lanes]
            rows_ref[tile, pl.ds(y_at, count), :] = vec[6:7, lanes] * full[:, lanes]
            for n in range(states):
                dec_ref[tile, n] = jnp.broadcast_to(decay2[n : n + 1, lanes], (reqs, LANES))
    rounded = mixed.astype(jnp.bfloat16)
    for j in range(blocks):
        dt = softplus(
            jnp.dot(rounded[:, :rank], sw_ref[j], preferred_element_type=jnp.float32)
            + vec_ref[j, pl.ds(5, 1), :]
        )
        for k in range(per):
            dt_ref[j * per + k] = dt[:, k * LANES : (k + 1) * LANES]
    coefs = rounded[:, rank:].astype(jnp.float32)
    coef_ref[...] = coefs
    for t in range(count // reqs):
        spread(coefs[t * reqs : (t + 1) * reqs], t, b_ref, c_ref)
    accepted = acc_ref[...]
    at_ref[...] = jnp.zeros_like(at_ref)

    @pl.loop(0, tiles)
    def _(tile):
        state = [None] * states
        passed = None
        rows_ref[tile, pl.ds(state_at, states * reqs), :] = jnp.zeros((states * reqs, LANES), jnp.float32)
        for t in range(count // reqs):
            delta = dt_ref[tile, pl.ds(t * reqs, reqs), :]
            passed = delta if t == 0 else passed + delta
            rows_ref[tile, pl.ds(sum_at + t * reqs, reqs), :] = passed
            driven = delta * cv_ref[tile, pl.ds(t * reqs, reqs), :]
            chosen = accepted == t + late // reqs + 1
            pltpu.store(at_ref.at[tile], passed, mask=chosen)
            totals = [rows_ref[tile, pl.ds(y_at + t * reqs, reqs), :], None]
            for n in range(states):
                at = t * states + n
                added = driven * b_ref[at]
                state[n] = added if t == 0 else jnp.exp2(delta * dec_ref[tile, n]) * state[n] + added
                term = c_ref[at] * state[n]
                totals[n % 2] = term if totals[n % 2] is None else totals[n % 2] + term
                pltpu.store(
                    rows_ref.at[tile, pl.ds(state_at + n * reqs, reqs), :], state[n], mask=chosen
                )
            rows_ref[tile, pl.ds(y_at + t * reqs, reqs), :] = totals[0] + totals[1]

        @pl.when(tile % per == per - 1)
        def _():
            copy(tile // per).start()

    for j in range(blocks):
        copy(j).wait()


def row_offsets(count, tokens):
    return 0, count, 2 * count, 2 * count + tokens


def before(q_place, j_place, projected, weights, accepted, late, states):
    tokens = projected.shape[0]
    blocks = weights.shape[1]
    tiles = blocks * (BLOCK // LANES)
    count = tokens - late
    reqs = accepted.shape[0]
    rank = 4 * 32
    smem = pl.BlockSpec(memory_space=pltpu.SMEM)
    vmem = pl.BlockSpec(memory_space=pltpu.VMEM)
    f32 = jnp.float32
    spots = count // reqs * states
    rows = (tiles, 2 * count + tokens + states * reqs, LANES)
    return pl.pallas_call(
        before_kernel,
        out_shape=(
            pltpu.HBM(rows, f32),
            jax.ShapeDtypeStruct((tiles, reqs, LANES), f32),
            jax.ShapeDtypeStruct((count, 2 * states), f32),
            jax.ShapeDtypeStruct((blocks, rank + 2 * states, BLOCK), jnp.bfloat16),
            jax.ShapeDtypeStruct((blocks, rank, BLOCK), jnp.bfloat16),
            jax.ShapeDtypeStruct((blocks, 24, BLOCK), f32),
            jax.ShapeDtypeStruct((blocks, late, BLOCK), f32),
        ),
        in_specs=[smem, smem, vmem, vmem, vmem],
        out_specs=(pl.BlockSpec(memory_space=pltpu.HBM),) + (vmem,) * 6,
        scratch_shapes=[
            pltpu.VMEM(rows, f32),
            pltpu.VMEM((tiles, count, LANES), f32),
            pltpu.VMEM((tiles, count, LANES), f32),
            pltpu.VMEM((spots, reqs, LANES), f32),
            pltpu.VMEM((spots, reqs, LANES), f32),
            pltpu.VMEM((tiles, states, reqs, LANES), f32),
            pltpu.SemaphoreType.DMA((blocks,)),
        ],
        compiler_params=pltpu.CompilerParams(vmem_limit_bytes=24 << 20),
        cost_estimate=pl.CostEstimate(flops=200_000_000, bytes_accessed=8 << 20, transcendentals=4_000_000),
        name="before_states",
    )(q_place, j_place, projected, weights, accepted)


def after_kernel(
    moved_ref, acc_ref, at_ref, coef_ref, xw_ref, sw_ref, vec_ref, x_ref, rows_in, ow_in,
    out_ref, ns_ref,
    rows_ref, ow_ref, new_ref, pick_ref, total_ref, dt_ref, cv_ref, b_ref, c_ref, done_ref, sems, out_sem,
):
    reqs, draft, _ = out_ref.shape
    blocks, late, _ = x_ref.shape
    tiles = rows_ref.shape[0]
    tokens = reqs * draft
    count = tokens - late
    states = coef_ref.shape[1] // 2
    rank = sw_ref.shape[1]
    per = BLOCK // LANES
    y_at, sum_at, gate_at, state_at = row_offsets(count, tokens)

    def copies(j):
        some, cols = pl.ds(j * per, per), pl.ds(j * BLOCK, BLOCK)
        return [
            pltpu.make_async_copy(rows_in.at[some], rows_ref.at[some], sems.at[0, j]),
            pltpu.make_async_copy(ow_in.at[cols, :], ow_ref.at[cols, :], sems.at[1, j]),
            pltpu.make_async_copy(new_ref.at[j], ns_ref.at[:, cols], sems.at[2, j]),
        ]

    def result(k):
        cols = pl.ds(k * LANES, LANES)
        return pltpu.make_async_copy(done_ref.at[k], out_ref.at[:, :, cols], out_sem.at[k])

    queue = [copies(j)[i] for j in range(blocks) for i in range(2)]
    for copy in queue[:AHEAD]:
        copy.start()
    mixed = jnp.zeros((late, rank + 2 * states), jnp.float32)
    for j in range(blocks):
        history = [
            moved_ref[j, :, pl.ds((states + e) * BLOCK, BLOCK)].astype(jnp.float32) for e in range(3)
        ]
        conv = convolved(jnp.concatenate(history + [x_ref[j]], axis=0), vec_ref[j], late)
        cv_ref[j] = conv.astype(jnp.float32)
        mixed = mixed + mixed_of(conv, xw_ref[j])
    rounded = mixed.astype(jnp.bfloat16)
    for j in range(blocks):
        dt_ref[j] = softplus(
            jnp.dot(rounded[:, :rank], sw_ref[j], preferred_element_type=jnp.float32)
            + vec_ref[j, pl.ds(5, 1), :]
        )
    coefs = rounded[:, rank:].astype(jnp.float32)
    for t in range(draft):
        if t * reqs < late:
            rows = coefs[t * reqs : (t + 1) * reqs]
        else:
            rows = coef_ref[pl.ds(t * reqs - late, reqs), :]
        for n in range(states):
            at = t * states + n
            if t * reqs < late:
                b_ref[at] = jnp.broadcast_to(rows[:, n : n + 1], (reqs, LANES))
            c_ref[at] = jnp.broadcast_to(rows[:, states + n : states + n + 1], (reqs, LANES))
    accepted = acc_ref[...]
    def project(j, gated):
        added = jnp.dot(
            gated, ow_ref[pl.ds(j * BLOCK, BLOCK), :], preferred_element_type=jnp.float32
        )
        for k in range(total_ref.shape[0]):
            part = added[:, k * LANES : (k + 1) * LANES]
            total_ref[k] = part if j == 0 else total_ref[k] + part

    ready = None
    for j in range(blocks):
        for at in (2 * j - 1, 2 * j):
            if at >= 0:
                queue[at].wait()
                if at + AHEAD < len(queue):
                    queue[at + AHEAD].start()
        if ready is not None:
            project(j - 1, ready)
        gated = []
        for k in range(per):
            tile = j * per + k
            lanes = pl.ds(k * LANES, LANES)
            skip = vec_ref[j, pl.ds(6, 1), lanes]
            state = [
                moved_ref[j, :, pl.ds(n * BLOCK + k * LANES, LANES)].astype(jnp.float32)
                for n in range(states)
            ]
            decay = [
                jnp.broadcast_to(vec_ref[j, pl.ds(8 + n, 1), lanes], (reqs, LANES))
                for n in range(states)
            ]
            outs = []
            for t in range(late // reqs):
                rows = pl.ds(t * reqs, reqs)
                delta = dt_ref[j, rows, lanes]
                value = cv_ref[j, rows, lanes]
                driven = delta * value
                chosen = accepted == t + 1
                totals = [skip * value, None]
                for n in range(states):
                    at = t * states + n
                    state[n] = jnp.exp2(delta * decay[n]) * state[n] + driven * b_ref[at]
                    term = c_ref[at] * state[n]
                    totals[n % 2] = term if totals[n % 2] is None else totals[n % 2] + term
                    pltpu.store(pick_ref.at[tile, pl.ds(n * reqs, reqs), :], state[n], mask=chosen)
                outs.append(totals[0] + totals[1])
            beyond = accepted > late // reqs
            passed = at_ref[tile]
            for n in range(states):
                keep = pl.ds(n * reqs, reqs)
                ahead = rows_ref[tile, pl.ds(state_at + n * reqs, reqs), :]
                value = jnp.exp2(passed * decay[n]) * state[n] + ahead
                pltpu.store(pick_ref.at[tile, keep, :], value, mask=beyond)
            for t in range(late // reqs, draft):
                row = t * reqs - late
                passed = rows_ref[tile, pl.ds(sum_at + row, reqs), :]
                totals = [rows_ref[tile, pl.ds(y_at + row, reqs), :], None]
                for n in range(states):
                    term = c_ref[t * states + n] * (jnp.exp2(passed * decay[n]) * state[n])
                    totals[n % 2] = term if totals[n % 2] is None else totals[n % 2] + term
                outs.append(totals[0] + totals[1])
            for r in range(reqs):
                new_ref[j, pl.ds(r * states, states), lanes] = pick_ref[
                    tile, pl.ds(r, states, stride=reqs), :
                ]
            gated.append(jnp.concatenate(outs, axis=0) * rows_ref[tile, pl.ds(gate_at, tokens), :])
        copies(j)[2].start()
        ready = jnp.concatenate(gated, axis=1).astype(jnp.bfloat16)
    queue[-1].wait()
    project(blocks - 1, ready)
    for k in range(total_ref.shape[0]):
        for r in range(reqs):
            rows = total_ref[k, pl.ds(r, draft, stride=reqs), :]
            done_ref[k, r] = rows.astype(jnp.bfloat16)
        result(k).start()
    for j in range(blocks):
        copies(j)[2].wait()
    for k in range(total_ref.shape[0]):
        result(k).wait()


def after(moved, accepted, early, out_weight):
    rows, at, coefs, xw, sw, vec, x = early
    blocks, reqs, _ = moved.shape
    tiles = at.shape[0]
    states = coefs.shape[1] // 2
    late = x.shape[1]
    tokens = coefs.shape[0] + late
    draft = tokens // reqs
    inner, width = out_weight.shape
    vmem = pl.BlockSpec(memory_space=pltpu.VMEM)
    hbm = pl.BlockSpec(memory_space=pltpu.HBM)
    f32 = jnp.float32
    return pl.pallas_call(
        after_kernel,
        out_shape=(
            jax.ShapeDtypeStruct((reqs, draft, width), jnp.bfloat16),
            jax.ShapeDtypeStruct((reqs * states, inner), f32),
        ),
        in_specs=[vmem] * 8 + [hbm] * 2,
        out_specs=(hbm, hbm),
        scratch_shapes=[
            pltpu.VMEM(rows.shape, f32),
            pltpu.VMEM(out_weight.shape, jnp.bfloat16),
            pltpu.VMEM((blocks, reqs * states, BLOCK), f32),
            pltpu.VMEM((tiles, states * reqs, LANES), f32),
            pltpu.VMEM((width // LANES, tokens, LANES), f32),
            pltpu.VMEM((blocks, late, BLOCK), f32),
            pltpu.VMEM((blocks, late, BLOCK), f32),
            pltpu.VMEM((late // reqs * states, reqs, LANES), f32),
            pltpu.VMEM((draft * states, reqs, LANES), f32),
            pltpu.VMEM((width // LANES, reqs, draft, LANES), jnp.bfloat16),
            pltpu.SemaphoreType.DMA((3, blocks)),
            pltpu.SemaphoreType.DMA((width // LANES,)),
        ],
        compiler_params=pltpu.CompilerParams(vmem_limit_bytes=24 << 20),
        cost_estimate=pl.CostEstimate(
            flops=2 * tokens * inner * width, bytes_accessed=12 << 20, transcendentals=4_000_000
        ),
        name="after_states",
    )(moved, accepted, at, coefs, xw, sw, vec, x, in_hbm(rows), in_hbm(out_weight))


def exchange(values):
    return lax.all_to_all(values, "req", split_axis=0, concat_axis=0, tiled=True)


def select_kernel(mask_ref, arrived_ref, out_ref, kept_ref, sems):
    width = arrived_ref.shape[1] // 19
    copies = []
    for at in range(0, 19, 4):
        parts = [(0, 4)] if at < 16 else [(e + 1, 1) for e in range(3)]
        start = at
        for which, size in parts:
            cols = pl.ds(start * width, size * width)
            kept_ref[:, cols] = jnp.dot(
                mask_ref[which], arrived_ref[:, cols], preferred_element_type=jnp.float32
            ).astype(jnp.bfloat16)
            start += size
        cols = pl.ds(at * width, (start - at) * width)
        copies.append(pltpu.make_async_copy(kept_ref.at[:, cols], out_ref.at[:, cols], sems.at[at // 4]))
        copies[-1].start()
    for copy in copies:
        copy.wait()


def select(masks, arrived):
    if arrived.shape[1] % (19 * LANES) == 0:
        return pl.pallas_call(
            select_kernel,
            out_shape=pltpu.HBM(arrived.shape, jnp.bfloat16),
            in_specs=[pl.BlockSpec(memory_space=pltpu.VMEM)] * 2,
            out_specs=pl.BlockSpec(memory_space=pltpu.HBM),
            scratch_shapes=[pltpu.VMEM(arrived.shape, jnp.bfloat16), pltpu.SemaphoreType.DMA((5,))],
            compiler_params=pltpu.CompilerParams(vmem_limit_bytes=16 << 20),
            name="select_slots",
        )(masks, arrived)
    width = arrived.shape[1] // 19
    cut = [0] + [(16 + e) * width for e in range(4)]
    return jnp.concatenate(
        [
            jnp.dot(
                masks[i], arrived[:, cut[i] : cut[i + 1]], preferred_element_type=jnp.float32
            ).astype(jnp.bfloat16)
            for i in range(4)
        ],
        axis=1,
    )


def on_device(
    groups,
    hidden,
    norm_gain,
    in_weight,
    conv_weight,
    conv_bias,
    x_weight,
    step_weight,
    step_bias,
    log_decay,
    skip_gain,
    out_weight,
    old_states,
    old_edges,
    anchor,
    fresh_flag,
    accepted,
    request_ages,
):
    local_reqs, draft_len, width = hidden.shape
    inner_width = out_weight.shape[0]
    channels = conv_weight.shape[1]
    state_size = log_decay.shape[0]
    span = old_edges.shape[1]
    all_reqs = anchor.shape[0]
    blocks = inner_width // channels
    tokens = draft_len * local_reqs

    packed, share = prepared(
        old_states, old_edges, x_weight, step_weight, conv_weight, conv_bias, step_bias, skip_gain, log_decay
    )
    arrived = exchange(packed.reshape(all_reqs, (state_size + span) * channels))
    old_slot = jnp.arange(all_reqs, dtype=jnp.int32)
    chosen = (anchor[:, None] == old_slot[None, :]) & (fresh_flag[:, None] == 0)
    masks = jnp.stack([chosen] + [chosen & (span - e <= request_ages)[:, None] for e in range(span)])
    token_major = jnp.swapaxes(hidden, 0, 1).reshape(tokens, width)
    normed = rms_normed(token_major, norm_gain)
    projected = jnp.dot(normed, in_weight, preferred_element_type=jnp.float32).astype(jnp.bfloat16)
    masks, projected = lax.optimization_barrier((masks.astype(jnp.bfloat16), projected))
    moved = exchange(select(masks, arrived))

    top = blocks // 2
    weights = jnp.concatenate(
        [share[None]] + [moved_by(share[None], "req", bits) for bits in (top, top // 2, top + top // 2)]
    )
    weights = doubled(doubled(weights, "req", top // 4)[None], "grp", groups // 2)
    q_place, j_place = places("grp"), places("req")
    if channels != BLOCK:
        moved = moved.reshape(blocks, local_reqs, state_size + span, channels).transpose(1, 2, 0, 3)
        moved = moved.reshape(local_reqs, state_size + span, -1, BLOCK).transpose(2, 0, 1, 3)
        weights = jnp.take(weights, j_place, axis=1).swapaxes(1, 2)
        weights = weights.reshape(groups, SHARE, -1, BLOCK).swapaxes(1, 2)
        j_place = jnp.arange(inner_width // BLOCK, dtype=jnp.int32)
    moved = moved.reshape(inner_width // BLOCK, local_reqs, (state_size + span) * BLOCK)

    mine = lax.dynamic_slice_in_dim(accepted, lax.axis_index("req") * local_reqs, local_reqs, 0)
    mine = jnp.broadcast_to(mine[:, None], (local_reqs, LANES))
    early = before(q_place, j_place, projected, weights, mine, span * local_reqs, state_size)
    layer_out, new_states = after(moved, mine, early, out_weight)
    return layer_out, new_states.reshape(local_reqs, state_size, inner_width)


def solution(mesh):
    return jax.shard_map(
        functools.partial(on_device, mesh.shape["grp"]),
        mesh=mesh,
        in_specs=(
            P(("grp", "req"), None, None),
            P(),
            P(),
            P(None, "req"),
            P("req"),
            P("req", None),
            P(None, "req"),
            P("req"),
            P(None, "req"),
            P("req"),
            P(),
            P(("grp", "req"), None, None),
            P(("grp", "req"), None, None),
            P("grp"),
            P("grp"),
            P("grp"),
            P("grp"),
        ),
        out_specs=(P(("grp", "req"), None, None), P(("grp", "req"), None, None)),
        check_vma=False,
    )
```

```python
import functools

import jax
import jax.numpy as jnp
from jax import lax
from jax.experimental import pallas as pl
from jax.experimental.pallas import tpu as pltpu
from jax.sharding import PartitionSpec as P

EPS = 1e-05
LOG2E = 1.4426950408889634
LANES = 128
BLOCK = 256
SHARE = 88
AHEAD = 6


def rms_normed(values_in, norm_gain):
    values = values_in.astype(jnp.float32)
    factor = lax.rsqrt(jnp.mean(values * values, axis=-1, keepdims=True) + EPS)
    return (values * factor * norm_gain).astype(jnp.bfloat16)


def in_hbm(values):
    return pltpu.with_memory_space_constraint(values, pltpu.HBM)


def send_kernel(
    group_ref, state_ref, edge_ref, xt_ref, sw_ref, cw_ref, cb_ref, sb_ref, sk_ref, ld_ref,
    out_ref, share_ref,
    tile_ref, held_ref, send_ref, xt_in, sw_in, vec_ref, sems, few,
):
    blocks, slots, _ = out_ref.shape
    width = state_ref.shape[1] // blocks
    states = state_ref.shape[0] // slots
    per = width // LANES
    rank = sw_ref.shape[0]

    def load(tile):
        cols = pl.ds(tile * LANES, LANES)
        return pltpu.make_async_copy(state_ref.at[:, cols], tile_ref.at[tile], sems.at[0, tile])

    def store(dest):
        return pltpu.make_async_copy(send_ref.at[dest], out_ref.at[dest], sems.at[1, dest])

    small = [
        (edge_ref, held_ref),
        (xt_ref, xt_in),
        (sw_ref, sw_in),
        (cw_ref, vec_ref.at[pl.ds(0, 4), :]),
        (cb_ref, vec_ref.at[pl.ds(4, 1), :]),
        (sb_ref, vec_ref.at[pl.ds(5, 1), :]),
        (sk_ref, vec_ref.at[pl.ds(6, 1), :]),
        (ld_ref, vec_ref.at[pl.ds(8, 16), :]),
    ]
    copies = [pltpu.make_async_copy(x, y, few.at[i]) for i, (x, y) in enumerate(small)]
    vec_ref[pl.ds(7, 1), :] = jnp.zeros((1, width), jnp.float32)
    vec_ref[pl.ds(24, 8), :] = jnp.zeros((8, width), jnp.float32)
    copies[0].start()
    for tile in range(blocks * per):
        load(tile).start()
    for copy in copies[1:]:
        copy.start()
    copies[0].wait()
    for dest in range(blocks):
        for e in range(edge_ref.shape[0]):
            at = (states + e) * width
            send_ref[dest, :, pl.ds(at, width)] = held_ref[e, :, pl.ds(dest * width, width)]
        for part in range(per):
            tile = dest * per + part
            load(tile).wait()
            for n in range(states):
                rows = tile_ref[tile, pl.ds(n, slots, stride=states), :]
                send_ref[dest, :, pl.ds(n * width + part * LANES, LANES)] = rows.astype(jnp.bfloat16)
        store(dest).start()
    for copy in copies[1:]:
        copy.wait()
    for k in range(4):

        @pl.when(group_ref[0] == k)
        def _():
            vec = vec_ref[pl.ds(16 * (k % 2), 16), :]
            high = vec.astype(jnp.bfloat16).astype(jnp.float32)
            part = high if k < 2 else vec - high
            rows = [
                xt_in[pl.ds(32 * k, 32), :].astype(jnp.float32),
                xt_in[pl.ds(rank + 8 * k, 8), :].astype(jnp.float32),
                part[:8],
                sw_in[pl.ds(32 * k, 32), :].astype(jnp.float32),
                part[8:],
            ]
            share_ref[...] = jnp.concatenate(rows, axis=0).astype(jnp.bfloat16)

    for dest in range(blocks):
        store(dest).wait()


def prepared(
    old_states, old_edges, x_weight, step_weight, conv_weight, conv_bias, step_bias, skip_gain, log_decay
):
    slots, states, inner = old_states.shape
    span = old_edges.shape[1]
    width = x_weight.shape[0]
    blocks = inner // width
    rank = step_weight.shape[0]
    edges = jnp.swapaxes(old_edges, 0, 1)
    xt = x_weight.T
    group = lax.axis_index("grp").astype(jnp.int32)
    if width % LANES == 0 and slots == 8:
        tiles = inner // LANES
        vmem = pl.BlockSpec(memory_space=pltpu.VMEM)
        hbm = pl.BlockSpec(memory_space=pltpu.HBM)
        given = (
            old_states.reshape(slots * states, inner), edges, xt, step_weight, conv_weight,
            conv_bias[None], step_bias[None], skip_gain[None], log_decay,
        )
        return pl.pallas_call(
            send_kernel,
            out_shape=(
                pltpu.HBM((blocks, slots, (states + span) * width), jnp.bfloat16),
                jax.ShapeDtypeStruct((SHARE, width), jnp.bfloat16),
            ),
            in_specs=[pl.BlockSpec(memory_space=pltpu.SMEM)] + [hbm] * len(given),
            out_specs=(hbm, vmem),
            scratch_shapes=[
                pltpu.VMEM((tiles, slots * states, LANES), jnp.float32),
                pltpu.VMEM((span, slots, inner), jnp.bfloat16),
                pltpu.VMEM((blocks, slots, (states + span) * width), jnp.bfloat16),
                pltpu.VMEM(xt.shape, jnp.bfloat16),
                pltpu.VMEM(step_weight.shape, jnp.bfloat16),
                pltpu.VMEM((32, width), jnp.float32),
                pltpu.SemaphoreType.DMA((2, tiles)),
                pltpu.SemaphoreType.DMA((8,)),
            ],
            compiler_params=pltpu.CompilerParams(vmem_limit_bytes=16 << 20),
            name="send_states",
        )(group[None], *[in_hbm(x) for x in given])
    lead = jnp.swapaxes(old_states.astype(jnp.bfloat16), 0, 1)
    both = jnp.concatenate([lead, edges], axis=0)
    both = both.reshape(states + span, slots, blocks, width)
    packed = both.transpose(2, 1, 0, 3).reshape(blocks, slots, (states + span) * width)
    none = jnp.zeros_like(conv_bias)[None]
    vec = jnp.concatenate(
        [conv_weight, conv_bias[None], step_bias[None], skip_gain[None], none, log_decay], axis=0
    )
    vec = jnp.pad(vec, ((0, 8), (0, 0)))
    high = vec.astype(jnp.bfloat16)
    halves = jnp.concatenate([high, (vec - high.astype(jnp.float32)).astype(jnp.bfloat16)], axis=0)
    halves = halves.reshape(4, 16, width)
    stacked = jnp.concatenate(
        [
            xt[:rank].reshape(4, 32, width),
            xt[rank:].reshape(4, 8, width),
            halves[:, :8],
            step_weight.reshape(4, 32, width),
            halves[:, 8:],
        ],
        axis=1,
    )
    return packed, lax.dynamic_index_in_dim(stacked, group, 0, keepdims=False)


def moved_by(values, axis, bits):
    return lax.ppermute(values, axis, [(i, i ^ bits) for i in range(lax.axis_size(axis))])


def doubled(values, axis, bit):
    while bit:
        values = jnp.concatenate([values, moved_by(values, axis, bit)], axis=0)
        bit //= 2
    return values


def places(axis):
    size = lax.axis_size(axis)
    offset = jnp.arange(size, dtype=jnp.int32) ^ lax.axis_index(axis).astype(jnp.int32)
    place = jnp.zeros_like(offset)
    bit, top = 1, size // 2
    while top:
        place = place | jnp.where((offset & bit) != 0, top, 0)
        bit, top = bit * 2, top // 2
    return place


def block_weights(w_ref, q_ref, j_ref, j):
    at = j_ref[j]
    quarters = [w_ref.at[q_ref[q], at] for q in range(4)]
    f32 = jnp.float32
    xw = jnp.concatenate(
        [w[pl.ds(0, 32), :].astype(f32) for w in quarters] + [w[pl.ds(32, 8), :].astype(f32) for w in quarters],
        axis=0,
    ).astype(jnp.bfloat16)
    sw = jnp.concatenate([w[pl.ds(48, 32), :] for w in quarters], axis=0)
    first = [w[pl.ds(40, 8), :].astype(f32) for w in quarters]
    second = [w[pl.ds(80, 8), :].astype(f32) for w in quarters]
    high = jnp.concatenate([first[0], second[0], first[1]], axis=0)
    low = jnp.concatenate([first[2], second[2], first[3]], axis=0)
    return xw, sw, high + low


def silu(values):
    return values / (1.0 + jnp.exp(-values))


def convolved(sequence, vec, count):
    reqs = (sequence.shape[0] - count) // 3
    running = vec[4:5]
    for k in range(4):
        running = running + vec[k : k + 1] * sequence[k * reqs : k * reqs + count]
    return silu(running).astype(jnp.bfloat16)


def softplus(values):
    return jnp.maximum(values, 0.0) + jnp.log1p(jnp.exp(-jnp.abs(values)))


def mixed_of(conv, xw):
    return lax.dot_general(conv, xw, (((1,), (1,)), ((), ())), preferred_element_type=jnp.float32)


def spread(rows, t, b_ref, c_ref):
    reqs, both = rows.shape
    states = both // 2
    for n in range(states):
        b_ref[t * states + n] = jnp.broadcast_to(rows[:, n : n + 1], (reqs, LANES))
        c_ref[t * states + n] = jnp.broadcast_to(rows[:, states + n : states + n + 1], (reqs, LANES))


def before_kernel(
    q_ref, j_ref, proj_ref, w_ref, acc_ref,
    rows_out, at_ref, coef_ref, xw_ref, sw_ref, vec_ref, x_ref,
    rows_ref, dt_ref, cv_ref, b_ref, c_ref, dec_ref, sems,
):
    blocks = w_ref.shape[1]
    tiles, count, _ = dt_ref.shape
    tokens = proj_ref.shape[0]
    late = tokens - count
    reqs = late // 3
    states = b_ref.shape[0] * reqs // count
    inner = blocks * BLOCK
    rank = sw_ref.shape[1]
    per = BLOCK // LANES
    y_at, sum_at, gate_at, state_at = row_offsets(count, tokens)

    def copy(j):
        some = pl.ds(j * per, per)
        return pltpu.make_async_copy(rows_ref.at[some], rows_out.at[some], sems.at[j])

    mixed = jnp.zeros((count, rank + 2 * states), jnp.float32)
    for j in range(blocks):
        xw, sw, vec = block_weights(w_ref, q_ref, j_ref, j)
        values = proj_ref[:, pl.ds(j * BLOCK, BLOCK)].astype(jnp.float32)
        conv = convolved(values, vec, count)
        mixed = mixed + mixed_of(conv, xw)
        xw_ref[j] = xw
        sw_ref[j] = sw
        x_ref[j] = values[:late]
        vec_ref[j, pl.ds(0, 8), :] = vec[:8]
        decay2 = jnp.exp(vec[8:]) * (-LOG2E)
        vec_ref[j, pl.ds(8, states), :] = decay2
        full = conv.astype(jnp.float32)
        gate = silu(proj_ref[:, pl.ds(inner + j * BLOCK, BLOCK)].astype(jnp.float32))
        for k in range(per):
            tile = j * per + k
            lanes = slice(k * LANES, (k + 1) * LANES)
            cv_ref[tile] = full[:, lanes]
            rows_ref[tile, pl.ds(gate_at, tokens), :] = gate[:, lanes]
            rows_ref[tile, pl.ds(y_at, count), :] = vec[6:7, lanes] * full[:, lanes]
            for n in range(states):
                dec_ref[tile, n] = jnp.broadcast_to(decay2[n : n + 1, lanes], (reqs, LANES))
    rounded = mixed.astype(jnp.bfloat16)
    for j in range(blocks):
        dt = softplus(
            jnp.dot(rounded[:, :rank], sw_ref[j], preferred_element_type=jnp.float32)
            + vec_ref[j, pl.ds(5, 1), :]
        )
        for k in range(per):
            dt_ref[j * per + k] = dt[:, k * LANES : (k + 1) * LANES]
    coefs = rounded[:, rank:].astype(jnp.float32)
    coef_ref[...] = coefs
    for t in range(count // reqs):
        spread(coefs[t * reqs : (t + 1) * reqs], t, b_ref, c_ref)
    accepted = acc_ref[...]
    at_ref[...] = jnp.zeros_like(at_ref)

    @pl.loop(0, tiles)
    def _(tile):
        state = [None] * states
        passed = None
        rows_ref[tile, pl.ds(state_at, states * reqs), :] = jnp.zeros((states * reqs, LANES), jnp.float32)
        for t in range(count // reqs):
            delta = dt_ref[tile, pl.ds(t * reqs, reqs), :]
            passed = delta if t == 0 else passed + delta
            rows_ref[tile, pl.ds(sum_at + t * reqs, reqs), :] = passed
            driven = delta * cv_ref[tile, pl.ds(t * reqs, reqs), :]
            chosen = accepted == t + late // reqs + 1
            pltpu.store(at_ref.at[tile], passed, mask=chosen)
            totals = [rows_ref[tile, pl.ds(y_at + t * reqs, reqs), :], None]
            for n in range(states):
                at = t * states + n
                added = driven * b_ref[at]
                state[n] = added if t == 0 else jnp.exp2(delta * dec_ref[tile, n]) * state[n] + added
                term = c_ref[at] * state[n]
                totals[n % 2] = term if totals[n % 2] is None else totals[n % 2] + term
                pltpu.store(
                    rows_ref.at[tile, pl.ds(state_at + n * reqs, reqs), :], state[n], mask=chosen
                )
            rows_ref[tile, pl.ds(y_at + t * reqs, reqs), :] = totals[0] + totals[1]

        @pl.when(tile % per == per - 1)
        def _():
            copy(tile // per).start()

    for j in range(blocks):
        copy(j).wait()


def row_offsets(count, tokens):
    return 0, count, 2 * count, 2 * count + tokens


def before(q_place, j_place, projected, weights, accepted, late, states):
    tokens = projected.shape[0]
    blocks = weights.shape[1]
    tiles = blocks * (BLOCK // LANES)
    count = tokens - late
    reqs = accepted.shape[0]
    rank = 4 * 32
    smem = pl.BlockSpec(memory_space=pltpu.SMEM)
    vmem = pl.BlockSpec(memory_space=pltpu.VMEM)
    f32 = jnp.float32
    spots = count // reqs * states
    rows = (tiles, 2 * count + tokens + states * reqs, LANES)
    return pl.pallas_call(
        before_kernel,
        out_shape=(
            pltpu.HBM(rows, f32),
            jax.ShapeDtypeStruct((tiles, reqs, LANES), f32),
            jax.ShapeDtypeStruct((count, 2 * states), f32),
            jax.ShapeDtypeStruct((blocks, rank + 2 * states, BLOCK), jnp.bfloat16),
            jax.ShapeDtypeStruct((blocks, rank, BLOCK), jnp.bfloat16),
            jax.ShapeDtypeStruct((blocks, 24, BLOCK), f32),
            jax.ShapeDtypeStruct((blocks, late, BLOCK), f32),
        ),
        in_specs=[smem, smem, vmem, vmem, vmem],
        out_specs=(pl.BlockSpec(memory_space=pltpu.HBM),) + (vmem,) * 6,
        scratch_shapes=[
            pltpu.VMEM(rows, f32),
            pltpu.VMEM((tiles, count, LANES), f32),
            pltpu.VMEM((tiles, count, LANES), f32),
            pltpu.VMEM((spots, reqs, LANES), f32),
            pltpu.VMEM((spots, reqs, LANES), f32),
            pltpu.VMEM((tiles, states, reqs, LANES), f32),
            pltpu.SemaphoreType.DMA((blocks,)),
        ],
        compiler_params=pltpu.CompilerParams(vmem_limit_bytes=24 << 20),
        cost_estimate=pl.CostEstimate(flops=200_000_000, bytes_accessed=8 << 20, transcendentals=4_000_000),
        name="before_states",
    )(q_place, j_place, projected, weights, accepted)


def after_kernel(
    moved_ref, acc_ref, at_ref, coef_ref, xw_ref, sw_ref, vec_ref, x_ref, rows_in, ow_in,
    out_ref, ns_ref,
    rows_ref, ow_ref, new_ref, pick_ref, total_ref, dt_ref, cv_ref, b_ref, c_ref, done_ref, sems, out_sem,
):
    reqs, draft, _ = out_ref.shape
    blocks, late, _ = x_ref.shape
    tiles = rows_ref.shape[0]
    tokens = reqs * draft
    count = tokens - late
    states = coef_ref.shape[1] // 2
    rank = sw_ref.shape[1]
    per = BLOCK // LANES
    y_at, sum_at, gate_at, state_at = row_offsets(count, tokens)

    def copies(j):
        some, cols = pl.ds(j * per, per), pl.ds(j * BLOCK, BLOCK)
        return [
            pltpu.make_async_copy(rows_in.at[some], rows_ref.at[some], sems.at[0, j]),
            pltpu.make_async_copy(ow_in.at[cols, :], ow_ref.at[cols, :], sems.at[1, j]),
            pltpu.make_async_copy(new_ref.at[j], ns_ref.at[:, cols], sems.at[2, j]),
        ]

    def result(k):
        cols = pl.ds(k * LANES, LANES)
        return pltpu.make_async_copy(done_ref.at[k], out_ref.at[:, :, cols], out_sem.at[k])

    queue = [copies(j)[i] for j in range(blocks) for i in range(2)]
    for copy in queue[:AHEAD]:
        copy.start()
    mixed = jnp.zeros((late, rank + 2 * states), jnp.float32)
    for j in range(blocks):
        history = [
            moved_ref[j, :, pl.ds((states + e) * BLOCK, BLOCK)].astype(jnp.float32) for e in range(3)
        ]
        conv = convolved(jnp.concatenate(history + [x_ref[j]], axis=0), vec_ref[j], late)
        cv_ref[j] = conv.astype(jnp.float32)
        mixed = mixed + mixed_of(conv, xw_ref[j])
    rounded = mixed.astype(jnp.bfloat16)
    for j in range(blocks):
        dt_ref[j] = softplus(
            jnp.dot(rounded[:, :rank], sw_ref[j], preferred_element_type=jnp.float32)
            + vec_ref[j, pl.ds(5, 1), :]
        )
    coefs = rounded[:, rank:].astype(jnp.float32)
    for t in range(draft):
        if t * reqs < late:
            rows = coefs[t * reqs : (t + 1) * reqs]
        else:
            rows = coef_ref[pl.ds(t * reqs - late, reqs), :]
        for n in range(states):
            at = t * states + n
            if t * reqs < late:
                b_ref[at] = jnp.broadcast_to(rows[:, n : n + 1], (reqs, LANES))
            c_ref[at] = jnp.broadcast_to(rows[:, states + n : states + n + 1], (reqs, LANES))
    accepted = acc_ref[...]
    def project(j, gated):
        added = jnp.dot(
            gated, ow_ref[pl.ds(j * BLOCK, BLOCK), :], preferred_element_type=jnp.float32
        )
        for k in range(total_ref.shape[0]):
            part = added[:, k * LANES : (k + 1) * LANES]
            total_ref[k] = part if j == 0 else total_ref[k] + part

    ready = None
    for j in range(blocks):
        for at in (2 * j - 1, 2 * j):
            if at >= 0:
                queue[at].wait()
                if at + AHEAD < len(queue):
                    queue[at + AHEAD].start()
        if ready is not None:
            project(j - 1, ready)
        gated = []
        for k in range(per):
            tile = j * per + k
            lanes = pl.ds(k * LANES, LANES)
            skip = vec_ref[j, pl.ds(6, 1), lanes]
            state = [
                moved_ref[j, :, pl.ds(n * BLOCK + k * LANES, LANES)].astype(jnp.float32)
                for n in range(states)
            ]
            decay = [
                jnp.broadcast_to(vec_ref[j, pl.ds(8 + n, 1), lanes], (reqs, LANES))
                for n in range(states)
            ]
            outs = []
            for t in range(late // reqs):
                rows = pl.ds(t * reqs, reqs)
                delta = dt_ref[j, rows, lanes]
                value = cv_ref[j, rows, lanes]
                driven = delta * value
                chosen = accepted == t + 1
                totals = [skip * value, None]
                for n in range(states):
                    at = t * states + n
                    state[n] = jnp.exp2(delta * decay[n]) * state[n] + driven * b_ref[at]
                    term = c_ref[at] * state[n]
                    totals[n % 2] = term if totals[n % 2] is None else totals[n % 2] + term
                    pltpu.store(pick_ref.at[tile, pl.ds(n * reqs, reqs), :], state[n], mask=chosen)
                outs.append(totals[0] + totals[1])
            beyond = accepted > late // reqs
            passed = at_ref[tile]
            for n in range(states):
                keep = pl.ds(n * reqs, reqs)
                ahead = rows_ref[tile, pl.ds(state_at + n * reqs, reqs), :]
                value = jnp.exp2(passed * decay[n]) * state[n] + ahead
                pltpu.store(pick_ref.at[tile, keep, :], value, mask=beyond)
            for t in range(late // reqs, draft):
                row = t * reqs - late
                passed = rows_ref[tile, pl.ds(sum_at + row, reqs), :]
                totals = [rows_ref[tile, pl.ds(y_at + row, reqs), :], None]
                for n in range(states):
                    term = c_ref[t * states + n] * (jnp.exp2(passed * decay[n]) * state[n])
                    totals[n % 2] = term if totals[n % 2] is None else totals[n % 2] + term
                outs.append(totals[0] + totals[1])
            for r in range(reqs):
                new_ref[j, pl.ds(r * states, states), lanes] = pick_ref[
                    tile, pl.ds(r, states, stride=reqs), :
                ]
            gated.append(jnp.concatenate(outs, axis=0) * rows_ref[tile, pl.ds(gate_at, tokens), :])
        copies(j)[2].start()
        ready = jnp.concatenate(gated, axis=1).astype(jnp.bfloat16)
    queue[-1].wait()
    project(blocks - 1, ready)
    for k in range(total_ref.shape[0]):
        for r in range(reqs):
            rows = total_ref[k, pl.ds(r, draft, stride=reqs), :]
            done_ref[k, r] = rows.astype(jnp.bfloat16)
        result(k).start()
    for j in range(blocks):
        copies(j)[2].wait()
    for k in range(total_ref.shape[0]):
        result(k).wait()


def after(moved, accepted, early, out_weight):
    rows, at, coefs, xw, sw, vec, x = early
    blocks, reqs, _ = moved.shape
    tiles = at.shape[0]
    states = coefs.shape[1] // 2
    late = x.shape[1]
    tokens = coefs.shape[0] + late
    draft = tokens // reqs
    inner, width = out_weight.shape
    vmem = pl.BlockSpec(memory_space=pltpu.VMEM)
    hbm = pl.BlockSpec(memory_space=pltpu.HBM)
    f32 = jnp.float32
    return pl.pallas_call(
        after_kernel,
        out_shape=(
            jax.ShapeDtypeStruct((reqs, draft, width), jnp.bfloat16),
            jax.ShapeDtypeStruct((reqs * states, inner), f32),
        ),
        in_specs=[vmem] * 8 + [hbm] * 2,
        out_specs=(hbm, hbm),
        scratch_shapes=[
            pltpu.VMEM(rows.shape, f32),
            pltpu.VMEM(out_weight.shape, jnp.bfloat16),
            pltpu.VMEM((blocks, reqs * states, BLOCK), f32),
            pltpu.VMEM((tiles, states * reqs, LANES), f32),
            pltpu.VMEM((width // LANES, tokens, LANES), f32),
            pltpu.VMEM((blocks, late, BLOCK), f32),
            pltpu.VMEM((blocks, late, BLOCK), f32),
            pltpu.VMEM((late // reqs * states, reqs, LANES), f32),
            pltpu.VMEM((draft * states, reqs, LANES), f32),
            pltpu.VMEM((width // LANES, reqs, draft, LANES), jnp.bfloat16),
            pltpu.SemaphoreType.DMA((3, blocks)),
            pltpu.SemaphoreType.DMA((width // LANES,)),
        ],
        compiler_params=pltpu.CompilerParams(vmem_limit_bytes=24 << 20),
        cost_estimate=pl.CostEstimate(
            flops=2 * tokens * inner * width, bytes_accessed=12 << 20, transcendentals=4_000_000
        ),
        name="after_states",
    )(moved, accepted, at, coefs, xw, sw, vec, x, in_hbm(rows), in_hbm(out_weight))


def exchange(values):
    return lax.all_to_all(values, "req", split_axis=0, concat_axis=0, tiled=True)


def select_kernel(mask_ref, arrived_ref, out_ref, kept_ref, sems):
    width = arrived_ref.shape[1] // 19
    copies = []
    for at in range(0, 19, 4):
        parts = [(0, 4)] if at < 16 else [(e + 1, 1) for e in range(3)]
        start = at
        for which, size in parts:
            cols = pl.ds(start * width, size * width)
            kept_ref[:, cols] = jnp.dot(
                mask_ref[which], arrived_ref[:, cols], preferred_element_type=jnp.float32
            ).astype(jnp.bfloat16)
            start += size
        cols = pl.ds(at * width, (start - at) * width)
        copies.append(pltpu.make_async_copy(kept_ref.at[:, cols], out_ref.at[:, cols], sems.at[at // 4]))
        copies[-1].start()
    for copy in copies:
        copy.wait()


def select(masks, arrived):
    if arrived.shape[1] % (19 * LANES) == 0:
        return pl.pallas_call(
            select_kernel,
            out_shape=pltpu.HBM(arrived.shape, jnp.bfloat16),
            in_specs=[pl.BlockSpec(memory_space=pltpu.VMEM)] * 2,
            out_specs=pl.BlockSpec(memory_space=pltpu.HBM),
            scratch_shapes=[pltpu.VMEM(arrived.shape, jnp.bfloat16), pltpu.SemaphoreType.DMA((5,))],
            compiler_params=pltpu.CompilerParams(vmem_limit_bytes=16 << 20),
            name="select_slots",
        )(masks, arrived)
    width = arrived.shape[1] // 19
    cut = [0] + [(16 + e) * width for e in range(4)]
    return jnp.concatenate(
        [
            jnp.dot(
                masks[i], arrived[:, cut[i] : cut[i + 1]], preferred_element_type=jnp.float32
            ).astype(jnp.bfloat16)
            for i in range(4)
        ],
        axis=1,
    )


def on_device(
    groups,
    hidden,
    norm_gain,
    in_weight,
    conv_weight,
    conv_bias,
    x_weight,
    step_weight,
    step_bias,
    log_decay,
    skip_gain,
    out_weight,
    old_states,
    old_edges,
    anchor,
    fresh_flag,
    accepted,
    request_ages,
):
    local_reqs, draft_len, width = hidden.shape
    inner_width = out_weight.shape[0]
    channels = conv_weight.shape[1]
    state_size = log_decay.shape[0]
    span = old_edges.shape[1]
    all_reqs = anchor.shape[0]
    blocks = inner_width // channels
    tokens = draft_len * local_reqs

    packed, share = prepared(
        old_states, old_edges, x_weight, step_weight, conv_weight, conv_bias, step_bias, skip_gain, log_decay
    )
    arrived = exchange(packed.reshape(all_reqs, (state_size + span) * channels))
    top = blocks // 2
    weights = jnp.concatenate(
        [share[None]] + [moved_by(share[None], "req", bits) for bits in (top, top // 2, top + top // 2)]
    )
    hidden, weights = lax.optimization_barrier((hidden, weights))
    weights = doubled(weights, "req", top // 4)[None]

    old_slot = jnp.arange(all_reqs, dtype=jnp.int32)
    chosen = (anchor[:, None] == old_slot[None, :]) & (fresh_flag[:, None] == 0)
    masks = jnp.stack([chosen] + [chosen & (span - e <= request_ages)[:, None] for e in range(span)])
    token_major = jnp.swapaxes(hidden, 0, 1).reshape(tokens, width)
    normed = rms_normed(token_major, norm_gain)
    projected = jnp.dot(normed, in_weight, preferred_element_type=jnp.float32).astype(jnp.bfloat16)
    masks, projected, weights = lax.optimization_barrier((masks.astype(jnp.bfloat16), projected, weights))
    moved = exchange(select(masks, arrived))

    q_place, j_place = places("grp"), places("req")
    weights = doubled(weights, "grp", groups // 2)
    if channels != BLOCK:
        moved = moved.reshape(blocks, local_reqs, state_size + span, channels).transpose(1, 2, 0, 3)
        moved = moved.reshape(local_reqs, state_size + span, -1, BLOCK).transpose(2, 0, 1, 3)
        weights = jnp.take(weights, j_place, axis=1).swapaxes(1, 2)
        weights = weights.reshape(groups, SHARE, -1, BLOCK).swapaxes(1, 2)
        j_place = jnp.arange(inner_width // BLOCK, dtype=jnp.int32)
    moved = moved.reshape(inner_width // BLOCK, local_reqs, (state_size + span) * BLOCK)

    mine = lax.dynamic_slice_in_dim(accepted, lax.axis_index("req") * local_reqs, local_reqs, 0)
    mine = jnp.broadcast_to(mine[:, None], (local_reqs, LANES))
    early = before(q_place, j_place, projected, weights, mine, span * local_reqs, state_size)
    layer_out, new_states = after(moved, mine, early, out_weight)
    return layer_out, new_states.reshape(local_reqs, state_size, inner_width)


def solution(mesh):
    return jax.shard_map(
        functools.partial(on_device, mesh.shape["grp"]),
        mesh=mesh,
        in_specs=(
            P(("grp", "req"), None, None),
            P(),
            P(),
            P(None, "req"),
            P("req"),
            P("req", None),
            P(None, "req"),
            P("req"),
            P(None, "req"),
            P("req"),
            P(),
            P(("grp", "req"), None, None),
            P(("grp", "req"), None, None),
            P("grp"),
            P("grp"),
            P("grp"),
            P("grp"),
        ),
        out_specs=(P(("grp", "req"), None, None), P(("grp", "req"), None, None)),
        check_vma=False,
    )
```

```python
import functools

import jax
import jax.numpy as jnp
from jax import lax
from jax.experimental import pallas as pl
from jax.experimental.pallas import tpu as pltpu
from jax.sharding import PartitionSpec as P

EPS = 1e-05
LOG2E = 1.4426950408889634
LANES = 128
BLOCK = 256
SHARE = 88
AHEAD = 6


def rms_normed(values_in, norm_gain):
    values = values_in.astype(jnp.float32)
    factor = lax.rsqrt(jnp.mean(values * values, axis=-1, keepdims=True) + EPS)
    return (values * factor * norm_gain).astype(jnp.bfloat16)


def in_hbm(values):
    return pltpu.with_memory_space_constraint(values, pltpu.HBM)


def send_kernel(
    group_ref, state_ref, edge_ref, xt_ref, sw_ref, cw_ref, cb_ref, sb_ref, sk_ref, ld_ref,
    out_ref, share_ref,
    tile_ref, held_ref, send_ref, xt_in, sw_in, vec_ref, sems, few,
):
    blocks, slots, _ = out_ref.shape
    width = state_ref.shape[1] // blocks
    states = state_ref.shape[0] // slots
    per = width // LANES
    rank = sw_ref.shape[0]

    def load(tile):
        cols = pl.ds(tile * LANES, LANES)
        return pltpu.make_async_copy(state_ref.at[:, cols], tile_ref.at[tile], sems.at[0, tile])

    def store(dest):
        return pltpu.make_async_copy(send_ref.at[dest], out_ref.at[dest], sems.at[1, dest])

    small = [
        (edge_ref, held_ref),
        (xt_ref, xt_in),
        (sw_ref, sw_in),
        (cw_ref, vec_ref.at[pl.ds(0, 4), :]),
        (cb_ref, vec_ref.at[pl.ds(4, 1), :]),
        (sb_ref, vec_ref.at[pl.ds(5, 1), :]),
        (sk_ref, vec_ref.at[pl.ds(6, 1), :]),
        (ld_ref, vec_ref.at[pl.ds(8, 16), :]),
    ]
    copies = [pltpu.make_async_copy(x, y, few.at[i]) for i, (x, y) in enumerate(small)]
    vec_ref[pl.ds(7, 1), :] = jnp.zeros((1, width), jnp.float32)
    vec_ref[pl.ds(24, 8), :] = jnp.zeros((8, width), jnp.float32)
    copies[0].start()
    for tile in range(blocks * per):
        load(tile).start()
    for copy in copies[1:]:
        copy.start()
    copies[0].wait()
    for dest in range(blocks):
        for e in range(edge_ref.shape[0]):
            at = (states + e) * width
            send_ref[dest, :, pl.ds(at, width)] = held_ref[e, :, pl.ds(dest * width, width)]
        for part in range(per):
            tile = dest * per + part
            load(tile).wait()
            for n in range(states):
                rows = tile_ref[tile, pl.ds(n, slots, stride=states), :]
                send_ref[dest, :, pl.ds(n * width + part * LANES, LANES)] = rows.astype(jnp.bfloat16)
        store(dest).start()
    for copy in copies[1:]:
        copy.wait()
    for k in range(4):

        @pl.when(group_ref[0] == k)
        def _():
            vec = vec_ref[pl.ds(16 * (k % 2), 16), :]
            high = vec.astype(jnp.bfloat16).astype(jnp.float32)
            part = high if k < 2 else vec - high
            rows = [
                xt_in[pl.ds(32 * k, 32), :].astype(jnp.float32),
                xt_in[pl.ds(rank + 8 * k, 8), :].astype(jnp.float32),
                part[:8],
                sw_in[pl.ds(32 * k, 32), :].astype(jnp.float32),
                part[8:],
            ]
            share_ref[...] = jnp.concatenate(rows, axis=0).astype(jnp.bfloat16)

    for dest in range(blocks):
        store(dest).wait()


def prepared(
    old_states, old_edges, x_weight, step_weight, conv_weight, conv_bias, step_bias, skip_gain, log_decay
):
    slots, states, inner = old_states.shape
    span = old_edges.shape[1]
    width = x_weight.shape[0]
    blocks = inner // width
    rank = step_weight.shape[0]
    edges = jnp.swapaxes(old_edges, 0, 1)
    xt = x_weight.T
    group = lax.axis_index("grp").astype(jnp.int32)
    if width % LANES == 0 and slots == 8:
        tiles = inner // LANES
        vmem = pl.BlockSpec(memory_space=pltpu.VMEM)
        hbm = pl.BlockSpec(memory_space=pltpu.HBM)
        given = (
            old_states.reshape(slots * states, inner), edges, xt, step_weight, conv_weight,
            conv_bias[None], step_bias[None], skip_gain[None], log_decay,
        )
        return pl.pallas_call(
            send_kernel,
            out_shape=(
                pltpu.HBM((blocks, slots, (states + span) * width), jnp.bfloat16),
                jax.ShapeDtypeStruct((SHARE, width), jnp.bfloat16),
            ),
            in_specs=[pl.BlockSpec(memory_space=pltpu.SMEM)] + [hbm] * len(given),
            out_specs=(hbm, vmem),
            scratch_shapes=[
                pltpu.VMEM((tiles, slots * states, LANES), jnp.float32),
                pltpu.VMEM((span, slots, inner), jnp.bfloat16),
                pltpu.VMEM((blocks, slots, (states + span) * width), jnp.bfloat16),
                pltpu.VMEM(xt.shape, jnp.bfloat16),
                pltpu.VMEM(step_weight.shape, jnp.bfloat16),
                pltpu.VMEM((32, width), jnp.float32),
                pltpu.SemaphoreType.DMA((2, tiles)),
                pltpu.SemaphoreType.DMA((8,)),
            ],
            compiler_params=pltpu.CompilerParams(vmem_limit_bytes=16 << 20),
            name="send_states",
        )(group[None], *[in_hbm(x) for x in given])
    lead = jnp.swapaxes(old_states.astype(jnp.bfloat16), 0, 1)
    both = jnp.concatenate([lead, edges], axis=0)
    both = both.reshape(states + span, slots, blocks, width)
    packed = both.transpose(2, 1, 0, 3).reshape(blocks, slots, (states + span) * width)
    none = jnp.zeros_like(conv_bias)[None]
    vec = jnp.concatenate(
        [conv_weight, conv_bias[None], step_bias[None], skip_gain[None], none, log_decay], axis=0
    )
    vec = jnp.pad(vec, ((0, 8), (0, 0)))
    high = vec.astype(jnp.bfloat16)
    halves = jnp.concatenate([high, (vec - high.astype(jnp.float32)).astype(jnp.bfloat16)], axis=0)
    halves = halves.reshape(4, 16, width)
    stacked = jnp.concatenate(
        [
            xt[:rank].reshape(4, 32, width),
            xt[rank:].reshape(4, 8, width),
            halves[:, :8],
            step_weight.reshape(4, 32, width),
            halves[:, 8:],
        ],
        axis=1,
    )
    return packed, lax.dynamic_index_in_dim(stacked, group, 0, keepdims=False)


def moved_by(values, axis, bits):
    return lax.ppermute(values, axis, [(i, i ^ bits) for i in range(lax.axis_size(axis))])


def doubled(values, axis, bit):
    while bit:
        values = jnp.concatenate([values, moved_by(values, axis, bit)], axis=0)
        bit //= 2
    return values


def places(axis):
    size = lax.axis_size(axis)
    offset = jnp.arange(size, dtype=jnp.int32) ^ lax.axis_index(axis).astype(jnp.int32)
    place = jnp.zeros_like(offset)
    bit, top = 1, size // 2
    while top:
        place = place | jnp.where((offset & bit) != 0, top, 0)
        bit, top = bit * 2, top // 2
    return place


def block_weights(w_ref, q_ref, j_ref, j):
    at = j_ref[j]
    quarters = [w_ref.at[q_ref[q], at] for q in range(4)]
    f32 = jnp.float32
    xw = jnp.concatenate(
        [w[pl.ds(0, 32), :].astype(f32) for w in quarters] + [w[pl.ds(32, 8), :].astype(f32) for w in quarters],
        axis=0,
    ).astype(jnp.bfloat16)
    sw = jnp.concatenate([w[pl.ds(48, 32), :] for w in quarters], axis=0)
    first = [w[pl.ds(40, 8), :].astype(f32) for w in quarters]
    second = [w[pl.ds(80, 8), :].astype(f32) for w in quarters]
    high = jnp.concatenate([first[0], second[0], first[1]], axis=0)
    low = jnp.concatenate([first[2], second[2], first[3]], axis=0)
    return xw, sw, high + low


def silu(values):
    return values / (1.0 + jnp.exp(-values))


def convolved(sequence, vec, count):
    reqs = (sequence.shape[0] - count) // 3
    running = vec[4:5]
    for k in range(4):
        running = running + vec[k : k + 1] * sequence[k * reqs : k * reqs + count]
    return silu(running).astype(jnp.bfloat16)


def softplus(values):
    return jnp.maximum(values, 0.0) + jnp.log1p(jnp.exp(-jnp.abs(values)))


def mixed_of(conv, xw):
    return lax.dot_general(conv, xw, (((1,), (1,)), ((), ())), preferred_element_type=jnp.float32)


def spread(rows, t, b_ref, c_ref):
    reqs, both = rows.shape
    states = both // 2
    for n in range(states):
        b_ref[t * states + n] = jnp.broadcast_to(rows[:, n : n + 1], (reqs, LANES))
        c_ref[t * states + n] = jnp.broadcast_to(rows[:, states + n : states + n + 1], (reqs, LANES))


def before_kernel(
    q_ref, j_ref, proj_ref, w_ref, acc_ref,
    rows_out, at_ref, coef_ref, xw_ref, sw_ref, vec_ref, x_ref,
    rows_ref, dt_ref, cv_ref, b_ref, c_ref, dec_ref, sems,
):
    blocks = w_ref.shape[1]
    tiles, count, _ = dt_ref.shape
    tokens = proj_ref.shape[0]
    late = tokens - count
    reqs = late // 3
    states = b_ref.shape[0] * reqs // count
    inner = blocks * BLOCK
    rank = sw_ref.shape[1]
    per = BLOCK // LANES
    y_at, sum_at, gate_at, state_at = row_offsets(count, tokens)

    def copy(j):
        some = pl.ds(j * per, per)
        return pltpu.make_async_copy(rows_ref.at[some], rows_out.at[some], sems.at[j])

    mixed = jnp.zeros((count, rank + 2 * states), jnp.float32)
    for j in range(blocks):
        xw, sw, vec = block_weights(w_ref, q_ref, j_ref, j)
        values = proj_ref[:, pl.ds(j * BLOCK, BLOCK)].astype(jnp.float32)
        conv = convolved(values, vec, count)
        mixed = mixed + mixed_of(conv, xw)
        xw_ref[j] = xw
        sw_ref[j] = sw
        x_ref[j] = values[:late]
        vec_ref[j, pl.ds(0, 8), :] = vec[:8]
        decay2 = jnp.exp(vec[8:]) * (-LOG2E)
        vec_ref[j, pl.ds(8, states), :] = decay2
        full = conv.astype(jnp.float32)
        gate = silu(proj_ref[:, pl.ds(inner + j * BLOCK, BLOCK)].astype(jnp.float32))
        for k in range(per):
            tile = j * per + k
            lanes = slice(k * LANES, (k + 1) * LANES)
            cv_ref[tile] = full[:, lanes]
            rows_ref[tile, pl.ds(gate_at, tokens), :] = gate[:, lanes]
            rows_ref[tile, pl.ds(y_at, count), :] = vec[6:7, lanes] * full[:, lanes]
            for n in range(states):
                dec_ref[tile, n] = jnp.broadcast_to(decay2[n : n + 1, lanes], (reqs, LANES))
    rounded = mixed.astype(jnp.bfloat16)
    for j in range(blocks):
        dt = softplus(
            jnp.dot(rounded[:, :rank], sw_ref[j], preferred_element_type=jnp.float32)
            + vec_ref[j, pl.ds(5, 1), :]
        )
        for k in range(per):
            dt_ref[j * per + k] = dt[:, k * LANES : (k + 1) * LANES]
    coefs = rounded[:, rank:].astype(jnp.float32)
    coef_ref[...] = coefs
    for t in range(count // reqs):
        spread(coefs[t * reqs : (t + 1) * reqs], t, b_ref, c_ref)
    accepted = acc_ref[...]
    at_ref[...] = jnp.zeros_like(at_ref)

    @pl.loop(0, tiles)
    def _(tile):
        state = [None] * states
        passed = None
        rows_ref[tile, pl.ds(state_at, states * reqs), :] = jnp.zeros((states * reqs, LANES), jnp.float32)
        for t in range(count // reqs):
            delta = dt_ref[tile, pl.ds(t * reqs, reqs), :]
            passed = delta if t == 0 else passed + delta
            rows_ref[tile, pl.ds(sum_at + t * reqs, reqs), :] = passed
            driven = delta * cv_ref[tile, pl.ds(t * reqs, reqs), :]
            chosen = accepted == t + late // reqs + 1
            pltpu.store(at_ref.at[tile], passed, mask=chosen)
            totals = [rows_ref[tile, pl.ds(y_at + t * reqs, reqs), :], None]
            for n in range(states):
                at = t * states + n
                added = driven * b_ref[at]
                state[n] = added if t == 0 else jnp.exp2(delta * dec_ref[tile, n]) * state[n] + added
                term = c_ref[at] * state[n]
                totals[n % 2] = term if totals[n % 2] is None else totals[n % 2] + term
                pltpu.store(
                    rows_ref.at[tile, pl.ds(state_at + n * reqs, reqs), :], state[n], mask=chosen
                )
            rows_ref[tile, pl.ds(y_at + t * reqs, reqs), :] = totals[0] + totals[1]

        @pl.when(tile % per == per - 1)
        def _():
            copy(tile // per).start()

    for j in range(blocks):
        copy(j).wait()


def row_offsets(count, tokens):
    return 0, count, 2 * count, 2 * count + tokens


def before(q_place, j_place, projected, weights, accepted, late, states):
    tokens = projected.shape[0]
    blocks = weights.shape[1]
    tiles = blocks * (BLOCK // LANES)
    count = tokens - late
    reqs = accepted.shape[0]
    rank = 4 * 32
    smem = pl.BlockSpec(memory_space=pltpu.SMEM)
    vmem = pl.BlockSpec(memory_space=pltpu.VMEM)
    f32 = jnp.float32
    spots = count // reqs * states
    rows = (tiles, 2 * count + tokens + states * reqs, LANES)
    return pl.pallas_call(
        before_kernel,
        out_shape=(
            pltpu.HBM(rows, f32),
            jax.ShapeDtypeStruct((tiles, reqs, LANES), f32),
            jax.ShapeDtypeStruct((count, 2 * states), f32),
            jax.ShapeDtypeStruct((blocks, rank + 2 * states, BLOCK), jnp.bfloat16),
            jax.ShapeDtypeStruct((blocks, rank, BLOCK), jnp.bfloat16),
            jax.ShapeDtypeStruct((blocks, 24, BLOCK), f32),
            jax.ShapeDtypeStruct((blocks, late, BLOCK), f32),
        ),
        in_specs=[smem, smem, vmem, vmem, vmem],
        out_specs=(pl.BlockSpec(memory_space=pltpu.HBM),) + (vmem,) * 6,
        scratch_shapes=[
            pltpu.VMEM(rows, f32),
            pltpu.VMEM((tiles, count, LANES), f32),
            pltpu.VMEM((tiles, count, LANES), f32),
            pltpu.VMEM((spots, reqs, LANES), f32),
            pltpu.VMEM((spots, reqs, LANES), f32),
            pltpu.VMEM((tiles, states, reqs, LANES), f32),
            pltpu.SemaphoreType.DMA((blocks,)),
        ],
        compiler_params=pltpu.CompilerParams(vmem_limit_bytes=24 << 20),
        cost_estimate=pl.CostEstimate(flops=200_000_000, bytes_accessed=8 << 20, transcendentals=4_000_000),
        name="before_states",
    )(q_place, j_place, projected, weights, accepted)


def after_kernel(
    moved_ref, acc_ref, at_ref, coef_ref, xw_ref, sw_ref, vec_ref, x_ref, rows_in, ow_in,
    out_ref, ns_ref,
    rows_ref, ow_ref, new_ref, pick_ref, total_ref, dt_ref, cv_ref, b_ref, c_ref, done_ref, sems, out_sem,
):
    reqs, draft, _ = out_ref.shape
    blocks, late, _ = x_ref.shape
    tiles = rows_ref.shape[0]
    tokens = reqs * draft
    count = tokens - late
    states = coef_ref.shape[1] // 2
    rank = sw_ref.shape[1]
    per = BLOCK // LANES
    y_at, sum_at, gate_at, state_at = row_offsets(count, tokens)

    def copies(j):
        some, cols = pl.ds(j * per, per), pl.ds(j * BLOCK, BLOCK)
        return [
            pltpu.make_async_copy(rows_in.at[some], rows_ref.at[some], sems.at[0, j]),
            pltpu.make_async_copy(ow_in.at[cols, :], ow_ref.at[cols, :], sems.at[1, j]),
            pltpu.make_async_copy(new_ref.at[j], ns_ref.at[:, cols], sems.at[2, j]),
        ]

    def result(k):
        cols = pl.ds(k * LANES, LANES)
        return pltpu.make_async_copy(done_ref.at[k], out_ref.at[:, :, cols], out_sem.at[k])

    queue = [copies(j)[i] for j in range(blocks) for i in range(2)]
    for copy in queue[:AHEAD]:
        copy.start()
    mixed = jnp.zeros((late, rank + 2 * states), jnp.float32)
    for j in range(blocks):
        history = [
            moved_ref[j, :, pl.ds((states + e) * BLOCK, BLOCK)].astype(jnp.float32) for e in range(3)
        ]
        conv = convolved(jnp.concatenate(history + [x_ref[j]], axis=0), vec_ref[j], late)
        cv_ref[j] = conv.astype(jnp.float32)
        mixed = mixed + mixed_of(conv, xw_ref[j])
    rounded = mixed.astype(jnp.bfloat16)
    for j in range(blocks):
        dt_ref[j] = softplus(
            jnp.dot(rounded[:, :rank], sw_ref[j], preferred_element_type=jnp.float32)
            + vec_ref[j, pl.ds(5, 1), :]
        )
    coefs = rounded[:, rank:].astype(jnp.float32)
    for t in range(draft):
        if t * reqs < late:
            rows = coefs[t * reqs : (t + 1) * reqs]
        else:
            rows = coef_ref[pl.ds(t * reqs - late, reqs), :]
        for n in range(states):
            at = t * states + n
            if t * reqs < late:
                b_ref[at] = jnp.broadcast_to(rows[:, n : n + 1], (reqs, LANES))
            c_ref[at] = jnp.broadcast_to(rows[:, states + n : states + n + 1], (reqs, LANES))
    accepted = acc_ref[...]
    def project(j, gated):
        added = jnp.dot(
            gated, ow_ref[pl.ds(j * BLOCK, BLOCK), :], preferred_element_type=jnp.float32
        )
        for k in range(total_ref.shape[0]):
            part = added[:, k * LANES : (k + 1) * LANES]
            total_ref[k] = part if j == 0 else total_ref[k] + part

    ready = None
    for j in range(blocks):
        for at in (2 * j - 1, 2 * j):
            if at >= 0:
                queue[at].wait()
                if at + AHEAD < len(queue):
                    queue[at + AHEAD].start()
        if ready is not None:
            project(j - 1, ready)
        gated = []
        for k in range(per):
            tile = j * per + k
            lanes = pl.ds(k * LANES, LANES)
            skip = vec_ref[j, pl.ds(6, 1), lanes]
            state = [
                moved_ref[j, :, pl.ds(n * BLOCK + k * LANES, LANES)].astype(jnp.float32)
                for n in range(states)
            ]
            decay = [
                jnp.broadcast_to(vec_ref[j, pl.ds(8 + n, 1), lanes], (reqs, LANES))
                for n in range(states)
            ]
            outs = []
            for t in range(late // reqs):
                rows = pl.ds(t * reqs, reqs)
                delta = dt_ref[j, rows, lanes]
                value = cv_ref[j, rows, lanes]
                driven = delta * value
                chosen = accepted == t + 1
                totals = [skip * value, None]
                for n in range(states):
                    at = t * states + n
                    state[n] = jnp.exp2(delta * decay[n]) * state[n] + driven * b_ref[at]
                    term = c_ref[at] * state[n]
                    totals[n % 2] = term if totals[n % 2] is None else totals[n % 2] + term
                    pltpu.store(pick_ref.at[tile, pl.ds(n * reqs, reqs), :], state[n], mask=chosen)
                outs.append(totals[0] + totals[1])
            beyond = accepted > late // reqs
            passed = at_ref[tile]
            for n in range(states):
                keep = pl.ds(n * reqs, reqs)
                ahead = rows_ref[tile, pl.ds(state_at + n * reqs, reqs), :]
                value = jnp.exp2(passed * decay[n]) * state[n] + ahead
                pltpu.store(pick_ref.at[tile, keep, :], value, mask=beyond)
            for t in range(late // reqs, draft):
                row = t * reqs - late
                passed = rows_ref[tile, pl.ds(sum_at + row, reqs), :]
                totals = [rows_ref[tile, pl.ds(y_at + row, reqs), :], None]
                for n in range(states):
                    term = c_ref[t * states + n] * (jnp.exp2(passed * decay[n]) * state[n])
                    totals[n % 2] = term if totals[n % 2] is None else totals[n % 2] + term
                outs.append(totals[0] + totals[1])
            for r in range(reqs):
                new_ref[j, pl.ds(r * states, states), lanes] = pick_ref[
                    tile, pl.ds(r, states, stride=reqs), :
                ]
            gated.append(jnp.concatenate(outs, axis=0) * rows_ref[tile, pl.ds(gate_at, tokens), :])
        copies(j)[2].start()
        ready = jnp.concatenate(gated, axis=1).astype(jnp.bfloat16)
    queue[-1].wait()
    project(blocks - 1, ready)
    for k in range(total_ref.shape[0]):
        for r in range(reqs):
            rows = total_ref[k, pl.ds(r, draft, stride=reqs), :]
            done_ref[k, r] = rows.astype(jnp.bfloat16)
        result(k).start()
    for j in range(blocks):
        copies(j)[2].wait()
    for k in range(total_ref.shape[0]):
        result(k).wait()


def after(moved, accepted, early, out_weight):
    rows, at, coefs, xw, sw, vec, x = early
    blocks, reqs, _ = moved.shape
    tiles = at.shape[0]
    states = coefs.shape[1] // 2
    late = x.shape[1]
    tokens = coefs.shape[0] + late
    draft = tokens // reqs
    inner, width = out_weight.shape
    vmem = pl.BlockSpec(memory_space=pltpu.VMEM)
    hbm = pl.BlockSpec(memory_space=pltpu.HBM)
    f32 = jnp.float32
    return pl.pallas_call(
        after_kernel,
        out_shape=(
            jax.ShapeDtypeStruct((reqs, draft, width), jnp.bfloat16),
            jax.ShapeDtypeStruct((reqs * states, inner), f32),
        ),
        in_specs=[vmem] * 8 + [hbm] * 2,
        out_specs=(hbm, hbm),
        scratch_shapes=[
            pltpu.VMEM(rows.shape, f32),
            pltpu.VMEM(out_weight.shape, jnp.bfloat16),
            pltpu.VMEM((blocks, reqs * states, BLOCK), f32),
            pltpu.VMEM((tiles, states * reqs, LANES), f32),
            pltpu.VMEM((width // LANES, tokens, LANES), f32),
            pltpu.VMEM((blocks, late, BLOCK), f32),
            pltpu.VMEM((blocks, late, BLOCK), f32),
            pltpu.VMEM((late // reqs * states, reqs, LANES), f32),
            pltpu.VMEM((draft * states, reqs, LANES), f32),
            pltpu.VMEM((width // LANES, reqs, draft, LANES), jnp.bfloat16),
            pltpu.SemaphoreType.DMA((3, blocks)),
            pltpu.SemaphoreType.DMA((width // LANES,)),
        ],
        compiler_params=pltpu.CompilerParams(vmem_limit_bytes=24 << 20),
        cost_estimate=pl.CostEstimate(
            flops=2 * tokens * inner * width, bytes_accessed=12 << 20, transcendentals=4_000_000
        ),
        name="after_states",
    )(moved, accepted, at, coefs, xw, sw, vec, x, in_hbm(rows), in_hbm(out_weight))


def exchange(values):
    return lax.all_to_all(values, "req", split_axis=0, concat_axis=0, tiled=True)


def select_kernel(mask_ref, arrived_ref, out_ref, kept_ref, sems):
    width = arrived_ref.shape[1] // 19
    copies = []
    for at in range(0, 19, 4):
        parts = [(0, 4)] if at < 16 else [(e + 1, 1) for e in range(3)]
        start = at
        for which, size in parts:
            cols = pl.ds(start * width, size * width)
            kept_ref[:, cols] = jnp.dot(
                mask_ref[which], arrived_ref[:, cols], preferred_element_type=jnp.float32
            ).astype(jnp.bfloat16)
            start += size
        cols = pl.ds(at * width, (start - at) * width)
        copies.append(pltpu.make_async_copy(kept_ref.at[:, cols], out_ref.at[:, cols], sems.at[at // 4]))
        copies[-1].start()
    for copy in copies:
        copy.wait()


def select(masks, arrived):
    if arrived.shape[1] % (19 * LANES) == 0:
        return pl.pallas_call(
            select_kernel,
            out_shape=pltpu.HBM(arrived.shape, jnp.bfloat16),
            in_specs=[pl.BlockSpec(memory_space=pltpu.VMEM)] * 2,
            out_specs=pl.BlockSpec(memory_space=pltpu.HBM),
            scratch_shapes=[pltpu.VMEM(arrived.shape, jnp.bfloat16), pltpu.SemaphoreType.DMA((5,))],
            compiler_params=pltpu.CompilerParams(vmem_limit_bytes=16 << 20),
            name="select_slots",
        )(masks, arrived)
    width = arrived.shape[1] // 19
    cut = [0] + [(16 + e) * width for e in range(4)]
    return jnp.concatenate(
        [
            jnp.dot(
                masks[i], arrived[:, cut[i] : cut[i + 1]], preferred_element_type=jnp.float32
            ).astype(jnp.bfloat16)
            for i in range(4)
        ],
        axis=1,
    )


def on_device(
    groups,
    hidden,
    norm_gain,
    in_weight,
    conv_weight,
    conv_bias,
    x_weight,
    step_weight,
    step_bias,
    log_decay,
    skip_gain,
    out_weight,
    old_states,
    old_edges,
    anchor,
    fresh_flag,
    accepted,
    request_ages,
):
    local_reqs, draft_len, width = hidden.shape
    inner_width = out_weight.shape[0]
    channels = conv_weight.shape[1]
    state_size = log_decay.shape[0]
    span = old_edges.shape[1]
    all_reqs = anchor.shape[0]
    blocks = inner_width // channels
    tokens = draft_len * local_reqs

    packed, share = prepared(
        old_states, old_edges, x_weight, step_weight, conv_weight, conv_bias, step_bias, skip_gain, log_decay
    )
    arrived = exchange(packed.reshape(all_reqs, (state_size + span) * channels))
    top = blocks // 2
    own = share[None]
    far, near = moved_by(own, "req", top), moved_by(own, "req", top // 2)
    hidden, far = lax.optimization_barrier((hidden, far))
    token_major = jnp.swapaxes(hidden, 0, 1).reshape(tokens, width)
    normed = rms_normed(token_major, norm_gain)
    projected = jnp.dot(normed, in_weight, preferred_element_type=jnp.float32).astype(jnp.bfloat16)
    weights = jnp.concatenate([own, far, near, moved_by(far, "req", top // 2)])
    weights, projected = lax.optimization_barrier((weights, projected))
    weights = doubled(weights, "req", top // 4)[None]

    old_slot = jnp.arange(all_reqs, dtype=jnp.int32)
    chosen = (anchor[:, None] == old_slot[None, :]) & (fresh_flag[:, None] == 0)
    masks = jnp.stack([chosen] + [chosen & (span - e <= request_ages)[:, None] for e in range(span)])
    masks, projected = lax.optimization_barrier((masks.astype(jnp.bfloat16), projected))
    moved = exchange(select(masks, arrived))

    q_place, j_place = places("grp"), places("req")
    weights = doubled(weights, "grp", groups // 2)
    if channels != BLOCK:
        moved = moved.reshape(blocks, local_reqs, state_size + span, channels).transpose(1, 2, 0, 3)
        moved = moved.reshape(local_reqs, state_size + span, -1, BLOCK).transpose(2, 0, 1, 3)
        weights = jnp.take(weights, j_place, axis=1).swapaxes(1, 2)
        weights = weights.reshape(groups, SHARE, -1, BLOCK).swapaxes(1, 2)
        j_place = jnp.arange(inner_width // BLOCK, dtype=jnp.int32)
    moved = moved.reshape(inner_width // BLOCK, local_reqs, (state_size + span) * BLOCK)

    mine = lax.dynamic_slice_in_dim(accepted, lax.axis_index("req") * local_reqs, local_reqs, 0)
    mine = jnp.broadcast_to(mine[:, None], (local_reqs, LANES))
    early = before(q_place, j_place, projected, weights, mine, span * local_reqs, state_size)
    layer_out, new_states = after(moved, mine, early, out_weight)
    return layer_out, new_states.reshape(local_reqs, state_size, inner_width)


def solution(mesh):
    return jax.shard_map(
        functools.partial(on_device, mesh.shape["grp"]),
        mesh=mesh,
        in_specs=(
            P(("grp", "req"), None, None),
            P(),
            P(),
            P(None, "req"),
            P("req"),
            P("req", None),
            P(None, "req"),
            P("req"),
            P(None, "req"),
            P("req"),
            P(),
            P(("grp", "req"), None, None),
            P(("grp", "req"), None, None),
            P("grp"),
            P("grp"),
            P("grp"),
            P("grp"),
        ),
        out_specs=(P(("grp", "req"), None, None), P(("grp", "req"), None, None)),
        check_vma=False,
    )
```

```python
import functools

import jax
import jax.numpy as jnp
from jax import lax
from jax.experimental import pallas as pl
from jax.experimental.pallas import tpu as pltpu
from jax.sharding import PartitionSpec as P

EPS = 1e-05
LOG2E = 1.4426950408889634
LANES = 128
BLOCK = 256
SHARE = 88
AHEAD = 6


def rms_normed(values_in, norm_gain):
    values = values_in.astype(jnp.float32)
    factor = lax.rsqrt(jnp.mean(values * values, axis=-1, keepdims=True) + EPS)
    return (values * factor * norm_gain).astype(jnp.bfloat16)


def in_hbm(values):
    return pltpu.with_memory_space_constraint(values, pltpu.HBM)


def send_kernel(
    group_ref, state_ref, edge_ref, xt_ref, sw_ref, cw_ref, cb_ref, sb_ref, sk_ref, ld_ref,
    out_ref, share_ref,
    tile_ref, held_ref, send_ref, xt_in, sw_in, vec_ref, sems, few,
):
    blocks, slots, _ = out_ref.shape
    width = state_ref.shape[1] // blocks
    states = state_ref.shape[0] // slots
    per = width // LANES
    rank = sw_ref.shape[0]

    def load(tile):
        cols = pl.ds(tile * LANES, LANES)
        return pltpu.make_async_copy(state_ref.at[:, cols], tile_ref.at[tile], sems.at[0, tile])

    def store(dest):
        return pltpu.make_async_copy(send_ref.at[dest], out_ref.at[dest], sems.at[1, dest])

    small = [
        (edge_ref, held_ref),
        (xt_ref, xt_in),
        (sw_ref, sw_in),
        (cw_ref, vec_ref.at[pl.ds(0, 4), :]),
        (cb_ref, vec_ref.at[pl.ds(4, 1), :]),
        (sb_ref, vec_ref.at[pl.ds(5, 1), :]),
        (sk_ref, vec_ref.at[pl.ds(6, 1), :]),
        (ld_ref, vec_ref.at[pl.ds(8, 16), :]),
    ]
    copies = [pltpu.make_async_copy(x, y, few.at[i]) for i, (x, y) in enumerate(small)]
    vec_ref[pl.ds(7, 1), :] = jnp.zeros((1, width), jnp.float32)
    vec_ref[pl.ds(24, 8), :] = jnp.zeros((8, width), jnp.float32)
    copies[0].start()
    for tile in range(blocks * per):
        load(tile).start()
    for copy in copies[1:]:
        copy.start()
    copies[0].wait()
    for dest in range(blocks):
        for e in range(edge_ref.shape[0]):
            at = (states + e) * width
            send_ref[dest, :, pl.ds(at, width)] = held_ref[e, :, pl.ds(dest * width, width)]
        for part in range(per):
            tile = dest * per + part
            load(tile).wait()
            for n in range(states):
                rows = tile_ref[tile, pl.ds(n, slots, stride=states), :]
                send_ref[dest, :, pl.ds(n * width + part * LANES, LANES)] = rows.astype(jnp.bfloat16)
        store(dest).start()
    for copy in copies[1:]:
        copy.wait()
    for k in range(4):

        @pl.when(group_ref[0] == k)
        def _():
            vec = vec_ref[pl.ds(16 * (k % 2), 16), :]
            high = vec.astype(jnp.bfloat16).astype(jnp.float32)
            part = high if k < 2 else vec - high
            rows = [
                xt_in[pl.ds(32 * k, 32), :].astype(jnp.float32),
                xt_in[pl.ds(rank + 8 * k, 8), :].astype(jnp.float32),
                part[:8],
                sw_in[pl.ds(32 * k, 32), :].astype(jnp.float32),
                part[8:],
            ]
            share_ref[...] = jnp.concatenate(rows, axis=0).astype(jnp.bfloat16)

    for dest in range(blocks):
        store(dest).wait()


def prepared(
    old_states, old_edges, x_weight, step_weight, conv_weight, conv_bias, step_bias, skip_gain, log_decay
):
    slots, states, inner = old_states.shape
    span = old_edges.shape[1]
    width = x_weight.shape[0]
    blocks = inner // width
    rank = step_weight.shape[0]
    edges = jnp.swapaxes(old_edges, 0, 1)
    xt = x_weight.T
    group = lax.axis_index("grp").astype(jnp.int32)
    if width % LANES == 0 and slots == 8:
        tiles = inner // LANES
        vmem = pl.BlockSpec(memory_space=pltpu.VMEM)
        hbm = pl.BlockSpec(memory_space=pltpu.HBM)
        given = (
            old_states.reshape(slots * states, inner), edges, xt, step_weight, conv_weight,
            conv_bias[None], step_bias[None], skip_gain[None], log_decay,
        )
        return pl.pallas_call(
            send_kernel,
            out_shape=(
                pltpu.HBM((blocks, slots, (states + span) * width), jnp.bfloat16),
                jax.ShapeDtypeStruct((SHARE, width), jnp.bfloat16),
            ),
            in_specs=[pl.BlockSpec(memory_space=pltpu.SMEM)] + [hbm] * len(given),
            out_specs=(hbm, vmem),
            scratch_shapes=[
                pltpu.VMEM((tiles, slots * states, LANES), jnp.float32),
                pltpu.VMEM((span, slots, inner), jnp.bfloat16),
                pltpu.VMEM((blocks, slots, (states + span) * width), jnp.bfloat16),
                pltpu.VMEM(xt.shape, jnp.bfloat16),
                pltpu.VMEM(step_weight.shape, jnp.bfloat16),
                pltpu.VMEM((32, width), jnp.float32),
                pltpu.SemaphoreType.DMA((2, tiles)),
                pltpu.SemaphoreType.DMA((8,)),
            ],
            compiler_params=pltpu.CompilerParams(vmem_limit_bytes=16 << 20),
            name="send_states",
        )(group[None], *[in_hbm(x) for x in given])
    lead = jnp.swapaxes(old_states.astype(jnp.bfloat16), 0, 1)
    both = jnp.concatenate([lead, edges], axis=0)
    both = both.reshape(states + span, slots, blocks, width)
    packed = both.transpose(2, 1, 0, 3).reshape(blocks, slots, (states + span) * width)
    none = jnp.zeros_like(conv_bias)[None]
    vec = jnp.concatenate(
        [conv_weight, conv_bias[None], step_bias[None], skip_gain[None], none, log_decay], axis=0
    )
    vec = jnp.pad(vec, ((0, 8), (0, 0)))
    high = vec.astype(jnp.bfloat16)
    halves = jnp.concatenate([high, (vec - high.astype(jnp.float32)).astype(jnp.bfloat16)], axis=0)
    halves = halves.reshape(4, 16, width)
    stacked = jnp.concatenate(
        [
            xt[:rank].reshape(4, 32, width),
            xt[rank:].reshape(4, 8, width),
            halves[:, :8],
            step_weight.reshape(4, 32, width),
            halves[:, 8:],
        ],
        axis=1,
    )
    return packed, lax.dynamic_index_in_dim(stacked, group, 0, keepdims=False)


def moved_by(values, axis, bits):
    return lax.ppermute(values, axis, [(i, i ^ bits) for i in range(lax.axis_size(axis))])


def doubled(values, axis, bits):
    for bit in bits:
        values = jnp.concatenate([values, moved_by(values, axis, bit)], axis=0)
    return values


def halvings(size):
    return [size >> k for k in range(1, size.bit_length())]


def places(axis, bits):
    size = lax.axis_size(axis)
    offset = jnp.arange(size, dtype=jnp.int32) ^ lax.axis_index(axis).astype(jnp.int32)
    place = jnp.zeros_like(offset)
    for k, bit in enumerate(bits):
        place = place | jnp.where((offset & bit) != 0, 1 << k, 0)
    return place


def block_weights(w_ref, q_ref, j_ref, j):
    at = j_ref[j]
    quarters = [w_ref.at[q_ref[q], at] for q in range(4)]
    f32 = jnp.float32
    xw = jnp.concatenate(
        [w[pl.ds(0, 32), :].astype(f32) for w in quarters] + [w[pl.ds(32, 8), :].astype(f32) for w in quarters],
        axis=0,
    ).astype(jnp.bfloat16)
    sw = jnp.concatenate([w[pl.ds(48, 32), :] for w in quarters], axis=0)
    first = [w[pl.ds(40, 8), :].astype(f32) for w in quarters]
    second = [w[pl.ds(80, 8), :].astype(f32) for w in quarters]
    high = jnp.concatenate([first[0], second[0], first[1]], axis=0)
    low = jnp.concatenate([first[2], second[2], first[3]], axis=0)
    return xw, sw, high + low


def silu(values):
    return values / (1.0 + jnp.exp(-values))


def convolved(sequence, vec, count):
    reqs = (sequence.shape[0] - count) // 3
    running = vec[4:5]
    for k in range(4):
        running = running + vec[k : k + 1] * sequence[k * reqs : k * reqs + count]
    return silu(running).astype(jnp.bfloat16)


def softplus(values):
    return jnp.maximum(values, 0.0) + jnp.log1p(jnp.exp(-jnp.abs(values)))


def mixed_of(conv, xw):
    return lax.dot_general(conv, xw, (((1,), (1,)), ((), ())), preferred_element_type=jnp.float32)


def spread(rows, t, b_ref, c_ref):
    reqs, both = rows.shape
    states = both // 2
    for n in range(states):
        b_ref[t * states + n] = jnp.broadcast_to(rows[:, n : n + 1], (reqs, LANES))
        c_ref[t * states + n] = jnp.broadcast_to(rows[:, states + n : states + n + 1], (reqs, LANES))


def before_kernel(
    q_ref, j_ref, proj_ref, w_ref, acc_ref,
    rows_out, at_ref, coef_ref, xw_ref, sw_ref, vec_ref, x_ref,
    rows_ref, dt_ref, cv_ref, b_ref, c_ref, dec_ref, sems,
):
    blocks = w_ref.shape[1]
    tiles, count, _ = dt_ref.shape
    tokens = proj_ref.shape[0]
    late = tokens - count
    reqs = late // 3
    states = b_ref.shape[0] * reqs // count
    inner = blocks * BLOCK
    rank = sw_ref.shape[1]
    per = BLOCK // LANES
    y_at, sum_at, gate_at, state_at = row_offsets(count, tokens)

    def copy(j):
        some = pl.ds(j * per, per)
        return pltpu.make_async_copy(rows_ref.at[some], rows_out.at[some], sems.at[j])

    mixed = jnp.zeros((count, rank + 2 * states), jnp.float32)
    for j in range(blocks):
        xw, sw, vec = block_weights(w_ref, q_ref, j_ref, j)
        values = proj_ref[:, pl.ds(j * BLOCK, BLOCK)].astype(jnp.float32)
        conv = convolved(values, vec, count)
        mixed = mixed + mixed_of(conv, xw)
        xw_ref[j] = xw
        sw_ref[j] = sw
        x_ref[j] = values[:late]
        vec_ref[j, pl.ds(0, 8), :] = vec[:8]
        decay2 = jnp.exp(vec[8:]) * (-LOG2E)
        vec_ref[j, pl.ds(8, states), :] = decay2
        full = conv.astype(jnp.float32)
        gate = silu(proj_ref[:, pl.ds(inner + j * BLOCK, BLOCK)].astype(jnp.float32))
        for k in range(per):
            tile = j * per + k
            lanes = slice(k * LANES, (k + 1) * LANES)
            cv_ref[tile] = full[:, lanes]
            rows_ref[tile, pl.ds(gate_at, tokens), :] = gate[:, lanes]
            rows_ref[tile, pl.ds(y_at, count), :] = vec[6:7, lanes] * full[:, lanes]
            for n in range(states):
                dec_ref[tile, n] = jnp.broadcast_to(decay2[n : n + 1, lanes], (reqs, LANES))
    rounded = mixed.astype(jnp.bfloat16)
    for j in range(blocks):
        dt = softplus(
            jnp.dot(rounded[:, :rank], sw_ref[j], preferred_element_type=jnp.float32)
            + vec_ref[j, pl.ds(5, 1), :]
        )
        for k in range(per):
            dt_ref[j * per + k] = dt[:, k * LANES : (k + 1) * LANES]
    coefs = rounded[:, rank:].astype(jnp.float32)
    coef_ref[...] = coefs
    for t in range(count // reqs):
        spread(coefs[t * reqs : (t + 1) * reqs], t, b_ref, c_ref)
    accepted = acc_ref[...]
    at_ref[...] = jnp.zeros_like(at_ref)

    @pl.loop(0, tiles)
    def _(tile):
        state = [None] * states
        passed = None
        rows_ref[tile, pl.ds(state_at, states * reqs), :] = jnp.zeros((states * reqs, LANES), jnp.float32)
        for t in range(count // reqs):
            delta = dt_ref[tile, pl.ds(t * reqs, reqs), :]
            passed = delta if t == 0 else passed + delta
            rows_ref[tile, pl.ds(sum_at + t * reqs, reqs), :] = passed
            driven = delta * cv_ref[tile, pl.ds(t * reqs, reqs), :]
            chosen = accepted == t + late // reqs + 1
            pltpu.store(at_ref.at[tile], passed, mask=chosen)
            totals = [rows_ref[tile, pl.ds(y_at + t * reqs, reqs), :], None]
            for n in range(states):
                at = t * states + n
                added = driven * b_ref[at]
                state[n] = added if t == 0 else jnp.exp2(delta * dec_ref[tile, n]) * state[n] + added
                term = c_ref[at] * state[n]
                totals[n % 2] = term if totals[n % 2] is None else totals[n % 2] + term
                pltpu.store(
                    rows_ref.at[tile, pl.ds(state_at + n * reqs, reqs), :], state[n], mask=chosen
                )
            rows_ref[tile, pl.ds(y_at + t * reqs, reqs), :] = totals[0] + totals[1]

        @pl.when(tile % per == per - 1)
        def _():
            copy(tile // per).start()

    for j in range(blocks):
        copy(j).wait()


def row_offsets(count, tokens):
    return 0, count, 2 * count, 2 * count + tokens


def before(q_place, j_place, projected, weights, accepted, late, states):
    tokens = projected.shape[0]
    blocks = weights.shape[1]
    tiles = blocks * (BLOCK // LANES)
    count = tokens - late
    reqs = accepted.shape[0]
    rank = 4 * 32
    smem = pl.BlockSpec(memory_space=pltpu.SMEM)
    vmem = pl.BlockSpec(memory_space=pltpu.VMEM)
    f32 = jnp.float32
    spots = count // reqs * states
    rows = (tiles, 2 * count + tokens + states * reqs, LANES)
    return pl.pallas_call(
        before_kernel,
        out_shape=(
            pltpu.HBM(rows, f32),
            jax.ShapeDtypeStruct((tiles, reqs, LANES), f32),
            jax.ShapeDtypeStruct((count, 2 * states), f32),
            jax.ShapeDtypeStruct((blocks, rank + 2 * states, BLOCK), jnp.bfloat16),
            jax.ShapeDtypeStruct((blocks, rank, BLOCK), jnp.bfloat16),
            jax.ShapeDtypeStruct((blocks, 24, BLOCK), f32),
            jax.ShapeDtypeStruct((blocks, late, BLOCK), f32),
        ),
        in_specs=[smem, smem, vmem, vmem, vmem],
        out_specs=(pl.BlockSpec(memory_space=pltpu.HBM),) + (vmem,) * 6,
        scratch_shapes=[
            pltpu.VMEM(rows, f32),
            pltpu.VMEM((tiles, count, LANES), f32),
            pltpu.VMEM((tiles, count, LANES), f32),
            pltpu.VMEM((spots, reqs, LANES), f32),
            pltpu.VMEM((spots, reqs, LANES), f32),
            pltpu.VMEM((tiles, states, reqs, LANES), f32),
            pltpu.SemaphoreType.DMA((blocks,)),
        ],
        compiler_params=pltpu.CompilerParams(vmem_limit_bytes=24 << 20),
        cost_estimate=pl.CostEstimate(flops=200_000_000, bytes_accessed=8 << 20, transcendentals=4_000_000),
        name="before_states",
    )(q_place, j_place, projected, weights, accepted)


def after_kernel(
    moved_ref, acc_ref, at_ref, coef_ref, xw_ref, sw_ref, vec_ref, x_ref, rows_in, ow_in,
    out_ref, ns_ref,
    rows_ref, ow_ref, new_ref, pick_ref, total_ref, dt_ref, cv_ref, b_ref, c_ref, done_ref, sems, out_sem,
):
    reqs, draft, _ = out_ref.shape
    blocks, late, _ = x_ref.shape
    tiles = rows_ref.shape[0]
    tokens = reqs * draft
    count = tokens - late
    states = coef_ref.shape[1] // 2
    rank = sw_ref.shape[1]
    per = BLOCK // LANES
    y_at, sum_at, gate_at, state_at = row_offsets(count, tokens)

    def copies(j):
        some, cols = pl.ds(j * per, per), pl.ds(j * BLOCK, BLOCK)
        return [
            pltpu.make_async_copy(rows_in.at[some], rows_ref.at[some], sems.at[0, j]),
            pltpu.make_async_copy(ow_in.at[cols, :], ow_ref.at[cols, :], sems.at[1, j]),
            pltpu.make_async_copy(new_ref.at[j], ns_ref.at[:, cols], sems.at[2, j]),
        ]

    def result(k):
        cols = pl.ds(k * LANES, LANES)
        return pltpu.make_async_copy(done_ref.at[k], out_ref.at[:, :, cols], out_sem.at[k])

    queue = [copies(j)[i] for j in range(blocks) for i in range(2)]
    for copy in queue[:AHEAD]:
        copy.start()
    mixed = jnp.zeros((late, rank + 2 * states), jnp.float32)
    for j in range(blocks):
        history = [
            moved_ref[j, :, pl.ds((states + e) * BLOCK, BLOCK)].astype(jnp.float32) for e in range(3)
        ]
        conv = convolved(jnp.concatenate(history + [x_ref[j]], axis=0), vec_ref[j], late)
        cv_ref[j] = conv.astype(jnp.float32)
        mixed = mixed + mixed_of(conv, xw_ref[j])
    rounded = mixed.astype(jnp.bfloat16)
    for j in range(blocks):
        dt_ref[j] = softplus(
            jnp.dot(rounded[:, :rank], sw_ref[j], preferred_element_type=jnp.float32)
            + vec_ref[j, pl.ds(5, 1), :]
        )
    coefs = rounded[:, rank:].astype(jnp.float32)
    for t in range(draft):
        if t * reqs < late:
            rows = coefs[t * reqs : (t + 1) * reqs]
        else:
            rows = coef_ref[pl.ds(t * reqs - late, reqs), :]
        for n in range(states):
            at = t * states + n
            if t * reqs < late:
                b_ref[at] = jnp.broadcast_to(rows[:, n : n + 1], (reqs, LANES))
            c_ref[at] = jnp.broadcast_to(rows[:, states + n : states + n + 1], (reqs, LANES))
    accepted = acc_ref[...]
    def project(j, gated):
        added = jnp.dot(
            gated, ow_ref[pl.ds(j * BLOCK, BLOCK), :], preferred_element_type=jnp.float32
        )
        for k in range(total_ref.shape[0]):
            part = added[:, k * LANES : (k + 1) * LANES]
            total_ref[k] = part if j == 0 else total_ref[k] + part

    ready = None
    for j in range(blocks):
        for at in (2 * j - 1, 2 * j):
            if at >= 0:
                queue[at].wait()
                if at + AHEAD < len(queue):
                    queue[at + AHEAD].start()
        if ready is not None:
            project(j - 1, ready)
        gated = []
        for k in range(per):
            tile = j * per + k
            lanes = pl.ds(k * LANES, LANES)
            skip = vec_ref[j, pl.ds(6, 1), lanes]
            state = [
                moved_ref[j, :, pl.ds(n * BLOCK + k * LANES, LANES)].astype(jnp.float32)
                for n in range(states)
            ]
            decay = [
                jnp.broadcast_to(vec_ref[j, pl.ds(8 + n, 1), lanes], (reqs, LANES))
                for n in range(states)
            ]
            outs = []
            for t in range(late // reqs):
                rows = pl.ds(t * reqs, reqs)
                delta = dt_ref[j, rows, lanes]
                value = cv_ref[j, rows, lanes]
                driven = delta * value
                chosen = accepted == t + 1
                totals = [skip * value, None]
                for n in range(states):
                    at = t * states + n
                    state[n] = jnp.exp2(delta * decay[n]) * state[n] + driven * b_ref[at]
                    term = c_ref[at] * state[n]
                    totals[n % 2] = term if totals[n % 2] is None else totals[n % 2] + term
                    pltpu.store(pick_ref.at[tile, pl.ds(n * reqs, reqs), :], state[n], mask=chosen)
                outs.append(totals[0] + totals[1])
            beyond = accepted > late // reqs
            passed = at_ref[tile]
            for n in range(states):
                keep = pl.ds(n * reqs, reqs)
                ahead = rows_ref[tile, pl.ds(state_at + n * reqs, reqs), :]
                value = jnp.exp2(passed * decay[n]) * state[n] + ahead
                pltpu.store(pick_ref.at[tile, keep, :], value, mask=beyond)
            for t in range(late // reqs, draft):
                row = t * reqs - late
                passed = rows_ref[tile, pl.ds(sum_at + row, reqs), :]
                totals = [rows_ref[tile, pl.ds(y_at + row, reqs), :], None]
                for n in range(states):
                    term = c_ref[t * states + n] * (jnp.exp2(passed * decay[n]) * state[n])
                    totals[n % 2] = term if totals[n % 2] is None else totals[n % 2] + term
                outs.append(totals[0] + totals[1])
            for r in range(reqs):
                new_ref[j, pl.ds(r * states, states), lanes] = pick_ref[
                    tile, pl.ds(r, states, stride=reqs), :
                ]
            gated.append(jnp.concatenate(outs, axis=0) * rows_ref[tile, pl.ds(gate_at, tokens), :])
        copies(j)[2].start()
        ready = jnp.concatenate(gated, axis=1).astype(jnp.bfloat16)
    queue[-1].wait()
    project(blocks - 1, ready)
    for k in range(total_ref.shape[0]):
        for r in range(reqs):
            rows = total_ref[k, pl.ds(r, draft, stride=reqs), :]
            done_ref[k, r] = rows.astype(jnp.bfloat16)
        result(k).start()
    for j in range(blocks):
        copies(j)[2].wait()
    for k in range(total_ref.shape[0]):
        result(k).wait()


def after(moved, accepted, early, out_weight):
    rows, at, coefs, xw, sw, vec, x = early
    blocks, reqs, _ = moved.shape
    tiles = at.shape[0]
    states = coefs.shape[1] // 2
    late = x.shape[1]
    tokens = coefs.shape[0] + late
    draft = tokens // reqs
    inner, width = out_weight.shape
    vmem = pl.BlockSpec(memory_space=pltpu.VMEM)
    hbm = pl.BlockSpec(memory_space=pltpu.HBM)
    f32 = jnp.float32
    return pl.pallas_call(
        after_kernel,
        out_shape=(
            jax.ShapeDtypeStruct((reqs, draft, width), jnp.bfloat16),
            jax.ShapeDtypeStruct((reqs * states, inner), f32),
        ),
        in_specs=[vmem] * 8 + [hbm] * 2,
        out_specs=(hbm, hbm),
        scratch_shapes=[
            pltpu.VMEM(rows.shape, f32),
            pltpu.VMEM(out_weight.shape, jnp.bfloat16),
            pltpu.VMEM((blocks, reqs * states, BLOCK), f32),
            pltpu.VMEM((tiles, states * reqs, LANES), f32),
            pltpu.VMEM((width // LANES, tokens, LANES), f32),
            pltpu.VMEM((blocks, late, BLOCK), f32),
            pltpu.VMEM((blocks, late, BLOCK), f32),
            pltpu.VMEM((late // reqs * states, reqs, LANES), f32),
            pltpu.VMEM((draft * states, reqs, LANES), f32),
            pltpu.VMEM((width // LANES, reqs, draft, LANES), jnp.bfloat16),
            pltpu.SemaphoreType.DMA((3, blocks)),
            pltpu.SemaphoreType.DMA((width // LANES,)),
        ],
        compiler_params=pltpu.CompilerParams(vmem_limit_bytes=24 << 20),
        cost_estimate=pl.CostEstimate(
            flops=2 * tokens * inner * width, bytes_accessed=12 << 20, transcendentals=4_000_000
        ),
        name="after_states",
    )(moved, accepted, at, coefs, xw, sw, vec, x, in_hbm(rows), in_hbm(out_weight))


def exchange(values):
    return lax.all_to_all(values, "req", split_axis=0, concat_axis=0, tiled=True)


def select_kernel(mask_ref, arrived_ref, out_ref, kept_ref, sems):
    width = arrived_ref.shape[1] // 19
    copies = []
    for at in range(0, 19, 4):
        parts = [(0, 4)] if at < 16 else [(e + 1, 1) for e in range(3)]
        start = at
        for which, size in parts:
            cols = pl.ds(start * width, size * width)
            kept_ref[:, cols] = jnp.dot(
                mask_ref[which], arrived_ref[:, cols], preferred_element_type=jnp.float32
            ).astype(jnp.bfloat16)
            start += size
        cols = pl.ds(at * width, (start - at) * width)
        copies.append(pltpu.make_async_copy(kept_ref.at[:, cols], out_ref.at[:, cols], sems.at[at // 4]))
        copies[-1].start()
    for copy in copies:
        copy.wait()


def select(masks, arrived):
    if arrived.shape[1] % (19 * LANES) == 0:
        return pl.pallas_call(
            select_kernel,
            out_shape=pltpu.HBM(arrived.shape, jnp.bfloat16),
            in_specs=[pl.BlockSpec(memory_space=pltpu.VMEM)] * 2,
            out_specs=pl.BlockSpec(memory_space=pltpu.HBM),
            scratch_shapes=[pltpu.VMEM(arrived.shape, jnp.bfloat16), pltpu.SemaphoreType.DMA((5,))],
            compiler_params=pltpu.CompilerParams(vmem_limit_bytes=16 << 20),
            name="select_slots",
        )(masks, arrived)
    width = arrived.shape[1] // 19
    cut = [0] + [(16 + e) * width for e in range(4)]
    return jnp.concatenate(
        [
            jnp.dot(
                masks[i], arrived[:, cut[i] : cut[i + 1]], preferred_element_type=jnp.float32
            ).astype(jnp.bfloat16)
            for i in range(4)
        ],
        axis=1,
    )


def on_device(
    groups,
    hidden,
    norm_gain,
    in_weight,
    conv_weight,
    conv_bias,
    x_weight,
    step_weight,
    step_bias,
    log_decay,
    skip_gain,
    out_weight,
    old_states,
    old_edges,
    anchor,
    fresh_flag,
    accepted,
    request_ages,
):
    local_reqs, draft_len, width = hidden.shape
    inner_width = out_weight.shape[0]
    channels = conv_weight.shape[1]
    state_size = log_decay.shape[0]
    span = old_edges.shape[1]
    all_reqs = anchor.shape[0]
    blocks = inner_width // channels
    tokens = draft_len * local_reqs

    packed, share = prepared(
        old_states, old_edges, x_weight, step_weight, conv_weight, conv_bias, step_bias, skip_gain, log_decay
    )
    arrived = exchange(packed.reshape(all_reqs, (state_size + span) * channels))
    order = halvings(blocks)
    order = [order[0], order[-1]] + order[1:-1]
    own = share[None]
    far, near = moved_by(own, "req", order[0]), moved_by(own, "req", order[1])
    hidden, far = lax.optimization_barrier((hidden, far))
    token_major = jnp.swapaxes(hidden, 0, 1).reshape(tokens, width)
    normed = rms_normed(token_major, norm_gain)
    projected = jnp.dot(normed, in_weight, preferred_element_type=jnp.float32).astype(jnp.bfloat16)
    weights = jnp.concatenate([own, far, near, moved_by(far, "req", order[1])])
    weights, projected = lax.optimization_barrier((weights, projected))
    weights = doubled(weights, "req", order[2:])[None]

    old_slot = jnp.arange(all_reqs, dtype=jnp.int32)
    chosen = (anchor[:, None] == old_slot[None, :]) & (fresh_flag[:, None] == 0)
    masks = jnp.stack([chosen] + [chosen & (span - e <= request_ages)[:, None] for e in range(span)])
    masks, projected = lax.optimization_barrier((masks.astype(jnp.bfloat16), projected))
    moved = exchange(select(masks, arrived))

    q_place, j_place = places("grp", halvings(groups)), places("req", order)
    weights = doubled(weights, "grp", halvings(groups))
    if channels != BLOCK:
        moved = moved.reshape(blocks, local_reqs, state_size + span, channels).transpose(1, 2, 0, 3)
        moved = moved.reshape(local_reqs, state_size + span, -1, BLOCK).transpose(2, 0, 1, 3)
        weights = jnp.take(weights, j_place, axis=1).swapaxes(1, 2)
        weights = weights.reshape(groups, SHARE, -1, BLOCK).swapaxes(1, 2)
        j_place = jnp.arange(inner_width // BLOCK, dtype=jnp.int32)
    moved = moved.reshape(inner_width // BLOCK, local_reqs, (state_size + span) * BLOCK)

    mine = lax.dynamic_slice_in_dim(accepted, lax.axis_index("req") * local_reqs, local_reqs, 0)
    mine = jnp.broadcast_to(mine[:, None], (local_reqs, LANES))
    early = before(q_place, j_place, projected, weights, mine, span * local_reqs, state_size)
    layer_out, new_states = after(moved, mine, early, out_weight)
    return layer_out, new_states.reshape(local_reqs, state_size, inner_width)


def solution(mesh):
    return jax.shard_map(
        functools.partial(on_device, mesh.shape["grp"]),
        mesh=mesh,
        in_specs=(
            P(("grp", "req"), None, None),
            P(),
            P(),
            P(None, "req"),
            P("req"),
            P("req", None),
            P(None, "req"),
            P("req"),
            P(None, "req"),
            P("req"),
            P(),
            P(("grp", "req"), None, None),
            P(("grp", "req"), None, None),
            P("grp"),
            P("grp"),
            P("grp"),
            P("grp"),
        ),
        out_specs=(P(("grp", "req"), None, None), P(("grp", "req"), None, None)),
        check_vma=False,
    )
```

```python
import functools

import jax
import jax.numpy as jnp
from jax import lax
from jax.experimental import pallas as pl
from jax.experimental.pallas import tpu as pltpu
from jax.sharding import PartitionSpec as P

EPS = 1e-05
LOG2E = 1.4426950408889634
LANES = 128
BLOCK = 256
SHARE = 88
AHEAD = 6


def rms_normed(values_in, norm_gain):
    values = values_in.astype(jnp.float32)
    factor = lax.rsqrt(jnp.mean(values * values, axis=-1, keepdims=True) + EPS)
    return (values * factor * norm_gain).astype(jnp.bfloat16)


def in_hbm(values):
    return pltpu.with_memory_space_constraint(values, pltpu.HBM)


def send_kernel(
    group_ref, state_ref, edge_ref, xt_ref, sw_ref, cw_ref, cb_ref, sb_ref, sk_ref, ld_ref,
    out_ref, share_ref,
    tile_ref, held_ref, send_ref, xt_in, sw_in, vec_ref, sems, few,
):
    blocks, slots, _ = out_ref.shape
    width = state_ref.shape[1] // blocks
    states = state_ref.shape[0] // slots
    per = width // LANES
    rank = sw_ref.shape[0]

    def load(tile):
        cols = pl.ds(tile * LANES, LANES)
        return pltpu.make_async_copy(state_ref.at[:, cols], tile_ref.at[tile], sems.at[0, tile])

    def store(dest):
        return pltpu.make_async_copy(send_ref.at[dest], out_ref.at[dest], sems.at[1, dest])

    small = [
        (edge_ref, held_ref),
        (xt_ref, xt_in),
        (sw_ref, sw_in),
        (cw_ref, vec_ref.at[pl.ds(0, 4), :]),
        (cb_ref, vec_ref.at[pl.ds(4, 1), :]),
        (sb_ref, vec_ref.at[pl.ds(5, 1), :]),
        (sk_ref, vec_ref.at[pl.ds(6, 1), :]),
        (ld_ref, vec_ref.at[pl.ds(8, 16), :]),
    ]
    copies = [pltpu.make_async_copy(x, y, few.at[i]) for i, (x, y) in enumerate(small)]
    vec_ref[pl.ds(7, 1), :] = jnp.zeros((1, width), jnp.float32)
    vec_ref[pl.ds(24, 8), :] = jnp.zeros((8, width), jnp.float32)
    copies[0].start()
    for tile in range(blocks * per):
        load(tile).start()
    for copy in copies[1:]:
        copy.start()
    copies[0].wait()
    for dest in range(blocks):
        for e in range(edge_ref.shape[0]):
            at = (states + e) * width
            send_ref[dest, :, pl.ds(at, width)] = held_ref[e, :, pl.ds(dest * width, width)]
        for part in range(per):
            tile = dest * per + part
            load(tile).wait()
            for n in range(states):
                rows = tile_ref[tile, pl.ds(n, slots, stride=states), :]
                send_ref[dest, :, pl.ds(n * width + part * LANES, LANES)] = rows.astype(jnp.bfloat16)
        store(dest).start()
    for copy in copies[1:]:
        copy.wait()
    for k in range(4):

        @pl.when(group_ref[0] == k)
        def _():
            vec = vec_ref[pl.ds(16 * (k % 2), 16), :]
            high = vec.astype(jnp.bfloat16).astype(jnp.float32)
            part = high if k < 2 else vec - high
            rows = [
                xt_in[pl.ds(32 * k, 32), :].astype(jnp.float32),
                xt_in[pl.ds(rank + 8 * k, 8), :].astype(jnp.float32),
                part[:8],
                sw_in[pl.ds(32 * k, 32), :].astype(jnp.float32),
                part[8:],
            ]
            share_ref[...] = jnp.concatenate(rows, axis=0).astype(jnp.bfloat16)

    for dest in range(blocks):
        store(dest).wait()


def prepared(
    old_states, old_edges, x_weight, step_weight, conv_weight, conv_bias, step_bias, skip_gain, log_decay
):
    slots, states, inner = old_states.shape
    span = old_edges.shape[1]
    width = x_weight.shape[0]
    blocks = inner // width
    rank = step_weight.shape[0]
    edges = jnp.swapaxes(old_edges, 0, 1)
    xt = x_weight.T
    group = lax.axis_index("grp").astype(jnp.int32)
    if width % LANES == 0 and slots == 8:
        tiles = inner // LANES
        vmem = pl.BlockSpec(memory_space=pltpu.VMEM)
        hbm = pl.BlockSpec(memory_space=pltpu.HBM)
        given = (
            old_states.reshape(slots * states, inner), edges, xt, step_weight, conv_weight,
            conv_bias[None], step_bias[None], skip_gain[None], log_decay,
        )
        return pl.pallas_call(
            send_kernel,
            out_shape=(
                pltpu.HBM((blocks, slots, (states + span) * width), jnp.bfloat16),
                jax.ShapeDtypeStruct((SHARE, width), jnp.bfloat16),
            ),
            in_specs=[pl.BlockSpec(memory_space=pltpu.SMEM)] + [hbm] * len(given),
            out_specs=(hbm, vmem),
            scratch_shapes=[
                pltpu.VMEM((tiles, slots * states, LANES), jnp.float32),
                pltpu.VMEM((span, slots, inner), jnp.bfloat16),
                pltpu.VMEM((blocks, slots, (states + span) * width), jnp.bfloat16),
                pltpu.VMEM(xt.shape, jnp.bfloat16),
                pltpu.VMEM(step_weight.shape, jnp.bfloat16),
                pltpu.VMEM((32, width), jnp.float32),
                pltpu.SemaphoreType.DMA((2, tiles)),
                pltpu.SemaphoreType.DMA((8,)),
            ],
            compiler_params=pltpu.CompilerParams(vmem_limit_bytes=16 << 20),
            name="send_states",
        )(group[None], *[in_hbm(x) for x in given])
    lead = jnp.swapaxes(old_states.astype(jnp.bfloat16), 0, 1)
    both = jnp.concatenate([lead, edges], axis=0)
    both = both.reshape(states + span, slots, blocks, width)
    packed = both.transpose(2, 1, 0, 3).reshape(blocks, slots, (states + span) * width)
    none = jnp.zeros_like(conv_bias)[None]
    vec = jnp.concatenate(
        [conv_weight, conv_bias[None], step_bias[None], skip_gain[None], none, log_decay], axis=0
    )
    vec = jnp.pad(vec, ((0, 8), (0, 0)))
    high = vec.astype(jnp.bfloat16)
    halves = jnp.concatenate([high, (vec - high.astype(jnp.float32)).astype(jnp.bfloat16)], axis=0)
    halves = halves.reshape(4, 16, width)
    stacked = jnp.concatenate(
        [
            xt[:rank].reshape(4, 32, width),
            xt[rank:].reshape(4, 8, width),
            halves[:, :8],
            step_weight.reshape(4, 32, width),
            halves[:, 8:],
        ],
        axis=1,
    )
    return packed, lax.dynamic_index_in_dim(stacked, group, 0, keepdims=False)


def moved_by(values, axis, bits):
    return lax.ppermute(values, axis, [(i, i ^ bits) for i in range(lax.axis_size(axis))])


def doubled(values, axis, bits):
    for bit in bits:
        values = jnp.concatenate([values, moved_by(values, axis, bit)], axis=0)
    return values


def halvings(size):
    return [size >> k for k in range(1, size.bit_length())]


def places(axis, bits):
    size = lax.axis_size(axis)
    offset = jnp.arange(size, dtype=jnp.int32) ^ lax.axis_index(axis).astype(jnp.int32)
    place = jnp.zeros_like(offset)
    for k, bit in enumerate(bits):
        place = place | jnp.where((offset & bit) != 0, 1 << k, 0)
    return place


def block_weights(w_ref, q_ref, j_ref, j):
    at = j_ref[j]
    quarters = [w_ref.at[q_ref[q], at] for q in range(4)]
    f32 = jnp.float32
    xw = jnp.concatenate(
        [w[pl.ds(0, 32), :].astype(f32) for w in quarters] + [w[pl.ds(32, 8), :].astype(f32) for w in quarters],
        axis=0,
    ).astype(jnp.bfloat16)
    sw = jnp.concatenate([w[pl.ds(48, 32), :] for w in quarters], axis=0)
    first = [w[pl.ds(40, 8), :].astype(f32) for w in quarters]
    second = [w[pl.ds(80, 8), :].astype(f32) for w in quarters]
    high = jnp.concatenate([first[0], second[0], first[1]], axis=0)
    low = jnp.concatenate([first[2], second[2], first[3]], axis=0)
    return xw, sw, high + low


def silu(values):
    return values / (1.0 + jnp.exp(-values))


def convolved(sequence, vec, count):
    reqs = (sequence.shape[0] - count) // 3
    running = vec[4:5]
    for k in range(4):
        running = running + vec[k : k + 1] * sequence[k * reqs : k * reqs + count]
    return silu(running).astype(jnp.bfloat16)


def softplus(values):
    return jnp.maximum(values, 0.0) + jnp.log1p(jnp.exp(-jnp.abs(values)))


def mixed_of(conv, xw):
    return lax.dot_general(conv, xw, (((1,), (1,)), ((), ())), preferred_element_type=jnp.float32)


def spread(rows, t, b_ref, c_ref):
    reqs, both = rows.shape
    states = both // 2
    for n in range(states):
        b_ref[t * states + n] = jnp.broadcast_to(rows[:, n : n + 1], (reqs, LANES))
        c_ref[t * states + n] = jnp.broadcast_to(rows[:, states + n : states + n + 1], (reqs, LANES))


def before_kernel(
    q_ref, j_ref, proj_ref, w_ref, acc_ref,
    rows_out, at_ref, coef_ref, xw_ref, sw_ref, vec_ref, x_ref,
    rows_ref, dt_ref, cv_ref, b_ref, c_ref, dec_ref, sems,
):
    blocks = w_ref.shape[1]
    tiles, count, _ = dt_ref.shape
    tokens = proj_ref.shape[0]
    late = tokens - count
    reqs = late // 3
    states = b_ref.shape[0] * reqs // count
    inner = blocks * BLOCK
    rank = sw_ref.shape[1]
    per = BLOCK // LANES
    y_at, sum_at, gate_at, state_at = row_offsets(count, tokens)

    def copy(j):
        some = pl.ds(j * per, per)
        return pltpu.make_async_copy(rows_ref.at[some], rows_out.at[some], sems.at[j])

    mixed = jnp.zeros((count, rank + 2 * states), jnp.float32)
    for j in range(blocks):
        xw, sw, vec = block_weights(w_ref, q_ref, j_ref, j)
        values = proj_ref[:, pl.ds(j * BLOCK, BLOCK)].astype(jnp.float32)
        conv = convolved(values, vec, count)
        mixed = mixed + mixed_of(conv, xw)
        xw_ref[j] = xw
        sw_ref[j] = sw
        x_ref[j] = values[:late]
        vec_ref[j, pl.ds(0, 8), :] = vec[:8]
        decay2 = jnp.exp(vec[8:]) * (-LOG2E)
        vec_ref[j, pl.ds(8, states), :] = decay2
        full = conv.astype(jnp.float32)
        gate = silu(proj_ref[:, pl.ds(inner + j * BLOCK, BLOCK)].astype(jnp.float32))
        for k in range(per):
            tile = j * per + k
            lanes = slice(k * LANES, (k + 1) * LANES)
            cv_ref[tile] = full[:, lanes]
            rows_ref[tile, pl.ds(gate_at, tokens), :] = gate[:, lanes]
            rows_ref[tile, pl.ds(y_at, count), :] = vec[6:7, lanes] * full[:, lanes]
            for n in range(states):
                dec_ref[tile, n] = jnp.broadcast_to(decay2[n : n + 1, lanes], (reqs, LANES))
    rounded = mixed.astype(jnp.bfloat16)
    for j in range(blocks):
        dt = softplus(
            jnp.dot(rounded[:, :rank], sw_ref[j], preferred_element_type=jnp.float32)
            + vec_ref[j, pl.ds(5, 1), :]
        )
        for k in range(per):
            dt_ref[j * per + k] = dt[:, k * LANES : (k + 1) * LANES]
    coefs = rounded[:, rank:].astype(jnp.float32)
    coef_ref[...] = coefs
    for t in range(count // reqs):
        spread(coefs[t * reqs : (t + 1) * reqs], t, b_ref, c_ref)
    accepted = acc_ref[...]
    at_ref[...] = jnp.zeros_like(at_ref)

    @pl.loop(0, tiles)
    def _(tile):
        state = [None] * states
        passed = None
        rows_ref[tile, pl.ds(state_at, states * reqs), :] = jnp.zeros((states * reqs, LANES), jnp.float32)
        for t in range(count // reqs):
            delta = dt_ref[tile, pl.ds(t * reqs, reqs), :]
            passed = delta if t == 0 else passed + delta
            rows_ref[tile, pl.ds(sum_at + t * reqs, reqs), :] = passed
            driven = delta * cv_ref[tile, pl.ds(t * reqs, reqs), :]
            chosen = accepted == t + late // reqs + 1
            pltpu.store(at_ref.at[tile], passed, mask=chosen)
            totals = [rows_ref[tile, pl.ds(y_at + t * reqs, reqs), :], None]
            for n in range(states):
                at = t * states + n
                added = driven * b_ref[at]
                state[n] = added if t == 0 else jnp.exp2(delta * dec_ref[tile, n]) * state[n] + added
                term = c_ref[at] * state[n]
                totals[n % 2] = term if totals[n % 2] is None else totals[n % 2] + term
                pltpu.store(
                    rows_ref.at[tile, pl.ds(state_at + n * reqs, reqs), :], state[n], mask=chosen
                )
            rows_ref[tile, pl.ds(y_at + t * reqs, reqs), :] = totals[0] + totals[1]

        @pl.when(tile % per == per - 1)
        def _():
            copy(tile // per).start()

    for j in range(blocks):
        copy(j).wait()


def row_offsets(count, tokens):
    return 0, count, 2 * count, 2 * count + tokens


def before(q_place, j_place, projected, weights, accepted, late, states):
    tokens = projected.shape[0]
    blocks = weights.shape[1]
    tiles = blocks * (BLOCK // LANES)
    count = tokens - late
    reqs = accepted.shape[0]
    rank = 4 * 32
    smem = pl.BlockSpec(memory_space=pltpu.SMEM)
    vmem = pl.BlockSpec(memory_space=pltpu.VMEM)
    f32 = jnp.float32
    spots = count // reqs * states
    rows = (tiles, 2 * count + tokens + states * reqs, LANES)
    return pl.pallas_call(
        before_kernel,
        out_shape=(
            pltpu.HBM(rows, f32),
            jax.ShapeDtypeStruct((tiles, reqs, LANES), f32),
            jax.ShapeDtypeStruct((count, 2 * states), f32),
            jax.ShapeDtypeStruct((blocks, rank + 2 * states, BLOCK), jnp.bfloat16),
            jax.ShapeDtypeStruct((blocks, rank, BLOCK), jnp.bfloat16),
            jax.ShapeDtypeStruct((blocks, 24, BLOCK), f32),
            jax.ShapeDtypeStruct((blocks, late, BLOCK), f32),
        ),
        in_specs=[smem, smem, vmem, vmem, vmem],
        out_specs=(pl.BlockSpec(memory_space=pltpu.HBM),) + (vmem,) * 6,
        scratch_shapes=[
            pltpu.VMEM(rows, f32),
            pltpu.VMEM((tiles, count, LANES), f32),
            pltpu.VMEM((tiles, count, LANES), f32),
            pltpu.VMEM((spots, reqs, LANES), f32),
            pltpu.VMEM((spots, reqs, LANES), f32),
            pltpu.VMEM((tiles, states, reqs, LANES), f32),
            pltpu.SemaphoreType.DMA((blocks,)),
        ],
        compiler_params=pltpu.CompilerParams(vmem_limit_bytes=24 << 20),
        cost_estimate=pl.CostEstimate(flops=200_000_000, bytes_accessed=8 << 20, transcendentals=4_000_000),
        name="before_states",
    )(q_place, j_place, projected, weights, accepted)


def after_kernel(
    moved_ref, acc_ref, at_ref, coef_ref, xw_ref, sw_ref, vec_ref, x_ref, rows_in, ow_in,
    out_ref, ns_ref,
    rows_ref, ow_ref, new_ref, pick_ref, total_ref, dt_ref, cv_ref, b_ref, c_ref, done_ref, sems, out_sem,
):
    reqs, draft, _ = out_ref.shape
    blocks, late, _ = x_ref.shape
    tiles = rows_ref.shape[0]
    tokens = reqs * draft
    count = tokens - late
    states = coef_ref.shape[1] // 2
    rank = sw_ref.shape[1]
    per = BLOCK // LANES
    y_at, sum_at, gate_at, state_at = row_offsets(count, tokens)

    def copies(j):
        some, cols = pl.ds(j * per, per), pl.ds(j * BLOCK, BLOCK)
        return [
            pltpu.make_async_copy(rows_in.at[some], rows_ref.at[some], sems.at[0, j]),
            pltpu.make_async_copy(ow_in.at[cols, :], ow_ref.at[cols, :], sems.at[1, j]),
            pltpu.make_async_copy(new_ref.at[j], ns_ref.at[:, cols], sems.at[2, j]),
        ]

    def result(k):
        cols = pl.ds(k * LANES, LANES)
        return pltpu.make_async_copy(done_ref.at[k], out_ref.at[:, :, cols], out_sem.at[k])

    queue = [copies(j)[i] for j in range(blocks) for i in range(2)]
    for copy in queue[:AHEAD]:
        copy.start()
    mixed = jnp.zeros((late, rank + 2 * states), jnp.float32)
    for j in range(blocks):
        history = [
            moved_ref[j, :, pl.ds((states + e) * BLOCK, BLOCK)].astype(jnp.float32) for e in range(3)
        ]
        conv = convolved(jnp.concatenate(history + [x_ref[j]], axis=0), vec_ref[j], late)
        cv_ref[j] = conv.astype(jnp.float32)
        mixed = mixed + mixed_of(conv, xw_ref[j])
    rounded = mixed.astype(jnp.bfloat16)
    for j in range(blocks):
        dt_ref[j] = softplus(
            jnp.dot(rounded[:, :rank], sw_ref[j], preferred_element_type=jnp.float32)
            + vec_ref[j, pl.ds(5, 1), :]
        )
    coefs = rounded[:, rank:].astype(jnp.float32)
    for t in range(draft):
        if t * reqs < late:
            rows = coefs[t * reqs : (t + 1) * reqs]
        else:
            rows = coef_ref[pl.ds(t * reqs - late, reqs), :]
        for n in range(states):
            at = t * states + n
            if t * reqs < late:
                b_ref[at] = jnp.broadcast_to(rows[:, n : n + 1], (reqs, LANES))
            c_ref[at] = jnp.broadcast_to(rows[:, states + n : states + n + 1], (reqs, LANES))
    accepted = acc_ref[...]
    def project(j, gated):
        added = jnp.dot(
            gated, ow_ref[pl.ds(j * BLOCK, BLOCK), :], preferred_element_type=jnp.float32
        )
        for k in range(total_ref.shape[0]):
            part = added[:, k * LANES : (k + 1) * LANES]
            total_ref[k] = part if j == 0 else total_ref[k] + part

    ready = None
    for j in range(blocks):
        for at in (2 * j - 1, 2 * j):
            if at >= 0:
                queue[at].wait()
                if at + AHEAD < len(queue):
                    queue[at + AHEAD].start()
        if ready is not None:
            project(j - 1, ready)
        gated = []
        for k in range(per):
            tile = j * per + k
            lanes = pl.ds(k * LANES, LANES)
            skip = vec_ref[j, pl.ds(6, 1), lanes]
            state = [
                moved_ref[j, :, pl.ds(n * BLOCK + k * LANES, LANES)].astype(jnp.float32)
                for n in range(states)
            ]
            decay = [
                jnp.broadcast_to(vec_ref[j, pl.ds(8 + n, 1), lanes], (reqs, LANES))
                for n in range(states)
            ]
            outs = []
            for t in range(late // reqs):
                rows = pl.ds(t * reqs, reqs)
                delta = dt_ref[j, rows, lanes]
                value = cv_ref[j, rows, lanes]
                driven = delta * value
                chosen = accepted == t + 1
                totals = [skip * value, None]
                for n in range(states):
                    at = t * states + n
                    state[n] = jnp.exp2(delta * decay[n]) * state[n] + driven * b_ref[at]
                    term = c_ref[at] * state[n]
                    totals[n % 2] = term if totals[n % 2] is None else totals[n % 2] + term
                    pltpu.store(pick_ref.at[tile, pl.ds(n * reqs, reqs), :], state[n], mask=chosen)
                outs.append(totals[0] + totals[1])
            beyond = accepted > late // reqs
            passed = at_ref[tile]
            for n in range(states):
                keep = pl.ds(n * reqs, reqs)
                ahead = rows_ref[tile, pl.ds(state_at + n * reqs, reqs), :]
                value = jnp.exp2(passed * decay[n]) * state[n] + ahead
                pltpu.store(pick_ref.at[tile, keep, :], value, mask=beyond)
            for t in range(late // reqs, draft):
                row = t * reqs - late
                passed = rows_ref[tile, pl.ds(sum_at + row, reqs), :]
                totals = [rows_ref[tile, pl.ds(y_at + row, reqs), :], None]
                for n in range(states):
                    term = c_ref[t * states + n] * (jnp.exp2(passed * decay[n]) * state[n])
                    totals[n % 2] = term if totals[n % 2] is None else totals[n % 2] + term
                outs.append(totals[0] + totals[1])
            for r in range(reqs):
                new_ref[j, pl.ds(r * states, states), lanes] = pick_ref[
                    tile, pl.ds(r, states, stride=reqs), :
                ]
            gated.append(jnp.concatenate(outs, axis=0) * rows_ref[tile, pl.ds(gate_at, tokens), :])
        copies(j)[2].start()
        ready = jnp.concatenate(gated, axis=1).astype(jnp.bfloat16)
    queue[-1].wait()
    project(blocks - 1, ready)
    for k in range(total_ref.shape[0]):
        for r in range(reqs):
            rows = total_ref[k, pl.ds(r, draft, stride=reqs), :]
            done_ref[k, r] = rows.astype(jnp.bfloat16)
        result(k).start()
    for j in range(blocks):
        copies(j)[2].wait()
    for k in range(total_ref.shape[0]):
        result(k).wait()


def after(moved, accepted, early, out_weight):
    rows, at, coefs, xw, sw, vec, x = early
    blocks, reqs, _ = moved.shape
    tiles = at.shape[0]
    states = coefs.shape[1] // 2
    late = x.shape[1]
    tokens = coefs.shape[0] + late
    draft = tokens // reqs
    inner, width = out_weight.shape
    vmem = pl.BlockSpec(memory_space=pltpu.VMEM)
    hbm = pl.BlockSpec(memory_space=pltpu.HBM)
    f32 = jnp.float32
    return pl.pallas_call(
        after_kernel,
        out_shape=(
            jax.ShapeDtypeStruct((reqs, draft, width), jnp.bfloat16),
            jax.ShapeDtypeStruct((reqs * states, inner), f32),
        ),
        in_specs=[vmem] * 8 + [hbm] * 2,
        out_specs=(hbm, hbm),
        scratch_shapes=[
            pltpu.VMEM(rows.shape, f32),
            pltpu.VMEM(out_weight.shape, jnp.bfloat16),
            pltpu.VMEM((blocks, reqs * states, BLOCK), f32),
            pltpu.VMEM((tiles, states * reqs, LANES), f32),
            pltpu.VMEM((width // LANES, tokens, LANES), f32),
            pltpu.VMEM((blocks, late, BLOCK), f32),
            pltpu.VMEM((blocks, late, BLOCK), f32),
            pltpu.VMEM((late // reqs * states, reqs, LANES), f32),
            pltpu.VMEM((draft * states, reqs, LANES), f32),
            pltpu.VMEM((width // LANES, reqs, draft, LANES), jnp.bfloat16),
            pltpu.SemaphoreType.DMA((3, blocks)),
            pltpu.SemaphoreType.DMA((width // LANES,)),
        ],
        compiler_params=pltpu.CompilerParams(vmem_limit_bytes=24 << 20),
        cost_estimate=pl.CostEstimate(
            flops=2 * tokens * inner * width, bytes_accessed=12 << 20, transcendentals=4_000_000
        ),
        name="after_states",
    )(moved, accepted, at, coefs, xw, sw, vec, x, in_hbm(rows), in_hbm(out_weight))


def exchange(values):
    return lax.all_to_all(values, "req", split_axis=0, concat_axis=0, tiled=True)


def select_kernel(mask_ref, arrived_ref, out_ref, kept_ref, sems):
    width = arrived_ref.shape[1] // 19
    copies = []
    for at in range(0, 19, 4):
        parts = [(0, 4)] if at < 16 else [(e + 1, 1) for e in range(3)]
        start = at
        for which, size in parts:
            cols = pl.ds(start * width, size * width)
            kept_ref[:, cols] = jnp.dot(
                mask_ref[which], arrived_ref[:, cols], preferred_element_type=jnp.float32
            ).astype(jnp.bfloat16)
            start += size
        cols = pl.ds(at * width, (start - at) * width)
        copies.append(pltpu.make_async_copy(kept_ref.at[:, cols], out_ref.at[:, cols], sems.at[at // 4]))
        copies[-1].start()
    for copy in copies:
        copy.wait()


def select(masks, arrived):
    if arrived.shape[1] % (19 * LANES) == 0:
        return pl.pallas_call(
            select_kernel,
            out_shape=pltpu.HBM(arrived.shape, jnp.bfloat16),
            in_specs=[pl.BlockSpec(memory_space=pltpu.VMEM)] * 2,
            out_specs=pl.BlockSpec(memory_space=pltpu.HBM),
            scratch_shapes=[pltpu.VMEM(arrived.shape, jnp.bfloat16), pltpu.SemaphoreType.DMA((5,))],
            compiler_params=pltpu.CompilerParams(vmem_limit_bytes=16 << 20),
            name="select_slots",
        )(masks, arrived)
    width = arrived.shape[1] // 19
    cut = [0] + [(16 + e) * width for e in range(4)]
    return jnp.concatenate(
        [
            jnp.dot(
                masks[i], arrived[:, cut[i] : cut[i + 1]], preferred_element_type=jnp.float32
            ).astype(jnp.bfloat16)
            for i in range(4)
        ],
        axis=1,
    )


def on_device(
    groups,
    hidden,
    norm_gain,
    in_weight,
    conv_weight,
    conv_bias,
    x_weight,
    step_weight,
    step_bias,
    log_decay,
    skip_gain,
    out_weight,
    old_states,
    old_edges,
    anchor,
    fresh_flag,
    accepted,
    request_ages,
):
    local_reqs, draft_len, width = hidden.shape
    inner_width = out_weight.shape[0]
    channels = conv_weight.shape[1]
    state_size = log_decay.shape[0]
    span = old_edges.shape[1]
    all_reqs = anchor.shape[0]
    blocks = inner_width // channels
    tokens = draft_len * local_reqs

    packed, share = prepared(
        old_states, old_edges, x_weight, step_weight, conv_weight, conv_bias, step_bias, skip_gain, log_decay
    )
    arrived = exchange(packed.reshape(all_reqs, (state_size + span) * channels))
    order = halvings(blocks)
    order = [order[0], order[-1]] + order[1:-1]
    own = share[None]
    far, near = moved_by(own, "req", order[0]), moved_by(own, "req", order[1])
    weights = jnp.concatenate([own, far, near, moved_by(far, "req", order[1])])
    hidden, weights = lax.optimization_barrier((hidden, weights))
    token_major = jnp.swapaxes(hidden, 0, 1).reshape(tokens, width)
    normed = rms_normed(token_major, norm_gain)
    projected = jnp.dot(normed, in_weight, preferred_element_type=jnp.float32).astype(jnp.bfloat16)
    weights = doubled(weights, "req", order[2:])[None]

    old_slot = jnp.arange(all_reqs, dtype=jnp.int32)
    chosen = (anchor[:, None] == old_slot[None, :]) & (fresh_flag[:, None] == 0)
    masks = jnp.stack([chosen] + [chosen & (span - e <= request_ages)[:, None] for e in range(span)])
    masks, projected, weights = lax.optimization_barrier((masks.astype(jnp.bfloat16), projected, weights))
    moved = exchange(select(masks, arrived))

    q_place, j_place = places("grp", halvings(groups)), places("req", order)
    weights = doubled(weights, "grp", halvings(groups))
    if channels != BLOCK:
        moved = moved.reshape(blocks, local_reqs, state_size + span, channels).transpose(1, 2, 0, 3)
        moved = moved.reshape(local_reqs, state_size + span, -1, BLOCK).transpose(2, 0, 1, 3)
        weights = jnp.take(weights, j_place, axis=1).swapaxes(1, 2)
        weights = weights.reshape(groups, SHARE, -1, BLOCK).swapaxes(1, 2)
        j_place = jnp.arange(inner_width // BLOCK, dtype=jnp.int32)
    moved = moved.reshape(inner_width // BLOCK, local_reqs, (state_size + span) * BLOCK)

    mine = lax.dynamic_slice_in_dim(accepted, lax.axis_index("req") * local_reqs, local_reqs, 0)
    mine = jnp.broadcast_to(mine[:, None], (local_reqs, LANES))
    early = before(q_place, j_place, projected, weights, mine, span * local_reqs, state_size)
    layer_out, new_states = after(moved, mine, early, out_weight)
    return layer_out, new_states.reshape(local_reqs, state_size, inner_width)


def solution(mesh):
    return jax.shard_map(
        functools.partial(on_device, mesh.shape["grp"]),
        mesh=mesh,
        in_specs=(
            P(("grp", "req"), None, None),
            P(),
            P(),
            P(None, "req"),
            P("req"),
            P("req", None),
            P(None, "req"),
            P("req"),
            P(None, "req"),
            P("req"),
            P(),
            P(("grp", "req"), None, None),
            P(("grp", "req"), None, None),
            P("grp"),
            P("grp"),
            P("grp"),
            P("grp"),
        ),
        out_specs=(P(("grp", "req"), None, None), P(("grp", "req"), None, None)),
        check_vma=False,
    )
```
